128 devices in a mesh: dom: 128 (over x, y, z, core).
Axes of the slice: x: 4, y: 4, z: 4, core: 2. Of those that a mesh axis runs over, the one named last changes fastest.
Arguments:
- adjoint: float32 [4, 8, 64, 32768], P(None, None, None, 'dom'), may hold values from -1.5 to 1.5
- velocity: bfloat16 [3, 64, 32768], P(None, None, 'dom'), may hold values from -4 to 4
- metric: float32 [3, 32768], P(None, 'dom'), may hold values from 0.5 to 2
- face_scale: float32 [6, 32768], P(None, 'dom'), may hold values from 0.5 to 2
- resistance: float32 [2, 1024], P(None, 'dom'), may hold values from 0.5 to 2
- elem_count: int32 [128], P('dom'), may hold values from 192 to 256, as said below
- face_partner: int32 [6, 32768], P(None, 'dom'), may hold values from -1 to 1535, as said below
- link_face: int32 [128, 7, 32], P('dom'), may hold values from -1 to 1535, as said below
- outlet_face: int32 [128, 32], P('dom'), may hold values from 0 to 1535, as said below
- outlet_id: int32 [128, 32], P('dom'), may hold values from 0 to 1023, as said below
Outputs:
- adj_res: float32 [4, 8, 64, 32768], P(None, None, None, 'dom')
- multiplier: float32 [8, 1024], P(None, 'dom')
The draws below stay inside these ranges and needn't reach their ends.
Inputs may be any that keep to these rules, and one draw needn't show every extreme that they name: Elements e >= elem_count[p] of device p are padding. Some device uses all 256. `face_partner`: values are local face ids of the same device or -1. The relation is symmetric, never pairs a face with itself, names only faces of used elements, and forms exactly 256 pairs on each device. Faces named in link_face or outlet_face have -1. link_face[p][b][s] is a local face id of a used element of device p, or -1 exactly when s is at least the count of the pair of devices p and p XOR 2^b, a count shared by both and at least 16. For every b some pair uses all 32 slots. Used entries are distinct on a device and are not outlet faces. `outlet_face`: 32 distinct local face ids of used elements on each device. `outlet_id`: over all devices every outlet is named exactly 4 times.
All inputs are finite; a program needn't handle non-finite values.
Results may differ from the reference program's by a relative error of at most 0.0003.
Values sent between devices are 32-bit elements; how exact they have to be, the bound alone decides.
No kernel may reach another device: no remote copies, remote signals or barrier semaphores. Data moves between devices by JAX's collectives and lax.ppermute only.
A program may use at most 256 MiB of HBM per device.

```python
import math
import jax
import jax.numpy as jnp
import numpy as np
from jax import lax

COMPS = 4
OBJ = 8
NODES = 64
E_DEV = 256
CAP = 32
OUT_FACES = 32
NBITS = 7
ELEMENTS = 32768
NOUT = 1024
N_DOM = 128


def partition_layout(key):
    seeded = jax.random.fold_in(key, 4177)
    subkeys = jax.random.split(seeded, 6)
    counts = jax.random.randint(subkeys[0], (N_DOM,), E_DEV - E_DEV // 4, E_DEV + 1)
    fullest = jax.random.randint(subkeys[1], (), 0, N_DOM)
    counts = counts.at[fullest].set(E_DEV).astype(jnp.int32)
    face_ids = jnp.arange(6 * E_DEV, dtype=jnp.int32)
    element = face_ids % E_DEV
    jitter = jax.random.randint(subkeys[2], (N_DOM, 6 * E_DEV), 0, 65536)
    scores = jitter * (6 * E_DEV) + face_ids[None] + (element[None] >= counts[:, None]).astype(jnp.int32) * 2 ** 30
    ordering = jnp.argsort(scores, axis=1, stable=True).astype(jnp.int32)
    slot_total = NBITS * CAP
    ranks = jnp.arange(N_DOM, dtype=jnp.int32)
    powers = (2 ** jnp.arange(NBITS)).astype(jnp.int32)
    partners = jnp.bitwise_xor(ranks[:, None], powers[None])
    lowest = jnp.minimum(ranks[:, None], partners)
    drawn = jax.random.randint(subkeys[3], (N_DOM, NBITS), (CAP + 1) // 2, CAP + 1)
    filled = drawn[lowest, jnp.arange(NBITS)[None]]
    chosen = jax.random.randint(subkeys[4], (NBITS,), 0, N_DOM).astype(jnp.int32)
    chosen_low = jnp.minimum(chosen, jnp.bitwise_xor(chosen, powers))
    filled = jnp.where(lowest == chosen_low[None], CAP, filled)
    link_table = ordering[:, :slot_total].reshape(N_DOM, NBITS, CAP)
    link_table = jnp.where(jnp.arange(CAP)[None, None] < filled[:, :, None], link_table, -1).astype(jnp.int32)
    outlets = ordering[:, slot_total:slot_total + OUT_FACES]
    offset = slot_total + OUT_FACES
    leading = ordering[:, offset:offset + 2 * E_DEV:2]
    trailing = ordering[:, offset + 1:offset + 2 * E_DEV:2]
    row_index = jnp.broadcast_to(ranks[:, None], leading.shape)
    partner = jnp.full((N_DOM, 6 * E_DEV), -1, jnp.int32)
    partner = partner.at[row_index, leading].set(trailing)
    partner = partner.at[row_index, trailing].set(leading)
    partner_global = jnp.transpose(partner.reshape(N_DOM, 6, E_DEV), (1, 0, 2)).reshape(6, N_DOM * E_DEV)
    outlet_names = (jax.random.permutation(subkeys[5], N_DOM * OUT_FACES) % NOUT).astype(jnp.int32).reshape(N_DOM, OUT_FACES)
    return (counts, partner_global, link_table, outlets.astype(jnp.int32), outlet_names)


def draw_elem_count(key, part):
    return partition_layout(key)[0]


def draw_face_partner(key, part):
    return partition_layout(key)[1]


def draw_link_face(key, part):
    return partition_layout(key)[2]


def draw_outlet_face(key, part):
    return partition_layout(key)[3]


def draw_outlet_id(key, part):
    return partition_layout(key)[4]


def block_levels(own_key, extent, pieces, smallest, top_value):
    level = 1.0
    for position, blocks in pieces:
        steps = jax.random.uniform(jax.random.fold_in(jax.random.fold_in(own_key, 6), position), (blocks,), jnp.float32, smallest / len(pieces), top_value / len(pieces))
        level = level * jnp.repeat(jnp.exp(steps), extent[position] // blocks).reshape((-1,) + (1,) * (len(extent) - 1 - position))
    return level


def scatter_about(key, shape, width, reach, shards=(), kind=jnp.bfloat16):
    gain = block_levels(key, shape, shards, -0.22, 0.18) if shards else 1.0
    values = jax.random.normal(key, shape, jnp.float32) * width * gain
    return jnp.minimum(jnp.maximum(values, -reach), reach).astype(kind)


def setup_inputs(seed: int = 0) -> dict:
    splits = jax.random.split(jax.random.key(seed), 11)
    adjoint = scatter_about(splits[0], (COMPS, OBJ, NODES, ELEMENTS), 0.25, 1.5, ((3, 128),), jnp.float32)
    velocity = scatter_about(splits[1], (3, NODES, ELEMENTS), 1.0, 4.0, ((2, 128),))
    metric = jnp.clip(jnp.exp(math.log(2.0) - 1.3862944 * jax.random.uniform(splits[2], (3, ELEMENTS), jnp.float32) ** block_levels(splits[2], (3, ELEMENTS), ((1, 128),), -0.2, 0.2)), 0.5, 2.0)
    face_scale = jnp.clip(jnp.exp(math.log(2.0) - 1.3862944 * jax.random.uniform(splits[3], (6, ELEMENTS), jnp.float32) ** block_levels(splits[3], (6, ELEMENTS), ((1, 128),), -0.2, 0.2)), 0.5, 2.0)
    resistance = jnp.clip(jnp.exp(math.log(2.0) - 1.3862944 * jax.random.uniform(splits[4], (2, NOUT), jnp.float32) ** block_levels(splits[4], (2, NOUT), ((1, 128),), -0.2, 0.2)), 0.5, 2.0)
    elem_count = draw_elem_count(jax.random.fold_in(splits[10], 71), 0)
    face_partner = draw_face_partner(jax.random.fold_in(splits[10], 71), 0)
    link_face = draw_link_face(jax.random.fold_in(splits[10], 71), 0)
    outlet_face = draw_outlet_face(jax.random.fold_in(splits[10], 71), 0)
    outlet_id = draw_outlet_id(jax.random.fold_in(splits[10], 71), 0)
    return dict(adjoint=adjoint, velocity=velocity, metric=metric, face_scale=face_scale, resistance=resistance, elem_count=elem_count, face_partner=face_partner, link_face=link_face, outlet_face=outlet_face, outlet_id=outlet_id)


viscous_coef = 0.05
penalty_coef = 1.0

def gll_tables():
    root_five = math.sqrt(5.0)
    points = np.array([-1.0, -1.0 / root_five, 1.0 / root_five, 1.0])
    weights = np.array([1.0, 5.0, 5.0, 1.0]) / 6.0
    products = np.array([np.prod([points[i] - points[k] for k in range(4) if k != i]) for i in range(4)])
    derivative = np.zeros((4, 4))
    for i in range(4):
        for j in range(4):
            if i != j:
                derivative[i, j] = products[i] / (products[j] * (points[i] - points[j]))
        derivative[i, i] = -np.sum(derivative[i])
    return (derivative, weights)

def face_weights():
    weights = gll_tables()[1]
    return np.outer(weights, weights).reshape(16)

def face_traces(grid):
    face_list = []
    for face_num in range(6):
        node_axis = grid.ndim - 4 + face_num // 2
        face_slab = jnp.take(grid, 3 * (face_num % 2), axis=node_axis)
        face_list.append(face_slab.reshape(face_slab.shape[:-3] + (16, face_slab.shape[-1])))
    return jnp.stack(face_list, axis=-2)

def lift_faces(grid, facef):
    for face_num in range(6):
        node_axis = grid.ndim - 4 + face_num // 2
        layer_index = 3 * (face_num % 2)
        face_slab = facef[..., face_num, :]
        face_slab = face_slab.reshape(face_slab.shape[:-2] + (4, 4, face_slab.shape[-1]))
        face_slab = jnp.expand_dims(face_slab, node_axis)
        selector = [slice(None)] * grid.ndim
        selector[node_axis] = slice(layer_index, layer_index + 1)
        grid = grid.at[tuple(selector)].add(face_slab)
    return grid

def normal_velocity(vel_grid):
    traces = face_traces(vel_grid)
    columns = []
    for face_num in range(6):
        columns.append((2.0 * (face_num % 2) - 1.0) * traces[face_num // 2, :, face_num, :])
    return jnp.stack(columns, axis=1)

def outlet_moments(inner_cols, normal_flat, scale_flat, outlet_row, elements):
    weights = jnp.asarray(face_weights(), jnp.float32)
    gathered = jnp.take(inner_cols, outlet_row, axis=1).reshape(4, -1, 16, outlet_row.shape[0])
    face_num = outlet_row // elements
    direction = face_num // 2
    sign_value = (2 * (face_num % 2) - 1).astype(jnp.float32)
    selector = (jnp.arange(4, dtype=jnp.int32)[:, None] == direction[None, :]).astype(jnp.float32)
    normal_part = jnp.einsum('cojt,ct->ojt', gathered, selector, precision=lax.Precision.HIGHEST)
    outlet_scale = jnp.take(scale_flat, outlet_row)
    adj_moment = jnp.einsum('ojt,j->ot', normal_part, weights, precision=lax.Precision.HIGHEST) * (sign_value * outlet_scale)[None]
    flow_moment = jnp.einsum('jt,j->t', jnp.take(normal_flat, outlet_row, axis=1), weights, precision=lax.Precision.HIGHEST) * outlet_scale
    return jnp.concatenate([adj_moment, flow_moment[None]], axis=0)

def face_residual(grid, inner_cols, received_cols, partner_row, link_row, normal, scale_dev, outlet_row, mu_face):
    elements = scale_dev.shape[1]
    total_faces = 6 * elements
    slot_count = received_cols.shape[1]
    source = jnp.where(partner_row >= 0, partner_row, total_faces + slot_count)
    target = jnp.where(link_row >= 0, link_row, total_faces)
    source = source.at[target].set(total_faces + jnp.arange(slot_count, dtype=jnp.int32), mode='drop')
    extended = jnp.concatenate([inner_cols, received_cols, jnp.zeros((inner_cols.shape[0], 1), jnp.float32)], axis=1)
    outer_cols = jnp.take(extended, source, axis=1)
    objectives = mu_face.shape[0]
    inner = inner_cols.reshape(4, objectives, 16, 6, elements)
    outer = outer_cols.reshape(4, objectives, 16, 6, elements)
    upwind = 0.5 * jnp.abs(normal) + penalty_coef
    facef = scale_dev * (upwind * (inner - outer) - 0.5 * normal * (inner + outer))
    extra = jnp.zeros((objectives, total_faces), jnp.float32).at[:, outlet_row].set(mu_face).reshape(objectives, 6, elements)
    comp_mask = jnp.asarray(np.arange(6)[None, :] // 2 == np.arange(4)[:, None], jnp.float32)
    signs = jnp.asarray(2.0 * (np.arange(6) % 2) - 1.0, jnp.float32)
    weights = jnp.asarray(face_weights(), jnp.float32)
    facef = facef + comp_mask[:, None, None, :, None] * (signs[:, None] * scale_dev)[None, None, None] * weights[None, None, :, None, None] * extra[None, :, None]
    return lift_faces(grid, facef)

def apply_axis(matrix, grid, direction):
    pattern = ['mi,...ijke->...mjke', 'mj,...ijke->...imke', 'mk,...ijke->...ijme'][direction]
    return jnp.einsum(pattern, matrix, grid, precision=lax.Precision.HIGHEST)

def volume_terms(adjoint_grid, vel_grid, metric_dev):
    derivative = jnp.asarray(gll_tables()[0], jnp.float32)
    transposed = derivative.T
    volume = jnp.zeros_like(adjoint_grid)
    for direction in range(3):
        gain_row = metric_dev[direction]
        derived = apply_axis(derivative, adjoint_grid[:3], direction)
        velpart = gain_row * vel_grid[direction] * adjoint_grid[:3] + viscous_coef * gain_row * gain_row * derived
        velpart = velpart.at[direction].add(gain_row * adjoint_grid[3])
        pressure_part = gain_row * adjoint_grid[direction]
        stacked = jnp.concatenate([velpart, pressure_part[None]], axis=0)
        volume = volume + apply_axis(transposed, stacked, direction)
    for component in range(3):
        grads = metric_dev[component] * apply_axis(derivative, vel_grid, component)
        reaction = lax.optimization_barrier(jnp.sum(grads[:, None] * adjoint_grid[:3], axis=0))
        volume = volume.at[component].add(reaction)
    return volume

def reference(adjoint, velocity, metric, face_scale, resistance, elem_count, face_partner, link_face, outlet_face, outlet_id):
    objectives = adjoint.shape[1]
    slot_total = NBITS * CAP

    def take_block(array, device):
        return lax.dynamic_slice_in_dim(array, device * E_DEV, E_DEV, axis=array.ndim - 1)

    def local_parts(device):
        adjoint_dev = take_block(adjoint, device)
        vel_grid = take_block(velocity, device).astype(jnp.float32).reshape(3, 4, 4, 4, E_DEV)
        adjoint_grid = adjoint_dev.reshape(4, objectives, 4, 4, 4, E_DEV)
        inner_cols = face_traces(adjoint_grid).reshape(-1, 6 * E_DEV)
        return (adjoint_grid, vel_grid, inner_cols, normal_velocity(vel_grid))

    def first_section(device):
        adjoint_grid, vel_grid, inner_cols, normal = local_parts(device)
        link_row = link_face[device].reshape(-1)
        send_cols = jnp.take(inner_cols, jnp.maximum(link_row, 0), axis=1) * (link_row >= 0).astype(jnp.float32)[None]
        moments = outlet_moments(inner_cols, normal.reshape(16, -1), take_block(face_scale, device).reshape(-1), outlet_face[device], E_DEV)
        return (send_cols, moments)
    send_all, moment_all = lax.map(first_section, jnp.arange(N_DOM, dtype=jnp.int32))
    totals = jax.ops.segment_sum(jnp.transpose(moment_all, (0, 2, 1)).reshape(-1, objectives + 1), outlet_id.reshape(-1), num_segments=NOUT)
    multiplier = ((resistance[0] + 2.0 * resistance[1] * jnp.abs(totals[:, objectives]))[:, None] * totals[:, :objectives]).T
    partner_dev = np.arange(N_DOM)[:, None] ^ (1 << np.arange(NBITS))[None, :]
    grouped = send_all.reshape(N_DOM, -1, NBITS, CAP)
    received_all = grouped[partner_dev, :, np.arange(NBITS)[None, :], :]
    received_all = jnp.transpose(received_all, (0, 2, 1, 3)).reshape(N_DOM, -1, slot_total)
    mu_all = jnp.transpose(multiplier[:, outlet_id], (1, 0, 2))

    def second_section(device):
        adjoint_grid, vel_grid, inner_cols, normal = local_parts(device)
        volume = volume_terms(adjoint_grid, vel_grid, take_block(metric, device))
        grid = face_residual(volume, inner_cols, received_all[device], take_block(face_partner, device).reshape(-1), link_face[device].reshape(-1), normal, take_block(face_scale, device), outlet_face[device], mu_all[device])
        live = (jnp.arange(E_DEV, dtype=jnp.int32) < elem_count[device]).astype(jnp.float32)
        return grid.reshape(4, objectives, 64, E_DEV) * live
    blocks = lax.map(second_section, jnp.arange(N_DOM, dtype=jnp.int32))
    adj_res = jnp.transpose(blocks, (1, 2, 3, 0, 4)).reshape(4, objectives, 64, N_DOM * E_DEV)
    return (adj_res, multiplier)
```

```python
import math

import jax
import jax.numpy as jnp
import numpy as np
from jax import lax
from jax.experimental import pallas as pl
from jax.experimental.pallas import tpu as pltpu
from jax.sharding import PartitionSpec as P


F32 = jnp.float32
BF16 = jnp.bfloat16
VISCOUS = 0.05
PENALTY = 1.0
COMPS, OBJ, NODES, ELEMS = 4, 8, 64, 256
LANES = 128
CAP, LEVELS = 32, 7
FACE_ROWS = COMPS * CAP
MSG = 4
HIGHEST = lax.Precision.HIGHEST


def gll_tables():
    root_five = math.sqrt(5.0)
    points = np.array([-1.0, -1.0 / root_five, 1.0 / root_five, 1.0])
    weights = np.array([1.0, 5.0, 5.0, 1.0]) / 6.0
    products = np.array(
        [np.prod([points[i] - points[k] for k in range(4) if k != i]) for i in range(4)]
    )
    derivative = np.zeros((4, 4))
    for i in range(4):
        for j in range(4):
            if i != j:
                derivative[i, j] = products[i] / (products[j] * (points[i] - points[j]))
        derivative[i, i] = -np.sum(derivative[i])
    return (derivative, weights)


DERIV, WEIGHTS = gll_tables()
FACE_W = np.outer(WEIGHTS, WEIGHTS).reshape(16)


def split3(array):
    high = np.asarray(array, np.float32).astype(jnp.bfloat16)
    rest = np.asarray(array, np.float32) - high.astype(np.float32)
    middle = rest.astype(jnp.bfloat16)
    low = (rest - middle.astype(np.float32)).astype(jnp.bfloat16)
    return high, middle, low


def node_matrices():
    identity = np.eye(4)
    return np.concatenate(
        [
            np.kron(DERIV, np.kron(identity, identity)),
            np.kron(identity, np.kron(DERIV, identity)),
            np.kron(identity, np.kron(identity, DERIV)),
        ]
    )


def face_node(face, m):
    axis, layer = face // 2, 3 * (face % 2)
    a, b = m // 4, m % 4
    digits = [a, b]
    digits.insert(axis, layer)
    return 16 * digits[0] + 4 * digits[1] + digits[2]


def flow_matrix():
    table = np.zeros((3, 16, NODES), np.float32)
    for face in range(6):
        row = np.zeros(NODES)
        for m in range(16):
            row[face_node(face, m)] = FACE_W[m] * (2 * (face % 2) - 1)
        for part, values in enumerate(split3(row)):
            table[face // 2, 8 * (face % 2) + part] = values.astype(np.float32)
    return table.reshape(48, NODES)


def x_rows(comp, node, half):
    start = (comp * OBJ * 8 + node // 8) * 16 + half * 8 + node % 8
    return pl.ds(start, OBJ, stride=LANES)


def lane_slice(half):
    return slice(half * LANES, (half + 1) * LANES)


def slot_columns(link_ref, outlet_ref, square):
    square[...] = jnp.full((LANES, LANES), -1.0, F32)
    for level in range(LEVELS):
        square[level : level + 1, 0:CAP] = link_ref[level].astype(F32)
    square[LEVELS : LEVELS + 1, 0:CAP] = outlet_ref[...].astype(F32)
    turned = jnp.transpose(square[...])
    return jnp.concatenate(
        [
            jnp.broadcast_to(turned[0:CAP, b : b + 1], (CAP, LANES))
            for b in range(LEVELS + 1)
        ],
        axis=0,
    )


def one_hot(columns, face):
    lane = lax.broadcasted_iota(jnp.int32, columns.shape, 1).astype(F32)
    parts = [
        jnp.where(columns == lane + float(face * ELEMS + half * LANES), 1.0, 0.0)
        for half in range(2)
    ]
    return jnp.concatenate(parts, axis=1).astype(BF16)


def split2(value):
    high = value.astype(BF16)
    return high, (value - high.astype(F32)).astype(BF16)


NT = (((1,), (1,)), ((), ()))


def comp_traces(x_ref, comp):
    for face in range(6):
        for m in range(0, 16, 2):
            row = (comp * 16 + m) * OBJ
            for half in range(2):
                pair = jnp.concatenate(
                    [x_ref[x_rows(comp, face_node(face, m + i), half), :] for i in range(2)],
                    axis=0,
                )
                yield face, row, half, split2(pair)


def gather_kernel(
    x_any, vel_any, scale_any, link_any, outlet_any, ids_any, res_any, flow_any, count_any,
    message_ref, live_ref, s0_ref, s1_ref, s2_ref, s3_ref, s4_ref, s5_ref, s6_ref,
    x_ref, vel_ref, scale_ref, link_ref, outlet_ref, ids_ref, res_ref, flow_ref, count_ref,
    traces, square, stats, total, stat_total, sems,
):
    small = (
        (link_any, link_ref), (outlet_any, outlet_ref), (vel_any, vel_ref),
        (scale_any, scale_ref), (flow_any, flow_ref), (ids_any, ids_ref), (res_any, res_ref),
        (count_any, count_ref),
    )
    copies = [
        pltpu.make_async_copy(src, dst, sems.at[4 + i]) for i, (src, dst) in enumerate(small)
    ]
    blocks = [
        pltpu.make_async_copy(
            x_any.at[pl.ds(c * 1024, 1024), :], x_ref.at[pl.ds(c * 1024, 1024), :], sems.at[c]
        )
        for c in range(COMPS)
    ]
    for copy in blocks + copies:
        copy.start()
    stats[...] = jnp.zeros_like(stats)
    for comp in range(COMPS):
        blocks[comp].wait()
        for face, row, half, (high, low) in comp_traces(x_ref, comp):
            traces[face * 1024 + row : face * 1024 + row + 16, lane_slice(half)] = high
            traces[face * 1024 + 512 + row : face * 1024 + 528 + row, lane_slice(half)] = low
    for copy in copies:
        copy.wait()
    element = lax.broadcasted_iota(jnp.int32, (8, ELEMS), 1)
    live_ref[...] = jnp.where(element < count_ref[0], 1.0, 0.0)
    columns = slot_columns(link_ref, outlet_ref, square)
    for face in range(6):
        pick = one_hot(columns, face)
        both = lax.dot_general(
            pick, traces[face * 1024 : (face + 1) * 1024, :], NT, preferred_element_type=F32
        )
        both = both[:, :512] + both[:, 512:]
        total[...] = both if face == 0 else total[...] + both
        axis, sign = face // 2, 2.0 * (face % 2) - 1.0
        scale = scale_ref[face : face + 1, :]
        flow = jnp.dot(
            flow_ref[16 * axis : 16 * axis + 16, :], vel_ref[axis], preferred_element_type=F32
        )
        first = 8 * (face % 2)
        flow = (flow[first : first + 1] + flow[first + 1 : first + 2]) + flow[
            first + 2 : first + 3
        ]
        stats[0:1, :] = scale * sign
        stats[1:2, :] = flow * scale
        part = lax.dot_general(
            pick[LEVELS * CAP :].astype(F32), stats[...], NT,
            precision=HIGHEST, preferred_element_type=F32,
        )
        stat_total[...] = part if face == 0 else stat_total[...] + part
    for level, ref in enumerate((s0_ref, s1_ref, s2_ref, s3_ref, s4_ref, s5_ref, s6_ref)):
        for comp in range(COMPS):
            ref[comp * CAP : (comp + 1) * CAP, :] = total[
                level * CAP : (level + 1) * CAP, comp * LANES : (comp + 1) * LANES
            ]
    lane = lax.broadcasted_iota(jnp.int32, (CAP, LANES), 1)
    outlet_ids = columns[LEVELS * CAP :]
    axis = jnp.floor(outlet_ids * (1.0 / (2 * ELEMS)))
    moment = jnp.zeros((CAP, LANES), F32)
    for comp in range(3):
        moment += jnp.where(
            axis == float(comp), total[LEVELS * CAP :, comp * LANES : (comp + 1) * LANES], 0.0
        )
    node = lane[0:1] // OBJ
    weight = jnp.zeros((1, LANES), F32)
    for m in range(16):
        weight = jnp.where(node == m, float(FACE_W[m]), weight)
    moment = moment * weight
    for shift in (8, 16, 32, 64):
        moment = moment + pltpu.roll(moment, shift, 1)
    moment = moment * jnp.broadcast_to(stat_total[:, 0:1], (CAP, LANES))
    moment = jnp.where(
        lane < OBJ, moment,
        jnp.where(lane == OBJ, jnp.broadcast_to(stat_total[:, 1:2], (CAP, LANES)), 0.0),
    )
    spread = lax.broadcasted_iota(jnp.int32, (LANES, 4 * LANES), 0)
    group = lax.broadcasted_iota(jnp.int32, (LANES, 4 * LANES), 1) // CAP
    wide = jnp.dot(
        moment, jnp.where(spread == group, 1.0, 0.0), precision=HIGHEST,
        preferred_element_type=F32,
    )
    slot = lax.broadcasted_iota(jnp.int32, (CAP, 4 * LANES), 0)
    within = lax.broadcasted_iota(jnp.int32, (CAP, 4 * LANES), 1) % CAP
    flat = jnp.sum(jnp.where(slot == within, wide, 0.0), axis=0, keepdims=True)
    square[0:8, :] = jnp.zeros((8, LANES), F32)
    square[0:1, 0:CAP] = ids_ref[...].astype(F32)
    square[1:3, 0:OBJ] = res_ref[...]
    head = square[0:8, :]
    extra = (
        pltpu.roll(head, 32, 1)[0:1] + pltpu.roll(head, 64, 1)[1:2] + pltpu.roll(head, 72, 1)[2:3]
    )
    message = jnp.concatenate(
        [
            flat[:, 0:LANES],
            flat[:, LANES : 2 * LANES],
            flat[:, 2 * LANES : 3 * LANES] + extra,
            jnp.zeros((1, LANES), F32),
        ],
        axis=0,
    )
    double = jnp.concatenate([message, message], axis=0)
    for peer in range(64):
        message_ref[peer * 8 : (peer + 1) * 8, :] = double


def line_nodes(direction, line):
    p, q = line // 4, line % 4
    if direction == 0:
        return [16 * i + 4 * p + q for i in range(4)]
    if direction == 1:
        return [16 * p + 4 * i + q for i in range(4)]
    return [16 * p + 4 * q + i for i in range(4)]


def even_odd(v):
    return v[0] + v[3], v[1] + v[2], v[0] - v[3], v[1] - v[2]


STIFF = DERIV.T @ DERIV
EP, EQ = [0.5 * (DERIV[r, 0] - DERIV[3 - r, 0]) for r in range(2)]
OS = [0.5 * (DERIV[0, i] + DERIV[3, i]) for i in range(2)]
OT = [0.5 * (DERIV[1, i] + DERIV[2, i]) for i in range(2)]
KE = 0.5 * (STIFF[0, 0] + STIFF[0, 3])
KP = [0.5 * (STIFF[i, 0] - STIFF[i, 3]) for i in range(2)]
KQ = [0.5 * (STIFF[i, 1] - STIFF[i, 2]) for i in range(2)]


def transposed_parts(y):
    s, t, p, q = even_odd(y)
    even = float(EP) * p + float(EQ) * q
    odd = [float(OS[i]) * s + float(OT[i]) * t for i in range(2)]
    return even, odd


def combine(even, odd):
    return [odd[0] + even, odd[1] - even, -even - odd[1], even - odd[0]]


def acc_rows(comp, node, half):
    return pl.ds(((half * COMPS + comp) * NODES + node) * 8, 8)


def spread_row(ref, row):
    return ref[pl.ds(row, 8, stride=0), :]


def resolve_outlets(ids_ref, messages_ref, square, gathered, mult_ref, outlet_ref):
    rank = lax.axis_index("dom").astype(jnp.int32)
    for q in range(3):
        rows = messages_ref[pl.ds(q, LANES, stride=MSG), :]
        gathered[q * LANES : (q + 1) * LANES, :] = jnp.transpose(rows)
    square[...] = jnp.zeros((LANES, LANES), F32)
    square[0:1, 0:CAP] = ids_ref[...].astype(F32)
    own_ids = jnp.transpose(square[...])[0:CAP, 0:1]
    sub = lax.broadcasted_iota(jnp.int32, (8, LANES), 0)
    wanted = jnp.concatenate(
        [(rank * 8 + sub).astype(F32), jnp.broadcast_to(own_ids, (CAP, LANES))], axis=0
    )

    def step(t, sums):
        hit = [
            wanted[g * 8 : g * 8 + 8] == spread_row(gathered, 2 * LANES + CAP + t)
            for g in range(5)
        ]
        new = []
        for r in range(9):
            row = spread_row(gathered, r * CAP + t)
            for g in range(5):
                new.append(sums[r * 5 + g] + jnp.where(hit[g], row, 0.0))
        return tuple(new)

    sums = lax.fori_loop(
        0, CAP, step, tuple(jnp.zeros((8, LANES), F32) for _ in range(45))
    )
    device = lax.broadcasted_iota(jnp.int32, (8, LANES), 1).astype(F32)
    for g in range(5):
        linear = jnp.zeros((8, LANES), F32)
        quadratic = jnp.zeros((8, LANES), F32)
        for q in range(8):
            hit = wanted[g * 8 : g * 8 + 8] == device * 8.0 + float(q)
            linear += jnp.where(hit, spread_row(gathered, 2 * LANES + 64 + q), 0.0)
            quadratic += jnp.where(hit, spread_row(gathered, 2 * LANES + 72 + q), 0.0)
        flow = jnp.sum(sums[8 * 5 + g], axis=1, keepdims=True)
        factor = jnp.sum(linear, axis=1, keepdims=True) + 2.0 * jnp.sum(
            quadratic, axis=1, keepdims=True
        ) * jnp.abs(flow)
        lane = lax.broadcasted_iota(jnp.int32, (8, LANES), 1)
        table = jnp.zeros((8, LANES), F32)
        for o in range(OBJ):
            adj = jnp.sum(sums[o * 5 + g], axis=1, keepdims=True)
            table = jnp.where(lane == o, factor * adj, table)
        if g == 0:
            square[...] = jnp.zeros((LANES, LANES), F32)
            square[0:8, :] = table
            mult_ref[...] = jnp.transpose(square[...])[0:8, 0:8]
        else:
            outlet_ref[(g - 1) * 8 : g * 8, :] = table


def volume_kernel(
    x_ref, vel_ref, metric_ref, scale_ref, deriv_ref, ids_ref, messages_ref,
    acc_ref, mult_ref, outlet_ref,
    work, flux, plain, grads, square, gathered,
):
    resolve_outlets(ids_ref, messages_ref, square, gathered, mult_ref, outlet_ref)
    for j in range(3):
        product = jnp.dot(deriv_ref[...], vel_ref[j], preferred_element_type=F32)
        product = (product[0:192] + product[192:384]) + product[384:576]
        velocity = vel_ref[j].astype(F32)
        for half in range(2):
            cut = lane_slice(half)
            row = (j * 2 + half) * NODES
            plain[row : row + NODES, :] = velocity[:, cut]
            flux[row : row + NODES, :] = velocity[:, cut] * metric_ref[j : j + 1, cut]
            for c in range(3):
                row = ((c * 3 + j) * 2 + half) * NODES
                grads[row : row + NODES, :] = (
                    product[c * NODES : (c + 1) * NODES, cut] * metric_ref[c : c + 1, cut]
                )
    for half in range(2):
        cut = lane_slice(half)
        for direction in range(3):
            gain = jnp.broadcast_to(metric_ref[direction : direction + 1, cut], (8, LANES))
            visc = float(VISCOUS) * gain * gain
            v_even = visc * float(KE)
            v_p = [visc * float(KP[i]) for i in range(2)]
            v_q = [visc * float(KQ[i]) for i in range(2)]
            for line in range(16):
                nodes = line_nodes(direction, line)
                values = []
                for comp in range(COMPS):
                    if direction == 0:
                        loaded = [x_ref[x_rows(comp, n, half), :] for n in nodes]
                        for n, v in zip(nodes, loaded):
                            work[acc_rows(comp, n, half), :] = v
                    else:
                        loaded = [work[acc_rows(comp, n, half), :] for n in nodes]
                    values.append(loaded)
                base = (direction * 2 + half) * NODES
                speed = [spread_row(flux, base + n) for n in nodes]
                for comp in range(COMPS):
                    if comp < 3:
                        y = [speed[i] * values[comp][i] for i in range(4)]
                        if comp == direction:
                            y = [y[i] + gain * values[3][i] for i in range(4)]
                        even, odd = transposed_parts(y)
                        s, t, p, q = even_odd(values[comp])
                        even = even + v_even * (s - t)
                        odd = [odd[i] + (v_p[i] * p + v_q[i] * q) for i in range(2)]
                    else:
                        even, odd = transposed_parts(values[direction])
                        even = gain * even
                        odd = [gain * odd[i] for i in range(2)]
                    out = combine(even, odd)
                    for i, n in enumerate(nodes):
                        result = out[i]
                        if direction > 0:
                            result = result + acc_ref[acc_rows(comp, n, half), :]
                        acc_ref[acc_rows(comp, n, half), :] = result
        for n in range(NODES):
            values = [work[acc_rows(comp, n, half), :] for comp in range(COMPS)]
            digits = (n // 16, (n // 4) % 4, n % 4)
            inner = None
            for d in range(3):
                if digits[d] in (0, 3):
                    face = 2 * d + digits[d] // 3
                    speed = spread_row(plain, (d * 2 + half) * NODES + n)
                    part = jnp.maximum(-speed if face % 2 else speed, 0.0) + float(PENALTY)
                    part = part * jnp.broadcast_to(
                        scale_ref[face : face + 1, cut], (8, LANES)
                    )
                    inner = part if inner is None else inner + part
            for comp in range(COMPS):
                result = acc_ref[acc_rows(comp, n, half), :]
                if comp < 3:
                    for j in range(3):
                        grad = spread_row(grads, ((comp * 3 + j) * 2 + half) * NODES + n)
                        result = result + grad * values[j]
                if inner is not None:
                    result = result + inner * values[comp]
                acc_ref[acc_rows(comp, n, half), :] = result


def outer_gain(vel_row, scale_row, face):
    signed = vel_row if face % 2 else -vel_row
    return scale_row * (jnp.maximum(signed, 0.0) + float(PENALTY))


def fill_plain(vel_ref, plain):
    for d in range(3):
        velocity = vel_ref[d].astype(F32)
        for half in range(2):
            row = (d * 2 + half) * NODES
            plain[row : row + NODES, :] = velocity[:, lane_slice(half)]


def touching(node):
    digits = [node // 16, (node // 4) % 4, node % 4]
    found = []
    for d in range(3):
        if digits[d] in (0, 3):
            rest = digits[:d] + digits[d + 1 :]
            found.append((2 * d + digits[d] // 3, 4 * rest[0] + rest[1]))
    return found


def node_gain(plain, scale_ref, face, node, half):
    scale = jnp.broadcast_to(scale_ref[face : face + 1, lane_slice(half)], (8, LANES))
    return outer_gain(spread_row(plain, ((face // 2) * 2 + half) * NODES + node), scale, face)


def final_kernel(
    live_ref, x_ref, acc_ref, vel_ref, scale_ref, partner_ref, link_ref, outlet_ref,
    mult_ref, s0_ref, s1_ref, s2_ref, s3_ref, s4_ref, s5_ref, s6_ref,
    out_any,
    out_ref, traces, chosen, square, slots, turned, outer, outlet, plain, sem_out,
):
    columns = slot_columns(link_ref, outlet_ref, square)
    fill_plain(vel_ref, plain)
    slots[0 : LEVELS * CAP, 4 * LANES :] = jnp.zeros((LEVELS * CAP, LANES), F32)
    slots[LEVELS * CAP :, 4 * LANES :] = mult_ref[...]
    slots[LEVELS * CAP :, 0 : 4 * LANES] = jnp.zeros((CAP, 4 * LANES), F32)
    for level, ref in enumerate((s0_ref, s1_ref, s2_ref, s3_ref, s4_ref, s5_ref, s6_ref)):
        for comp in range(COMPS):
            slots[level * CAP : (level + 1) * CAP, comp * LANES : (comp + 1) * LANES] = ref[
                comp * CAP : (comp + 1) * CAP, :
            ]
    local_faces = 6 * ELEMS
    for comp in range(COMPS):
        for face, row, half, (high, low) in comp_traces(x_ref, comp):
            cols = slice(face * ELEMS + half * LANES, face * ELEMS + (half + 1) * LANES)
            traces[row : row + 16, cols] = high
            traces[512 + row : 528 + row, cols] = low
        high, low = split2(jnp.transpose(slots[:, comp * LANES : (comp + 1) * LANES]))
        traces[comp * LANES : (comp + 1) * LANES, local_faces:] = high
        traces[512 + comp * LANES : 512 + (comp + 1) * LANES, local_faces:] = low
    high, low = split2(jnp.transpose(slots[:, 4 * LANES :])[0:16])
    turned[0:16, :] = high
    turned[16:32, :] = low
    ids = lax.broadcasted_iota(jnp.int32, (ELEMS, ELEMS), 0)
    for face in range(6):
        target = partner_ref[face : face + 1, :]
        for source in range(6):
            chosen[source * ELEMS : (source + 1) * ELEMS, :] = jnp.where(
                ids == target - source * ELEMS, 1.0, 0.0
            ).astype(BF16)
        pick = one_hot(columns, face)
        chosen[local_faces:, :] = pick
        both = jnp.dot(traces[...], chosen[...], preferred_element_type=F32)
        outer[face * 512 : (face + 1) * 512, :] = both[:512] + both[512:]
        both = jnp.dot(turned[...], pick, preferred_element_type=F32)
        scale = scale_ref[face : face + 1, :] * (2.0 * (face % 2) - 1.0)
        outlet[face * 8 : (face + 1) * 8, :] = (both[0:8] + both[16:24]) * scale
    live = [live_ref[:, lane_slice(half)] > 0.5 for half in range(2)]
    flat = out_ref.reshape(4096, LANES)
    stores = []
    for high in range(8):
        for half in range(2):
            cut = lane_slice(half)
            for n in range(high * 8, high * 8 + 8):
                results = [acc_ref[acc_rows(comp, n, half), :] for comp in range(COMPS)]
                for face, m in touching(n):
                    gain = node_gain(plain, scale_ref, face, n, half)
                    for comp in range(COMPS):
                        row = face * 512 + (comp * 16 + m) * OBJ
                        results[comp] = results[comp] - gain * outer[row : row + 8, cut]
                    axis = face // 2
                    results[axis] = (
                        results[axis] + float(FACE_W[m]) * outlet[face * 8 : face * 8 + 8, cut]
                    )
                for comp in range(COMPS):
                    flat[x_rows(comp, n, half), :] = jnp.where(live[half], results[comp], 0.0)
        store = pltpu.make_async_copy(
            out_ref.at[:, high], out_any.at[:, high], sem_out.at[high]
        )
        store.start()
        stores.append(store)
    for store in stores:
        store.wait()


VMEM = pl.BlockSpec(memory_space=pltpu.VMEM)
ANY = pl.BlockSpec(memory_space=pltpu.MemorySpace.HBM)


def params(mebibytes):
    return pltpu.CompilerParams(vmem_limit_bytes=mebibytes * 2**20)


def cost(microseconds):
    return pl.CostEstimate(
        flops=int(microseconds * 1e3), bytes_accessed=int(microseconds * 3.0e6), transcendentals=0
    )


def f32(*shape):
    return jax.ShapeDtypeStruct(shape, F32)


def local(
    adjoint, velocity, metric, face_scale, resistance, elem_count, face_partner, link_face,
    outlet_face, outlet_id,
):
    x_view = (
        adjoint.reshape(COMPS, OBJ, 8, 8, 2, LANES).transpose(0, 1, 2, 4, 3, 5).reshape(4096, LANES)
    )
    link = link_face.transpose(1, 0, 2)
    deriv = jnp.asarray(np.concatenate(split3(node_matrices())), BF16)
    flow = jnp.asarray(flow_matrix(), BF16)
    devices = lax.axis_size("dom")

    message, live, *sent = pl.pallas_call(
        gather_kernel,
        out_shape=(f32(devices * MSG, LANES), f32(8, ELEMS)) + (f32(FACE_ROWS, LANES),) * LEVELS,
        in_specs=[ANY] * 9,
        out_specs=(VMEM,) * (2 + LEVELS),
        scratch_shapes=[
            pltpu.VMEM((4096, LANES), F32), pltpu.VMEM((3, NODES, ELEMS), BF16),
            pltpu.VMEM((6, ELEMS), F32), pltpu.VMEM((LEVELS, 1, CAP), jnp.int32),
            pltpu.VMEM((1, CAP), jnp.int32), pltpu.VMEM((1, CAP), jnp.int32),
            pltpu.VMEM((2, OBJ), F32), pltpu.VMEM((48, NODES), BF16),
            pltpu.SMEM((1,), jnp.int32),
            pltpu.VMEM((6 * 1024, ELEMS), BF16), pltpu.VMEM((LANES, LANES), F32),
            pltpu.VMEM((LANES, ELEMS), F32), pltpu.VMEM((256, 512), F32),
            pltpu.VMEM((CAP, LANES), F32), pltpu.SemaphoreType.DMA((12,)),
        ],
        compiler_params=params(60),
        cost_estimate=cost(5),
        name="gather",
    )(x_view, velocity, face_scale, link, outlet_face, outlet_id, resistance, flow,
      elem_count)

    messages = lax.all_to_all(
        message.reshape(devices, MSG, LANES), "dom", split_axis=0, concat_axis=0, tiled=True
    ).reshape(devices * MSG, LANES)
    received = [
        lax.ppermute(block, "dom", [(i, i ^ (1 << level)) for i in range(devices)])
        for level, block in enumerate(sent)
    ]

    acc, multiplier, outlet_terms = pl.pallas_call(
        volume_kernel,
        out_shape=(f32(4096, LANES), f32(OBJ, 8), f32(CAP, LANES)),
        in_specs=[VMEM] * 7,
        out_specs=(VMEM,) * 3,
        scratch_shapes=[
            pltpu.VMEM((4096, LANES), F32), pltpu.VMEM((384, LANES), F32),
            pltpu.VMEM((384, LANES), F32), pltpu.VMEM((1152, LANES), F32),
            pltpu.VMEM((LANES, LANES), F32), pltpu.VMEM((384, LANES), F32),
        ],
        compiler_params=params(12),
        cost_estimate=cost(5),
        name="volume",
    )(x_view, velocity, metric, face_scale, deriv, outlet_id, messages)

    out = pl.pallas_call(
        final_kernel,
        out_shape=f32(32, 8, 16, LANES),
        in_specs=[VMEM] * 16,
        out_specs=ANY,
        scratch_shapes=[
            pltpu.VMEM((32, 8, 16, LANES), F32),
            pltpu.VMEM((1024, 7 * ELEMS), BF16), pltpu.VMEM((7 * ELEMS, ELEMS), BF16),
            pltpu.VMEM((LANES, LANES), F32), pltpu.VMEM((256, 640), F32),
            pltpu.VMEM((32, ELEMS), BF16), pltpu.VMEM((6 * 512, ELEMS), F32),
            pltpu.VMEM((48, ELEMS), F32), pltpu.VMEM((384, LANES), F32),
            pltpu.SemaphoreType.DMA((8,)),
        ],
        compiler_params=params(20),
        cost_estimate=cost(9),
        name="finish",
    )(
        live, x_view, acc, velocity, face_scale, face_partner, link, outlet_face,
        outlet_terms, *received,
    )
    out = (
        out.reshape(COMPS, OBJ, 8, 2, 8, LANES).transpose(0, 1, 2, 4, 3, 5)
        .reshape(COMPS, OBJ, NODES, ELEMS)
    )
    return out, multiplier


def solution(mesh):
    placed = (
        P(None, None, None, "dom"), P(None, None, "dom"), P(None, "dom"), P(None, "dom"),
        P(None, "dom"), P("dom"), P(None, "dom"), P("dom", None, None), P("dom", None),
        P("dom", None),
    )
    return jax.shard_map(
        local, mesh=mesh, in_specs=placed,
        out_specs=(P(None, None, None, "dom"), P(None, "dom")), check_vma=False,
    )
```

```python
import math

import jax
import jax.numpy as jnp
import numpy as np
from jax import lax
from jax.experimental import pallas as pl
from jax.experimental.pallas import tpu as pltpu
from jax.sharding import PartitionSpec as P


F32 = jnp.float32
BF16 = jnp.bfloat16
VISCOUS = 0.05
PENALTY = 1.0
COMPS, OBJ, NODES, ELEMS = 4, 8, 64, 256
LANES = 128
CAP, LEVELS = 32, 7
FACE_ROWS = COMPS * CAP
MSG = 4
HIGHEST = lax.Precision.HIGHEST


def gll_tables():
    root_five = math.sqrt(5.0)
    points = np.array([-1.0, -1.0 / root_five, 1.0 / root_five, 1.0])
    weights = np.array([1.0, 5.0, 5.0, 1.0]) / 6.0
    products = np.array(
        [np.prod([points[i] - points[k] for k in range(4) if k != i]) for i in range(4)]
    )
    derivative = np.zeros((4, 4))
    for i in range(4):
        for j in range(4):
            if i != j:
                derivative[i, j] = products[i] / (products[j] * (points[i] - points[j]))
        derivative[i, i] = -np.sum(derivative[i])
    return (derivative, weights)


DERIV, WEIGHTS = gll_tables()
FACE_W = np.outer(WEIGHTS, WEIGHTS).reshape(16)


def split3(array):
    high = np.asarray(array, np.float32).astype(jnp.bfloat16)
    rest = np.asarray(array, np.float32) - high.astype(np.float32)
    middle = rest.astype(jnp.bfloat16)
    low = (rest - middle.astype(np.float32)).astype(jnp.bfloat16)
    return high, middle, low


def node_matrices():
    identity = np.eye(4)
    return np.concatenate(
        [
            np.kron(DERIV, np.kron(identity, identity)),
            np.kron(identity, np.kron(DERIV, identity)),
            np.kron(identity, np.kron(identity, DERIV)),
        ]
    )


def face_node(face, m):
    axis, layer = face // 2, 3 * (face % 2)
    a, b = m // 4, m % 4
    digits = [a, b]
    digits.insert(axis, layer)
    return 16 * digits[0] + 4 * digits[1] + digits[2]


def flow_matrix():
    table = np.zeros((3, 16, NODES), np.float32)
    for face in range(6):
        row = np.zeros(NODES)
        for m in range(16):
            row[face_node(face, m)] = FACE_W[m] * (2 * (face % 2) - 1)
        for part, values in enumerate(split3(row)):
            table[face // 2, 8 * (face % 2) + part] = values.astype(np.float32)
    return table.reshape(48, NODES)


def lane_slice(half):
    return slice(half * LANES, (half + 1) * LANES)


def slot_columns(link_ref, outlet_ref, square):
    square[...] = jnp.full((LANES, LANES), -1.0, F32)
    for level in range(LEVELS):
        square[level : level + 1, 0:CAP] = link_ref[level].astype(F32)
    square[LEVELS : LEVELS + 1, 0:CAP] = outlet_ref[...].astype(F32)
    turned = jnp.transpose(square[...])
    return jnp.concatenate(
        [
            jnp.broadcast_to(turned[0:CAP, b : b + 1], (CAP, LANES))
            for b in range(LEVELS + 1)
        ],
        axis=0,
    )


def one_hot(columns, face):
    lane = lax.broadcasted_iota(jnp.int32, columns.shape, 1).astype(F32)
    parts = [
        jnp.where(columns == lane + float(face * ELEMS + half * LANES), 1.0, 0.0)
        for half in range(2)
    ]
    return jnp.concatenate(parts, axis=1).astype(BF16)


def split2(value):
    high = value.astype(BF16)
    return high, (value - high.astype(F32)).astype(BF16)


NT = (((1,), (1,)), ((), ()))


def node_major(x_ref, work_ref, comp):
    for high in range(8):
        for half in range(2):
            block = jnp.stack(
                [
                    x_ref[pl.ds(((comp * OBJ + o) * 8 + high) * 16 + half * 8, 8), :]
                    for o in range(OBJ)
                ]
            )
            start = acc_rows(comp, high * 8, half).start
            work_ref[pl.ds(start, 64), :] = jnp.swapaxes(block, 0, 1).reshape(64, LANES)


def comp_traces(work_ref, comp):
    for face in range(6):
        for m in range(0, 16, 2):
            row = (comp * 16 + m) * OBJ
            for half in range(2):
                pair = jnp.concatenate(
                    [work_ref[acc_rows(comp, face_node(face, m + i), half), :] for i in range(2)],
                    axis=0,
                )
                yield face, row, half, split2(pair)


def gather_kernel(
    x_any, vel_any, scale_any, link_any, outlet_any, ids_any, res_any, flow_any, count_any,
    message_ref, live_ref, work_ref, s0_ref, z_ref, y_ref, x_out_ref,
    x_ref, vel_ref, scale_ref, link_ref, outlet_ref, ids_ref, res_ref, flow_ref, count_ref,
    traces, square, stats, total, stat_total, sems,
):
    small = (
        (link_any, link_ref), (outlet_any, outlet_ref), (vel_any, vel_ref),
        (scale_any, scale_ref), (flow_any, flow_ref), (ids_any, ids_ref), (res_any, res_ref),
        (count_any, count_ref),
    )
    copies = [
        pltpu.make_async_copy(src, dst, sems.at[4 + i]) for i, (src, dst) in enumerate(small)
    ]
    blocks = [
        pltpu.make_async_copy(
            x_any.at[pl.ds(c * 1024, 1024), :], x_ref.at[pl.ds(c * 1024, 1024), :], sems.at[c]
        )
        for c in range(COMPS)
    ]
    for copy in blocks + copies:
        copy.start()
    stats[...] = jnp.zeros_like(stats)
    for comp in range(COMPS):
        blocks[comp].wait()
        node_major(x_ref, work_ref, comp)
        for face, row, half, (high, low) in comp_traces(work_ref, comp):
            traces[face * 1024 + row : face * 1024 + row + 16, lane_slice(half)] = high
            traces[face * 1024 + 512 + row : face * 1024 + 528 + row, lane_slice(half)] = low
    for copy in copies:
        copy.wait()
    element = lax.broadcasted_iota(jnp.int32, (8, ELEMS), 1)
    live_ref[...] = jnp.where(element < count_ref[0], 1.0, 0.0)
    columns = slot_columns(link_ref, outlet_ref, square)
    for face in range(6):
        pick = one_hot(columns, face)
        both = lax.dot_general(
            pick, traces[face * 1024 : (face + 1) * 1024, :], NT, preferred_element_type=F32
        )
        both = both[:, :512] + both[:, 512:]
        total[...] = both if face == 0 else total[...] + both
        axis, sign = face // 2, 2.0 * (face % 2) - 1.0
        scale = scale_ref[face : face + 1, :]
        flow = jnp.dot(
            flow_ref[16 * axis : 16 * axis + 16, :], vel_ref[axis], preferred_element_type=F32
        )
        first = 8 * (face % 2)
        flow = (flow[first : first + 1] + flow[first + 1 : first + 2]) + flow[
            first + 2 : first + 3
        ]
        stats[0:1, :] = scale * sign
        stats[1:2, :] = flow * scale
        part = lax.dot_general(
            pick[LEVELS * CAP :].astype(F32), stats[...], NT,
            precision=HIGHEST, preferred_element_type=F32,
        )
        stat_total[...] = part if face == 0 else stat_total[...] + part
    homes = ((s0_ref, 0), (z_ref, 0), (z_ref, 1), (y_ref, 0), (y_ref, 1), (x_out_ref, 0), (x_out_ref, 1))
    for level, (ref, place) in enumerate(homes):
        for comp in range(COMPS):
            row = place * FACE_ROWS + comp * CAP
            ref[row : row + CAP, :] = total[
                level * CAP : (level + 1) * CAP, comp * LANES : (comp + 1) * LANES
            ]
    lane = lax.broadcasted_iota(jnp.int32, (CAP, LANES), 1)
    outlet_ids = columns[LEVELS * CAP :]
    axis = jnp.floor(outlet_ids * (1.0 / (2 * ELEMS)))
    moment = jnp.zeros((CAP, LANES), F32)
    for comp in range(3):
        moment += jnp.where(
            axis == float(comp), total[LEVELS * CAP :, comp * LANES : (comp + 1) * LANES], 0.0
        )
    node = lane[0:1] // OBJ
    weight = jnp.zeros((1, LANES), F32)
    for m in range(16):
        weight = jnp.where(node == m, float(FACE_W[m]), weight)
    moment = moment * weight
    for shift in (8, 16, 32, 64):
        moment = moment + pltpu.roll(moment, shift, 1)
    moment = moment * jnp.broadcast_to(stat_total[:, 0:1], (CAP, LANES))
    moment = jnp.where(
        lane < OBJ, moment,
        jnp.where(lane == OBJ, jnp.broadcast_to(stat_total[:, 1:2], (CAP, LANES)), 0.0),
    )
    spread = lax.broadcasted_iota(jnp.int32, (LANES, 4 * LANES), 0)
    group = lax.broadcasted_iota(jnp.int32, (LANES, 4 * LANES), 1) // CAP
    wide = jnp.dot(
        moment, jnp.where(spread == group, 1.0, 0.0), precision=HIGHEST,
        preferred_element_type=F32,
    )
    slot = lax.broadcasted_iota(jnp.int32, (CAP, 4 * LANES), 0)
    within = lax.broadcasted_iota(jnp.int32, (CAP, 4 * LANES), 1) % CAP
    flat = jnp.sum(jnp.where(slot == within, wide, 0.0), axis=0, keepdims=True)
    square[0:8, :] = jnp.zeros((8, LANES), F32)
    square[0:1, 0:CAP] = ids_ref[...].astype(F32)
    square[1:3, 0:OBJ] = res_ref[...]
    head = square[0:8, :]
    extra = (
        pltpu.roll(head, 32, 1)[0:1] + pltpu.roll(head, 64, 1)[1:2] + pltpu.roll(head, 72, 1)[2:3]
    )
    message = jnp.concatenate(
        [
            flat[:, 0:LANES],
            flat[:, LANES : 2 * LANES],
            flat[:, 2 * LANES : 3 * LANES] + extra,
            jnp.zeros((1, LANES), F32),
        ],
        axis=0,
    )
    double = jnp.concatenate([message, message], axis=0)
    for peer in range(64):
        message_ref[peer * 8 : (peer + 1) * 8, :] = double


def line_nodes(direction, line):
    p, q = line // 4, line % 4
    if direction == 0:
        return [16 * i + 4 * p + q for i in range(4)]
    if direction == 1:
        return [16 * p + 4 * i + q for i in range(4)]
    return [16 * p + 4 * q + i for i in range(4)]


def even_odd(v):
    return v[0] + v[3], v[1] + v[2], v[0] - v[3], v[1] - v[2]


STIFF = DERIV.T @ DERIV
EP, EQ = [0.5 * (DERIV[r, 0] - DERIV[3 - r, 0]) for r in range(2)]
OS = [0.5 * (DERIV[0, i] + DERIV[3, i]) for i in range(2)]
OT = [0.5 * (DERIV[1, i] + DERIV[2, i]) for i in range(2)]
KE = 0.5 * (STIFF[0, 0] + STIFF[0, 3])
KP = [0.5 * (STIFF[i, 0] - STIFF[i, 3]) for i in range(2)]
KQ = [0.5 * (STIFF[i, 1] - STIFF[i, 2]) for i in range(2)]


def transposed_parts(y):
    s, t, p, q = even_odd(y)
    even = float(EP) * p + float(EQ) * q
    odd = [float(OS[i]) * s + float(OT[i]) * t for i in range(2)]
    return even, odd


def combine(even, odd):
    return [odd[0] + even, odd[1] - even, -even - odd[1], even - odd[0]]


def acc_rows(comp, node, half):
    return pl.ds(((half * COMPS + comp) * NODES + node) * 8, 8)


def spread_row(ref, row):
    return ref[pl.ds(row, 8, stride=0), :]


def resolve_outlets(ids_ref, messages_ref, square, gathered, mult_ref, outlet_ref):
    rank = lax.axis_index("dom").astype(jnp.int32)
    for q in range(3):
        rows = messages_ref[pl.ds(q, LANES, stride=MSG), :]
        gathered[q * LANES : (q + 1) * LANES, :] = jnp.transpose(rows)
    square[...] = jnp.zeros((LANES, LANES), F32)
    square[0:1, 0:CAP] = ids_ref[...].astype(F32)
    own_ids = jnp.transpose(square[...])[0:CAP, 0:1]
    sub = lax.broadcasted_iota(jnp.int32, (8, LANES), 0)
    wanted = jnp.concatenate(
        [(rank * 8 + sub).astype(F32), jnp.broadcast_to(own_ids, (CAP, LANES))], axis=0
    )

    def step(t, sums):
        hit = [
            wanted[g * 8 : g * 8 + 8] == spread_row(gathered, 2 * LANES + CAP + t)
            for g in range(5)
        ]
        new = []
        for r in range(9):
            row = spread_row(gathered, r * CAP + t)
            for g in range(5):
                new.append(sums[r * 5 + g] + jnp.where(hit[g], row, 0.0))
        return tuple(new)

    sums = lax.fori_loop(
        0, CAP, step, tuple(jnp.zeros((8, LANES), F32) for _ in range(45))
    )
    device = lax.broadcasted_iota(jnp.int32, (8, LANES), 1).astype(F32)
    for g in range(5):
        linear = jnp.zeros((8, LANES), F32)
        quadratic = jnp.zeros((8, LANES), F32)
        for q in range(8):
            hit = wanted[g * 8 : g * 8 + 8] == device * 8.0 + float(q)
            linear += jnp.where(hit, spread_row(gathered, 2 * LANES + 64 + q), 0.0)
            quadratic += jnp.where(hit, spread_row(gathered, 2 * LANES + 72 + q), 0.0)
        flow = jnp.sum(sums[8 * 5 + g], axis=1, keepdims=True)
        factor = jnp.sum(linear, axis=1, keepdims=True) + 2.0 * jnp.sum(
            quadratic, axis=1, keepdims=True
        ) * jnp.abs(flow)
        lane = lax.broadcasted_iota(jnp.int32, (8, LANES), 1)
        table = jnp.zeros((8, LANES), F32)
        for o in range(OBJ):
            adj = jnp.sum(sums[o * 5 + g], axis=1, keepdims=True)
            table = jnp.where(lane == o, factor * adj, table)
        if g == 0:
            square[...] = jnp.zeros((LANES, LANES), F32)
            square[0:8, :] = table
            mult_ref[...] = jnp.transpose(square[...])[0:8, 0:8]
        else:
            outlet_ref[(g - 1) * 8 : g * 8, :] = table


def volume_kernel(
    work, vel_ref, metric_ref, scale_ref, deriv_ref, ids_ref, messages_ref,
    acc_ref, mult_ref, outlet_ref,
    flux, plain, grads, square, gathered,
):
    resolve_outlets(ids_ref, messages_ref, square, gathered, mult_ref, outlet_ref)
    for j in range(3):
        product = jnp.dot(deriv_ref[...], vel_ref[j], preferred_element_type=F32)
        product = (product[0:192] + product[192:384]) + product[384:576]
        velocity = vel_ref[j].astype(F32)
        for half in range(2):
            cut = lane_slice(half)
            row = (j * 2 + half) * NODES
            plain[row : row + NODES, :] = velocity[:, cut]
            flux[row : row + NODES, :] = velocity[:, cut] * metric_ref[j : j + 1, cut]
            for c in range(3):
                row = ((c * 3 + j) * 2 + half) * NODES
                grads[row : row + NODES, :] = (
                    product[c * NODES : (c + 1) * NODES, cut] * metric_ref[c : c + 1, cut]
                )
    for half in range(2):
        cut = lane_slice(half)
        for direction in range(3):
            gain = jnp.broadcast_to(metric_ref[direction : direction + 1, cut], (8, LANES))
            visc = float(VISCOUS) * gain * gain
            v_even = visc * float(KE)
            v_p = [visc * float(KP[i]) for i in range(2)]
            v_q = [visc * float(KQ[i]) for i in range(2)]
            for line in range(16):
                nodes = line_nodes(direction, line)
                values = []
                for comp in range(COMPS):
                    values.append([work[acc_rows(comp, n, half), :] for n in nodes])
                base = (direction * 2 + half) * NODES
                speed = [spread_row(flux, base + n) for n in nodes]
                for comp in range(COMPS):
                    if comp < 3:
                        y = [speed[i] * values[comp][i] for i in range(4)]
                        if comp == direction:
                            y = [y[i] + gain * values[3][i] for i in range(4)]
                        even, odd = transposed_parts(y)
                        s, t, p, q = even_odd(values[comp])
                        even = even + v_even * (s - t)
                        odd = [odd[i] + (v_p[i] * p + v_q[i] * q) for i in range(2)]
                    else:
                        even, odd = transposed_parts(values[direction])
                        even = gain * even
                        odd = [gain * odd[i] for i in range(2)]
                    out = combine(even, odd)
                    for i, n in enumerate(nodes):
                        result = out[i]
                        if direction > 0:
                            result = result + acc_ref[acc_rows(comp, n, half), :]
                        acc_ref[acc_rows(comp, n, half), :] = result
        for n in range(NODES):
            values = [work[acc_rows(comp, n, half), :] for comp in range(COMPS)]
            digits = (n // 16, (n // 4) % 4, n % 4)
            inner = None
            for d in range(3):
                if digits[d] in (0, 3):
                    face = 2 * d + digits[d] // 3
                    speed = spread_row(plain, (d * 2 + half) * NODES + n)
                    part = jnp.maximum(-speed if face % 2 else speed, 0.0) + float(PENALTY)
                    part = part * jnp.broadcast_to(
                        scale_ref[face : face + 1, cut], (8, LANES)
                    )
                    inner = part if inner is None else inner + part
            for comp in range(COMPS):
                result = acc_ref[acc_rows(comp, n, half), :]
                if comp < 3:
                    for j in range(3):
                        grad = spread_row(grads, ((comp * 3 + j) * 2 + half) * NODES + n)
                        result = result + grad * values[j]
                if inner is not None:
                    result = result + inner * values[comp]
                acc_ref[acc_rows(comp, n, half), :] = result


def outer_gain(vel_row, scale_row, face):
    signed = vel_row if face % 2 else -vel_row
    return scale_row * (jnp.maximum(signed, 0.0) + float(PENALTY))


def fill_plain(vel_ref, plain):
    for d in range(3):
        velocity = vel_ref[d].astype(F32)
        for half in range(2):
            row = (d * 2 + half) * NODES
            plain[row : row + NODES, :] = velocity[:, lane_slice(half)]


def touching(node):
    digits = [node // 16, (node // 4) % 4, node % 4]
    found = []
    for d in range(3):
        if digits[d] in (0, 3):
            rest = digits[:d] + digits[d + 1 :]
            found.append((2 * d + digits[d] // 3, 4 * rest[0] + rest[1]))
    return found


def node_gain(plain, scale_ref, face, node, half):
    scale = jnp.broadcast_to(scale_ref[face : face + 1, lane_slice(half)], (8, LANES))
    return outer_gain(spread_row(plain, ((face // 2) * 2 + half) * NODES + node), scale, face)


def final_kernel(
    live_ref, work_ref, acc_ref, vel_ref, scale_ref, partner_ref, link_ref, outlet_ref,
    mult_ref, s0_ref, s1_ref, s2_ref, s3_ref, s4_ref, s5_ref, s6_ref,
    out_any,
    out_ref, traces, chosen, square, slots, turned, outer, outlet, plain, sem_out,
):
    columns = slot_columns(link_ref, outlet_ref, square)
    fill_plain(vel_ref, plain)
    slots[0 : LEVELS * CAP, 4 * LANES :] = jnp.zeros((LEVELS * CAP, LANES), F32)
    slots[LEVELS * CAP :, 4 * LANES :] = mult_ref[...]
    slots[LEVELS * CAP :, 0 : 4 * LANES] = jnp.zeros((CAP, 4 * LANES), F32)
    for level, ref in enumerate((s0_ref, s1_ref, s2_ref, s3_ref, s4_ref, s5_ref, s6_ref)):
        for comp in range(COMPS):
            row = comp * CAP + (FACE_ROWS if level in (2, 4, 6) else 0)
            slots[level * CAP : (level + 1) * CAP, comp * LANES : (comp + 1) * LANES] = ref[
                row : row + CAP, :
            ]
    local_faces = 6 * ELEMS
    for comp in range(COMPS):
        for face, row, half, (high, low) in comp_traces(work_ref, comp):
            cols = slice(face * ELEMS + half * LANES, face * ELEMS + (half + 1) * LANES)
            traces[row : row + 16, cols] = high
            traces[512 + row : 528 + row, cols] = low
        high, low = split2(jnp.transpose(slots[:, comp * LANES : (comp + 1) * LANES]))
        traces[comp * LANES : (comp + 1) * LANES, local_faces:] = high
        traces[512 + comp * LANES : 512 + (comp + 1) * LANES, local_faces:] = low
    high, low = split2(jnp.transpose(slots[:, 4 * LANES :])[0:16])
    turned[0:16, :] = high
    turned[16:32, :] = low
    ids = lax.broadcasted_iota(jnp.int32, (ELEMS, ELEMS), 0)
    for face in range(6):
        target = partner_ref[face : face + 1, :]
        for source in range(6):
            chosen[source * ELEMS : (source + 1) * ELEMS, :] = jnp.where(
                ids == target - source * ELEMS, 1.0, 0.0
            ).astype(BF16)
        pick = one_hot(columns, face)
        chosen[local_faces:, :] = pick
        both = jnp.dot(traces[...], chosen[...], preferred_element_type=F32)
        outer[face * 512 : (face + 1) * 512, :] = both[:512] + both[512:]
        both = jnp.dot(turned[...], pick, preferred_element_type=F32)
        scale = scale_ref[face : face + 1, :] * (2.0 * (face % 2) - 1.0)
        outlet[face * 8 : (face + 1) * 8, :] = (both[0:8] + both[16:24]) * scale
    live = [live_ref[:, lane_slice(half)] > 0.5 for half in range(2)]
    stores = []
    for high in range(8):
        for half in range(2):
            cut = lane_slice(half)
            block = [[] for _ in range(COMPS)]
            for n in range(high * 8, high * 8 + 8):
                results = [acc_ref[acc_rows(comp, n, half), :] for comp in range(COMPS)]
                for face, m in touching(n):
                    gain = node_gain(plain, scale_ref, face, n, half)
                    for comp in range(COMPS):
                        row = face * 512 + (comp * 16 + m) * OBJ
                        results[comp] = results[comp] - gain * outer[row : row + 8, cut]
                    axis = face // 2
                    results[axis] = (
                        results[axis] + float(FACE_W[m]) * outlet[face * 8 : face * 8 + 8, cut]
                    )
                for comp in range(COMPS):
                    block[comp].append(jnp.where(live[half], results[comp], 0.0))
            for comp in range(COMPS):
                turned_block = jnp.swapaxes(jnp.stack(block[comp]), 0, 1)
                out_ref[comp * OBJ : (comp + 1) * OBJ, high, half * 8 : half * 8 + 8, :] = (
                    turned_block
                )
        store = pltpu.make_async_copy(
            out_ref.at[:, high], out_any.at[:, high], sem_out.at[high]
        )
        store.start()
        stores.append(store)
    for store in stores:
        store.wait()


VMEM = pl.BlockSpec(memory_space=pltpu.VMEM)
ANY = pl.BlockSpec(memory_space=pltpu.MemorySpace.HBM)


def params(mebibytes):
    return pltpu.CompilerParams(vmem_limit_bytes=mebibytes * 2**20)


def cost(microseconds):
    return pl.CostEstimate(
        flops=int(microseconds * 1e3), bytes_accessed=int(microseconds * 3.0e6), transcendentals=0
    )


def f32(*shape):
    return jax.ShapeDtypeStruct(shape, F32)


def local(
    adjoint, velocity, metric, face_scale, resistance, elem_count, face_partner, link_face,
    outlet_face, outlet_id,
):
    x_view = (
        adjoint.reshape(COMPS, OBJ, 8, 8, 2, LANES).transpose(0, 1, 2, 4, 3, 5).reshape(4096, LANES)
    )
    link = link_face.transpose(1, 0, 2)
    deriv = jnp.asarray(np.concatenate(split3(node_matrices())), BF16)
    flow = jnp.asarray(flow_matrix(), BF16)
    devices = lax.axis_size("dom")

    message, live, work, *sent = pl.pallas_call(
        gather_kernel,
        out_shape=(f32(devices * MSG, LANES), f32(8, ELEMS), f32(4096, LANES), f32(FACE_ROWS, LANES))
        + (f32(2 * FACE_ROWS, LANES),) * 3,
        in_specs=[ANY] * 9,
        out_specs=(VMEM,) * 7,
        scratch_shapes=[
            pltpu.VMEM((4096, LANES), F32), pltpu.VMEM((3, NODES, ELEMS), BF16),
            pltpu.VMEM((6, ELEMS), F32), pltpu.VMEM((LEVELS, 1, CAP), jnp.int32),
            pltpu.VMEM((1, CAP), jnp.int32), pltpu.VMEM((1, CAP), jnp.int32),
            pltpu.VMEM((2, OBJ), F32), pltpu.VMEM((48, NODES), BF16),
            pltpu.SMEM((1,), jnp.int32),
            pltpu.VMEM((6 * 1024, ELEMS), BF16), pltpu.VMEM((LANES, LANES), F32),
            pltpu.VMEM((LANES, ELEMS), F32), pltpu.VMEM((256, 512), F32),
            pltpu.VMEM((CAP, LANES), F32), pltpu.SemaphoreType.DMA((12,)),
        ],
        compiler_params=params(60),
        cost_estimate=cost(5),
        name="gather",
    )(x_view, velocity, face_scale, link, outlet_face, outlet_id, resistance, flow,
      elem_count)

    messages = lax.all_to_all(
        message.reshape(devices, MSG, LANES), "dom", split_axis=0, concat_axis=0, tiled=True
    ).reshape(devices * MSG, LANES)
    def swap(block, mask):
        return lax.ppermute(block, "dom", [(i, i ^ mask) for i in range(devices)])

    near = [swap(block, 2 << (2 * axis)) for axis, block in enumerate(sent[1:])]
    far = [swap(block, 6 << (2 * axis)) for axis, block in enumerate(near)]
    received = [swap(sent[0], 1)] + [block for pair in zip(near, far) for block in pair]

    acc, multiplier, outlet_terms = pl.pallas_call(
        volume_kernel,
        out_shape=(f32(4096, LANES), f32(OBJ, 8), f32(CAP, LANES)),
        in_specs=[VMEM] * 7,
        out_specs=(VMEM,) * 3,
        scratch_shapes=[
            pltpu.VMEM((384, LANES), F32), pltpu.VMEM((384, LANES), F32),
            pltpu.VMEM((1152, LANES), F32), pltpu.VMEM((LANES, LANES), F32), pltpu.VMEM((384, LANES), F32),
        ],
        compiler_params=params(12),
        cost_estimate=cost(5),
        name="volume",
    )(work, velocity, metric, face_scale, deriv, outlet_id, messages)

    out = pl.pallas_call(
        final_kernel,
        out_shape=f32(32, 8, 16, LANES),
        in_specs=[VMEM] * 16,
        out_specs=ANY,
        scratch_shapes=[
            pltpu.VMEM((32, 8, 16, LANES), F32),
            pltpu.VMEM((1024, 7 * ELEMS), BF16), pltpu.VMEM((7 * ELEMS, ELEMS), BF16),
            pltpu.VMEM((LANES, LANES), F32), pltpu.VMEM((256, 640), F32),
            pltpu.VMEM((32, ELEMS), BF16), pltpu.VMEM((6 * 512, ELEMS), F32),
            pltpu.VMEM((48, ELEMS), F32), pltpu.VMEM((384, LANES), F32),
            pltpu.SemaphoreType.DMA((8,)),
        ],
        compiler_params=params(20),
        cost_estimate=cost(9),
        name="finish",
    )(
        live, work, acc, velocity, face_scale, face_partner, link, outlet_face,
        outlet_terms, *received,
    )
    out = (
        out.reshape(COMPS, OBJ, 8, 2, 8, LANES).transpose(0, 1, 2, 4, 3, 5)
        .reshape(COMPS, OBJ, NODES, ELEMS)
    )
    return out, multiplier


def solution(mesh):
    placed = (
        P(None, None, None, "dom"), P(None, None, "dom"), P(None, "dom"), P(None, "dom"),
        P(None, "dom"), P("dom"), P(None, "dom"), P("dom", None, None), P("dom", None),
        P("dom", None),
    )
    return jax.shard_map(
        local, mesh=mesh, in_specs=placed,
        out_specs=(P(None, None, None, "dom"), P(None, "dom")), check_vma=False,
    )
```

```python
import math

import jax
import jax.numpy as jnp
import numpy as np
from jax import lax
from jax.experimental import pallas as pl
from jax.experimental.pallas import tpu as pltpu
from jax.sharding import PartitionSpec as P


F32 = jnp.float32
BF16 = jnp.bfloat16
VISCOUS = 0.05
PENALTY = 1.0
COMPS, OBJ, NODES, ELEMS = 4, 8, 64, 256
LANES = 128
CAP, LEVELS = 32, 7
FACE_ROWS = COMPS * CAP
MSG = 4
HIGHEST = lax.Precision.HIGHEST


def gll_tables():
    root_five = math.sqrt(5.0)
    points = np.array([-1.0, -1.0 / root_five, 1.0 / root_five, 1.0])
    weights = np.array([1.0, 5.0, 5.0, 1.0]) / 6.0
    products = np.array(
        [np.prod([points[i] - points[k] for k in range(4) if k != i]) for i in range(4)]
    )
    derivative = np.zeros((4, 4))
    for i in range(4):
        for j in range(4):
            if i != j:
                derivative[i, j] = products[i] / (products[j] * (points[i] - points[j]))
        derivative[i, i] = -np.sum(derivative[i])
    return (derivative, weights)


DERIV, WEIGHTS = gll_tables()
FACE_W = np.outer(WEIGHTS, WEIGHTS).reshape(16)


def split3(array):
    high = np.asarray(array, np.float32).astype(jnp.bfloat16)
    rest = np.asarray(array, np.float32) - high.astype(np.float32)
    middle = rest.astype(jnp.bfloat16)
    low = (rest - middle.astype(np.float32)).astype(jnp.bfloat16)
    return high, middle, low


def node_matrices():
    identity = np.eye(4)
    return np.concatenate(
        [
            np.kron(DERIV, np.kron(identity, identity)),
            np.kron(identity, np.kron(DERIV, identity)),
            np.kron(identity, np.kron(identity, DERIV)),
        ]
    )


def face_node(face, m):
    axis, layer = face // 2, 3 * (face % 2)
    a, b = m // 4, m % 4
    digits = [a, b]
    digits.insert(axis, layer)
    return 16 * digits[0] + 4 * digits[1] + digits[2]


def flow_matrix():
    table = np.zeros((3, 16, NODES), np.float32)
    for face in range(6):
        row = np.zeros(NODES)
        for m in range(16):
            row[face_node(face, m)] = FACE_W[m] * (2 * (face % 2) - 1)
        for part, values in enumerate(split3(row)):
            table[face // 2, 8 * (face % 2) + part] = values.astype(np.float32)
    return table.reshape(48, NODES)


def lane_slice(half):
    return slice(half * LANES, (half + 1) * LANES)


def slot_columns(link_ref, outlet_ref, square):
    square[...] = jnp.full((LANES, LANES), -1.0, F32)
    for level in range(LEVELS):
        square[level : level + 1, 0:CAP] = link_ref[level].astype(F32)
    square[LEVELS : LEVELS + 1, 0:CAP] = outlet_ref[...].astype(F32)
    turned = jnp.transpose(square[...])
    return jnp.concatenate(
        [
            jnp.broadcast_to(turned[0:CAP, b : b + 1], (CAP, LANES))
            for b in range(LEVELS + 1)
        ],
        axis=0,
    )


def one_hot(columns, face):
    lane = lax.broadcasted_iota(jnp.int32, columns.shape, 1).astype(F32)
    parts = [
        jnp.where(columns == lane + float(face * ELEMS + half * LANES), 1.0, 0.0)
        for half in range(2)
    ]
    return jnp.concatenate(parts, axis=1).astype(BF16)


def split2(value):
    high = value.astype(BF16)
    return high, (value - high.astype(F32)).astype(BF16)


NT = (((1,), (1,)), ((), ()))


def node_major(x_ref, work_ref, comp):
    for high in range(8):
        for half in range(2):
            block = jnp.stack(
                [
                    x_ref[pl.ds(((comp * OBJ + o) * 8 + high) * 16 + half * 8, 8), :]
                    for o in range(OBJ)
                ]
            )
            start = acc_rows(comp, high * 8, half).start
            work_ref[pl.ds(start, 64), :] = jnp.swapaxes(block, 0, 1).reshape(64, LANES)


def comp_traces(work_ref, comp):
    for face in range(6):
        for m in range(0, 16, 2):
            row = (comp * 16 + m) * OBJ
            for half in range(2):
                pair = jnp.concatenate(
                    [work_ref[acc_rows(comp, face_node(face, m + i), half), :] for i in range(2)],
                    axis=0,
                )
                yield face, row, half, split2(pair)


def fill_traces(work_ref, traces, comp):
    for face, row, half, (high, low) in comp_traces(work_ref, comp):
        cols = slice(face * ELEMS + half * LANES, face * ELEMS + (half + 1) * LANES)
        traces[row : row + 16, cols] = high
        traces[512 + row : 528 + row, cols] = low


def fill_pick(pick, row):
    sub = lax.broadcasted_iota(jnp.int32, (ELEMS, row.shape[1]), 0).astype(F32)
    for face in range(6):
        pick[face * ELEMS : (face + 1) * ELEMS, :] = jnp.where(
            sub == row - float(face * ELEMS), 1.0, 0.0
        ).astype(BF16)


def parts3(value):
    high = value.astype(BF16).astype(F32)
    rest = value - high
    middle = rest.astype(BF16).astype(F32)
    return high, middle, rest - middle


def gather_kernel(
    x_any, vel_any, scale_any, link_any, outlet_any, ids_any, res_any, flow_any, count_any,
    message_ref, live_ref,
    s0_ref, s1_ref, s2_ref, s3_ref, s4_ref, s5_ref, s6_ref,
    x_ref, vel_ref, scale_ref, link_ref, outlet_ref, ids_ref, res_ref, flow_ref, count_ref,
    work_ref, traces, pick, square, total, sems,
):
    small = (
        (link_any, link_ref), (outlet_any, outlet_ref), (vel_any, vel_ref),
        (scale_any, scale_ref), (flow_any, flow_ref), (ids_any, ids_ref), (res_any, res_ref),
        (count_any, count_ref),
    )
    copies = [
        pltpu.make_async_copy(src, dst, sems.at[4 + i]) for i, (src, dst) in enumerate(small)
    ]
    blocks = [
        pltpu.make_async_copy(
            x_any.at[pl.ds(c * 1024, 1024), :], x_ref.at[pl.ds(c * 1024, 1024), :], sems.at[c]
        )
        for c in range(COMPS)
    ]
    for copy in blocks + copies:
        copy.start()
    for copy in copies:
        copy.wait()
    element = lax.broadcasted_iota(jnp.int32, (8, ELEMS), 1)
    live_ref[...] = jnp.where(element < count_ref[...], 1.0, 0.0)
    square[0:8, :] = jnp.zeros((8, LANES), F32)
    for level in range(LEVELS):
        square[level : level + 1, 0:CAP] = link_ref[level].astype(F32)
    square[LEVELS : LEVELS + 1, 0:CAP] = outlet_ref[...].astype(F32)
    head = square[0:8, :]
    pieces = [
        (pltpu.roll(head, CAP * (b % 4), 1) if b % 4 else head)[b : b + 1] for b in range(8)
    ]
    row = jnp.concatenate([sum(pieces[1:4], pieces[0]), sum(pieces[5:], pieces[4])], axis=1)
    fill_pick(pick, row)
    kind = lax.broadcasted_iota(jnp.int32, (16, ELEMS), 0)
    for face in range(6):
        axis, sign = face // 2, 2.0 * (face % 2) - 1.0
        if face % 2 == 0:
            flows = jnp.dot(
                flow_ref[16 * axis : 16 * axis + 16, :], vel_ref[axis],
                preferred_element_type=F32,
            )
        scale = scale_ref[face : face + 1, :]
        first = 8 * (face % 2)
        flow = (flows[first : first + 1] + flows[first + 1 : first + 2]) + flows[
            first + 2 : first + 3
        ]
        table = jnp.where(kind == 6, float(axis), 0.0)
        for i, part in enumerate(parts3(scale * sign) + parts3(flow * scale)):
            table = jnp.where(kind == i, part, table)
        traces[1024:1040, face * ELEMS : (face + 1) * ELEMS] = table.astype(BF16)
    for comp in range(COMPS):
        blocks[comp].wait()
        node_major(x_ref, work_ref, comp)
        fill_traces(work_ref, traces, comp)
    both = jnp.dot(traces[...], pick[...], preferred_element_type=F32)
    chosen = both[:512] + both[512:1024]
    for comp in range(COMPS):
        for half in range(2):
            total[lane_slice(half), lane_slice(comp)] = jnp.transpose(
                chosen[lane_slice(comp), lane_slice(half)]
            )
    stats = both[1024:1040, LANES:]
    square[...] = jnp.zeros((LANES, LANES), F32)
    square[0:1, :] = (stats[0:1] + stats[1:2]) + stats[2:3]
    square[1:2, :] = (stats[3:4] + stats[4:5]) + stats[5:6]
    square[2:3, :] = stats[6:7]
    stats = jnp.transpose(square[...])[LANES - CAP :]
    homes = (s0_ref, s1_ref, s2_ref, s3_ref, s4_ref, s5_ref, s6_ref)
    for level, ref in enumerate(homes):
        for comp in range(COMPS):
            ref[comp * CAP : (comp + 1) * CAP, :] = total[
                level * CAP : (level + 1) * CAP, comp * LANES : (comp + 1) * LANES
            ]
    lane = lax.broadcasted_iota(jnp.int32, (CAP, LANES), 1)
    axis = jnp.broadcast_to(stats[:, 2:3], (CAP, LANES))
    moment = jnp.zeros((CAP, LANES), F32)
    for comp in range(3):
        moment += jnp.where(
            axis == float(comp), total[LEVELS * CAP :, comp * LANES : (comp + 1) * LANES], 0.0
        )
    node = lane[0:1] // OBJ
    weight = jnp.zeros((1, LANES), F32)
    for m in range(16):
        weight = jnp.where(node == m, float(FACE_W[m]), weight)
    moment = moment * weight
    for shift in (8, 16, 32, 64):
        moment = moment + pltpu.roll(moment, shift, 1)
    moment = moment * jnp.broadcast_to(stats[:, 0:1], (CAP, LANES))
    moment = jnp.where(
        lane < OBJ, moment,
        jnp.where(lane == OBJ, jnp.broadcast_to(stats[:, 1:2], (CAP, LANES)), 0.0),
    )
    spread = lax.broadcasted_iota(jnp.int32, (LANES, 4 * LANES), 0)
    group = lax.broadcasted_iota(jnp.int32, (LANES, 4 * LANES), 1) // CAP
    wide = jnp.dot(
        moment, jnp.where(spread == group, 1.0, 0.0), precision=HIGHEST,
        preferred_element_type=F32,
    )
    slot = lax.broadcasted_iota(jnp.int32, (CAP, 4 * LANES), 0)
    within = lax.broadcasted_iota(jnp.int32, (CAP, 4 * LANES), 1) % CAP
    flat = jnp.sum(jnp.where(slot == within, wide, 0.0), axis=0, keepdims=True)
    square[0:8, :] = jnp.zeros((8, LANES), F32)
    square[0:1, 0:CAP] = ids_ref[...].astype(F32)
    square[1:3, 0:OBJ] = res_ref[...]
    head = square[0:8, :]
    extra = (
        pltpu.roll(head, 32, 1)[0:1] + pltpu.roll(head, 64, 1)[1:2] + pltpu.roll(head, 72, 1)[2:3]
    )
    message = jnp.concatenate(
        [
            flat[:, 0:LANES],
            flat[:, LANES : 2 * LANES],
            flat[:, 2 * LANES : 3 * LANES] + extra,
            jnp.zeros((1, LANES), F32),
        ],
        axis=0,
    )
    double = jnp.concatenate([message, message], axis=0)
    for peer in range(64):
        message_ref[peer * 8 : (peer + 1) * 8, :] = double


def line_nodes(direction, line):
    p, q = line // 4, line % 4
    if direction == 0:
        return [16 * i + 4 * p + q for i in range(4)]
    if direction == 1:
        return [16 * p + 4 * i + q for i in range(4)]
    return [16 * p + 4 * q + i for i in range(4)]


def even_odd(v):
    return v[0] + v[3], v[1] + v[2], v[0] - v[3], v[1] - v[2]


STIFF = DERIV.T @ DERIV
EP, EQ = [0.5 * (DERIV[r, 0] - DERIV[3 - r, 0]) for r in range(2)]
OS = [0.5 * (DERIV[0, i] + DERIV[3, i]) for i in range(2)]
OT = [0.5 * (DERIV[1, i] + DERIV[2, i]) for i in range(2)]
KE = 0.5 * (STIFF[0, 0] + STIFF[0, 3])
KP = [0.5 * (STIFF[i, 0] - STIFF[i, 3]) for i in range(2)]
KQ = [0.5 * (STIFF[i, 1] - STIFF[i, 2]) for i in range(2)]


def transposed_parts(y):
    s, t, p, q = even_odd(y)
    even = float(EP) * p + float(EQ) * q
    odd = [float(OS[i]) * s + float(OT[i]) * t for i in range(2)]
    return even, odd


def combine(even, odd):
    return [odd[0] + even, odd[1] - even, -even - odd[1], even - odd[0]]


def acc_rows(comp, node, half):
    return pl.ds(((half * COMPS + comp) * NODES + node) * 8, 8)


def spread_row(ref, row):
    return ref[pl.ds(row, 8, stride=0), :]


def resolve_outlets(ids_ref, messages_ref, square, gathered, mult_ref, outlet_ref):
    rank = lax.axis_index("dom").astype(jnp.int32)
    for q in range(3):
        rows = messages_ref[pl.ds(q, LANES, stride=MSG), :]
        gathered[q * LANES : (q + 1) * LANES, :] = jnp.transpose(rows)
    square[...] = jnp.zeros((LANES, LANES), F32)
    square[0:1, 0:CAP] = ids_ref[...].astype(F32)
    own_ids = jnp.transpose(square[...])[0:CAP, 0:1]
    sub = lax.broadcasted_iota(jnp.int32, (8, LANES), 0)
    wanted = jnp.concatenate(
        [(rank * 8 + sub).astype(F32), jnp.broadcast_to(own_ids, (CAP, LANES))], axis=0
    )

    def step(t, sums):
        hit = [
            wanted[g * 8 : g * 8 + 8] == spread_row(gathered, 2 * LANES + CAP + t)
            for g in range(5)
        ]
        new = []
        for r in range(9):
            row = spread_row(gathered, r * CAP + t)
            for g in range(5):
                new.append(sums[r * 5 + g] + jnp.where(hit[g], row, 0.0))
        return tuple(new)

    sums = lax.fori_loop(
        0, CAP, step, tuple(jnp.zeros((8, LANES), F32) for _ in range(45))
    )
    device = lax.broadcasted_iota(jnp.int32, (8, LANES), 1).astype(F32)
    for g in range(5):
        linear = jnp.zeros((8, LANES), F32)
        quadratic = jnp.zeros((8, LANES), F32)
        for q in range(8):
            hit = wanted[g * 8 : g * 8 + 8] == device * 8.0 + float(q)
            linear += jnp.where(hit, spread_row(gathered, 2 * LANES + 64 + q), 0.0)
            quadratic += jnp.where(hit, spread_row(gathered, 2 * LANES + 72 + q), 0.0)
        flow = jnp.sum(sums[8 * 5 + g], axis=1, keepdims=True)
        factor = jnp.sum(linear, axis=1, keepdims=True) + 2.0 * jnp.sum(
            quadratic, axis=1, keepdims=True
        ) * jnp.abs(flow)
        lane = lax.broadcasted_iota(jnp.int32, (8, LANES), 1)
        table = jnp.zeros((8, LANES), F32)
        for o in range(OBJ):
            adj = jnp.sum(sums[o * 5 + g], axis=1, keepdims=True)
            table = jnp.where(lane == o, factor * adj, table)
        if g == 0:
            square[...] = jnp.zeros((LANES, LANES), F32)
            square[0:8, :] = table
            mult_ref[...] = jnp.transpose(square[...])[0:8, 0:8]
        else:
            outlet_ref[(g - 1) * 8 : g * 8, :] = table


def gather_pairs(work, partner_ref, pairs_ref, targets_ref, traces, pick):
    partner = partner_ref[...].astype(F32)
    ids = (
        lax.broadcasted_iota(jnp.int32, (6, ELEMS), 1)
        + lax.broadcasted_iota(jnp.int32, (6, ELEMS), 0) * ELEMS
    ).astype(F32)
    first = partner > ids
    flags = jnp.where(first, 1.0, 0.0)
    before = jnp.where(
        lax.broadcasted_iota(jnp.int32, (ELEMS, ELEMS), 0)
        < lax.broadcasted_iota(jnp.int32, (ELEMS, ELEMS), 1),
        1.0, 0.0,
    ).astype(BF16)
    padded = jnp.concatenate([flags, jnp.zeros((10, ELEMS), F32)], axis=0).astype(BF16)
    inside = jnp.dot(padded, before, preferred_element_type=F32)
    number = lax.broadcasted_iota(jnp.int32, (256, LANES), 0).astype(F32)
    offset = jnp.zeros((1, 1), F32)
    ranks = []
    for face in range(6):
        ranks.append(
            jnp.where(first[face : face + 1], inside[face : face + 1] + offset, -1.0)
        )
        offset = offset + jnp.sum(flags[face : face + 1], axis=1, keepdims=True)
    for which, table in enumerate((ids, partner)):
        found = jnp.zeros((256, LANES), F32)
        for face in range(6):
            for half in range(2):
                cut = lane_slice(half)
                found += jnp.where(
                    number == ranks[face][:, cut], table[face : face + 1, cut], 0.0
                )
        column = jnp.sum(found, axis=1, keepdims=True)
        targets_ref[256 * (1 - which) : 256 * (2 - which), :] = jnp.broadcast_to(
            column, (256, LANES)
        )
    row = jnp.concatenate(
        [
            jnp.transpose(targets_ref[start : start + LANES, :])[0:1]
            for start in (256, 384, 0, 128)
        ],
        axis=1,
    )
    fill_pick(pick, row)
    for comp in range(COMPS):
        fill_traces(work, traces, comp)
    pairs_ref[...] = jnp.dot(
        traces[...], pick[...], preferred_element_type=F32
    ).astype(BF16)


def volume_kernel(
    x_ref, vel_ref, metric_ref, scale_ref, deriv_ref, partner_ref, ids_ref, messages_ref,
    acc_ref, mult_ref, outlet_ref, pairs_ref, targets_ref,
    work, flux, plain, grads, square, gathered, traces, pick,
):
    for comp in range(COMPS):
        node_major(x_ref, work, comp)
    resolve_outlets(ids_ref, messages_ref, square, gathered, mult_ref, outlet_ref)
    gather_pairs(work, partner_ref, pairs_ref, targets_ref, traces, pick)
    for j in range(3):
        product = jnp.dot(deriv_ref[...], vel_ref[j], preferred_element_type=F32)
        product = (product[0:192] + product[192:384]) + product[384:576]
        velocity = vel_ref[j].astype(F32)
        for half in range(2):
            cut = lane_slice(half)
            row = (j * 2 + half) * NODES
            plain[row : row + NODES, :] = velocity[:, cut]
            flux[row : row + NODES, :] = velocity[:, cut] * metric_ref[j : j + 1, cut]
            for c in range(3):
                row = ((c * 3 + j) * 2 + half) * NODES
                grads[row : row + NODES, :] = (
                    product[c * NODES : (c + 1) * NODES, cut] * metric_ref[c : c + 1, cut]
                )
    for half in range(2):
        cut = lane_slice(half)
        for direction in range(3):
            gain = jnp.broadcast_to(metric_ref[direction : direction + 1, cut], (8, LANES))
            visc = float(VISCOUS) * gain * gain
            v_even = visc * float(KE)
            v_p = [visc * float(KP[i]) for i in range(2)]
            v_q = [visc * float(KQ[i]) for i in range(2)]
            for line in range(16):
                nodes = line_nodes(direction, line)
                values = []
                for comp in range(COMPS):
                    values.append([work[acc_rows(comp, n, half), :] for n in nodes])
                inner = [None] * 4
                if direction == 2:
                    inner = [inner_gain(plain, scale_ref, n, half) for n in nodes]
                base = (direction * 2 + half) * NODES
                speed = [spread_row(flux, base + n) for n in nodes]
                for comp in range(COMPS):
                    if comp < 3:
                        y = [speed[i] * values[comp][i] for i in range(4)]
                        if comp == direction:
                            y = [y[i] + gain * values[3][i] for i in range(4)]
                        even, odd = transposed_parts(y)
                        s, t, p, q = even_odd(values[comp])
                        even = even + v_even * (s - t)
                        odd = [odd[i] + (v_p[i] * p + v_q[i] * q) for i in range(2)]
                    else:
                        even, odd = transposed_parts(values[direction])
                        even = gain * even
                        odd = [gain * odd[i] for i in range(2)]
                    out = combine(even, odd)
                    for i, n in enumerate(nodes):
                        result = out[i]
                        if direction > 0:
                            result = result + acc_ref[acc_rows(comp, n, half), :]
                        if direction == 2 and comp < 3:
                            for j in range(3):
                                row = ((comp * 3 + j) * 2 + half) * NODES + n
                                result = result + spread_row(grads, row) * values[j][i]
                        if inner[i] is not None:
                            result = result + inner[i] * values[comp][i]
                        acc_ref[acc_rows(comp, n, half), :] = result


def inner_gain(plain, scale_ref, node, half):
    total = None
    for face, _ in touching(node):
        speed = spread_row(plain, ((face // 2) * 2 + half) * NODES + node)
        part = jnp.maximum(-speed if face % 2 else speed, 0.0) + float(PENALTY)
        part = part * jnp.broadcast_to(scale_ref[face : face + 1, lane_slice(half)], (8, LANES))
        total = part if total is None else total + part
    return total


def outer_gain(vel_row, scale_row, face):
    signed = vel_row if face % 2 else -vel_row
    return scale_row * (jnp.maximum(signed, 0.0) + float(PENALTY))


def fill_plain(vel_ref, plain):
    for d in range(3):
        velocity = vel_ref[d].astype(F32)
        for half in range(2):
            row = (d * 2 + half) * NODES
            plain[row : row + NODES, :] = velocity[:, lane_slice(half)]


def touching(node):
    digits = [node // 16, (node // 4) % 4, node % 4]
    found = []
    for d in range(3):
        if digits[d] in (0, 3):
            rest = digits[:d] + digits[d + 1 :]
            found.append((2 * d + digits[d] // 3, 4 * rest[0] + rest[1]))
    return found


def node_gain(plain, scale_ref, face, node, half):
    scale = jnp.broadcast_to(scale_ref[face : face + 1, lane_slice(half)], (8, LANES))
    return outer_gain(spread_row(plain, ((face // 2) * 2 + half) * NODES + node), scale, face)


def final_kernel(
    live_ref, pairs_ref, targets_ref, acc_ref, vel_ref, scale_ref, link_ref, outlet_ref,
    mult_ref, s0_ref, s1_ref, s2_ref, s3_ref, s4_ref, s5_ref, s6_ref,
    out_any,
    out_ref, traces, chosen, square, slots, outer, outlet, plain, sem_out,
):
    columns = slot_columns(link_ref, outlet_ref, square)
    fill_plain(vel_ref, plain)
    slots[0 : LEVELS * CAP, 4 * LANES :] = jnp.zeros((LEVELS * CAP, LANES), F32)
    slots[LEVELS * CAP :, 4 * LANES :] = mult_ref[...]
    slots[LEVELS * CAP :, 0 : 4 * LANES] = jnp.zeros((CAP, 4 * LANES), F32)
    for level, ref in enumerate((s0_ref, s1_ref, s2_ref, s3_ref, s4_ref, s5_ref, s6_ref)):
        for comp in range(COMPS):
            row = comp * CAP
            slots[level * CAP : (level + 1) * CAP, comp * LANES : (comp + 1) * LANES] = ref[
                row : row + CAP, :
            ]
    traces[0:1024, 0:512] = pairs_ref[...]
    traces[1024:1056, 0:512] = jnp.zeros((32, 512), BF16)
    for comp in range(COMPS):
        high, low = split2(jnp.transpose(slots[:, comp * LANES : (comp + 1) * LANES]))
        traces[comp * LANES : (comp + 1) * LANES, 512:] = high
        traces[512 + comp * LANES : 512 + (comp + 1) * LANES, 512:] = low
    high, low = split2(jnp.transpose(slots[:, 4 * LANES :])[0:16])
    traces[1024:1040, 512:] = high
    traces[1040:1056, 512:] = low
    for face in range(6):
        chosen[0:512, :] = one_hot(targets_ref[...], face)
        chosen[512:, :] = one_hot(columns, face)
        both = jnp.dot(traces[...], chosen[...], preferred_element_type=F32)
        outer[face * 512 : (face + 1) * 512, :] = both[:512] + both[512:1024]
        scale = scale_ref[face : face + 1, :] * (2.0 * (face % 2) - 1.0)
        outlet[face * 8 : (face + 1) * 8, :] = (both[1024:1032] + both[1040:1048]) * scale
    live = [live_ref[:, lane_slice(half)] > 0.5 for half in range(2)]
    stores = []
    for high in range(8):
        for half in range(2):
            cut = lane_slice(half)
            block = [[] for _ in range(COMPS)]
            for n in range(high * 8, high * 8 + 8):
                results = [acc_ref[acc_rows(comp, n, half), :] for comp in range(COMPS)]
                for face, m in touching(n):
                    gain = node_gain(plain, scale_ref, face, n, half)
                    for comp in range(COMPS):
                        row = face * 512 + (comp * 16 + m) * OBJ
                        results[comp] = results[comp] - gain * outer[row : row + 8, cut]
                    axis = face // 2
                    results[axis] = (
                        results[axis] + float(FACE_W[m]) * outlet[face * 8 : face * 8 + 8, cut]
                    )
                for comp in range(COMPS):
                    block[comp].append(jnp.where(live[half], results[comp], 0.0))
            for comp in range(COMPS):
                turned_block = jnp.swapaxes(jnp.stack(block[comp]), 0, 1)
                out_ref[comp * OBJ : (comp + 1) * OBJ, high, half * 8 : half * 8 + 8, :] = (
                    turned_block
                )
        store = pltpu.make_async_copy(
            out_ref.at[:, high], out_any.at[:, high], sem_out.at[high]
        )
        store.start()
        stores.append(store)
    for store in stores:
        store.wait()


VMEM = pl.BlockSpec(memory_space=pltpu.VMEM)
ANY = pl.BlockSpec(memory_space=pltpu.MemorySpace.HBM)


def params(mebibytes):
    return pltpu.CompilerParams(vmem_limit_bytes=mebibytes * 2**20)


def cost(microseconds):
    return pl.CostEstimate(
        flops=int(microseconds * 1e3), bytes_accessed=int(microseconds * 3.0e6), transcendentals=0
    )


def f32(*shape):
    return jax.ShapeDtypeStruct(shape, F32)


def local(
    adjoint, velocity, metric, face_scale, resistance, elem_count, face_partner, link_face,
    outlet_face, outlet_id,
):
    x_view = (
        adjoint.reshape(COMPS, OBJ, 8, 8, 2, LANES).transpose(0, 1, 2, 4, 3, 5).reshape(4096, LANES)
    )
    link = link_face.transpose(1, 0, 2)
    deriv = jnp.asarray(np.concatenate(split3(node_matrices())), BF16)
    flow = jnp.asarray(flow_matrix(), BF16)
    devices = lax.axis_size("dom")

    message, live, *sent = pl.pallas_call(
        gather_kernel,
        out_shape=(f32(devices * MSG, LANES), f32(8, ELEMS))
        + (f32(FACE_ROWS, LANES),) * LEVELS,
        in_specs=[ANY] * 9,
        out_specs=(VMEM,) * (2 + LEVELS),
        scratch_shapes=[
            pltpu.VMEM((4096, LANES), F32), pltpu.VMEM((3, NODES, ELEMS), BF16),
            pltpu.VMEM((6, ELEMS), F32), pltpu.VMEM((LEVELS, 1, CAP), jnp.int32),
            pltpu.VMEM((1, CAP), jnp.int32), pltpu.VMEM((1, CAP), jnp.int32),
            pltpu.VMEM((2, OBJ), F32), pltpu.VMEM((48, NODES), BF16),
            pltpu.VMEM((1, 1), jnp.int32), pltpu.VMEM((4096, LANES), F32),
            pltpu.VMEM((1040, 6 * ELEMS), BF16), pltpu.VMEM((6 * ELEMS, 256), BF16),
            pltpu.VMEM((LANES, LANES), F32), pltpu.VMEM((256, 512), F32),
            pltpu.SemaphoreType.DMA((12,)),
        ],
        compiler_params=params(60),
        cost_estimate=cost(5),
        name="gather",
    )(x_view, velocity, face_scale, link, outlet_face, outlet_id, resistance, flow,
      elem_count.reshape(1, 1))

    messages = lax.all_to_all(
        message.reshape(devices, MSG, LANES), "dom", split_axis=0, concat_axis=0, tiled=True
    ).reshape(devices * MSG, LANES)
    def swap(block, mask):
        return lax.ppermute(block, "dom", [(i, i ^ mask) for i in range(devices)])

    received = [swap(block, 1 << level) for level, block in enumerate(sent)]

    acc, multiplier, outlet_terms, pairs, targets = pl.pallas_call(
        volume_kernel,
        out_shape=(
            f32(4096, LANES), f32(OBJ, 8), f32(CAP, LANES),
            jax.ShapeDtypeStruct((1024, 512), BF16), f32(512, LANES),
        ),
        in_specs=[VMEM] * 8,
        out_specs=(VMEM,) * 5,
        scratch_shapes=[
            pltpu.VMEM((4096, LANES), F32), pltpu.VMEM((384, LANES), F32),
            pltpu.VMEM((384, LANES), F32), pltpu.VMEM((1152, LANES), F32),
            pltpu.VMEM((LANES, LANES), F32), pltpu.VMEM((384, LANES), F32),
            pltpu.VMEM((1024, 6 * ELEMS), BF16),
            pltpu.VMEM((6 * ELEMS, 512), BF16),
        ],
        compiler_params=params(20),
        cost_estimate=cost(5),
        name="volume",
    )(x_view, velocity, metric, face_scale, deriv, face_partner, outlet_id, messages)

    out = pl.pallas_call(
        final_kernel,
        out_shape=f32(32, 8, 16, LANES),
        in_specs=[VMEM] * 16,
        out_specs=ANY,
        scratch_shapes=[
            pltpu.VMEM((32, 8, 16, LANES), F32),
            pltpu.VMEM((1056, 768), BF16), pltpu.VMEM((768, ELEMS), BF16),
            pltpu.VMEM((LANES, LANES), F32), pltpu.VMEM((256, 640), F32),
            pltpu.VMEM((6 * 512, ELEMS), F32),
            pltpu.VMEM((48, ELEMS), F32), pltpu.VMEM((384, LANES), F32),
            pltpu.SemaphoreType.DMA((8,)),
        ],
        compiler_params=params(20),
        cost_estimate=cost(9),
        name="finish",
    )(
        live, pairs, targets, acc, velocity, face_scale, link, outlet_face,
        outlet_terms, *received,
    )
    out = (
        out.reshape(COMPS, OBJ, 8, 2, 8, LANES).transpose(0, 1, 2, 4, 3, 5)
        .reshape(COMPS, OBJ, NODES, ELEMS)
    )
    return out, multiplier


def solution(mesh):
    placed = (
        P(None, None, None, "dom"), P(None, None, "dom"), P(None, "dom"), P(None, "dom"),
        P(None, "dom"), P("dom"), P(None, "dom"), P("dom", None, None), P("dom", None),
        P("dom", None),
    )
    return jax.shard_map(
        local, mesh=mesh, in_specs=placed,
        out_specs=(P(None, None, None, "dom"), P(None, "dom")), check_vma=False,
    )
```

```python
import math

import jax
import jax.numpy as jnp
import numpy as np
from jax import lax
from jax.experimental import pallas as pl
from jax.experimental.pallas import tpu as pltpu
from jax.sharding import PartitionSpec as P


F32 = jnp.float32
BF16 = jnp.bfloat16
VISCOUS = 0.05
PENALTY = 1.0
COMPS, OBJ, NODES, ELEMS = 4, 8, 64, 256
LANES = 128
CAP, LEVELS = 32, 7
FACE_ROWS = COMPS * CAP
MSG = 4
HIGHEST = lax.Precision.HIGHEST


def gll_tables():
    root_five = math.sqrt(5.0)
    points = np.array([-1.0, -1.0 / root_five, 1.0 / root_five, 1.0])
    weights = np.array([1.0, 5.0, 5.0, 1.0]) / 6.0
    products = np.array(
        [np.prod([points[i] - points[k] for k in range(4) if k != i]) for i in range(4)]
    )
    derivative = np.zeros((4, 4))
    for i in range(4):
        for j in range(4):
            if i != j:
                derivative[i, j] = products[i] / (products[j] * (points[i] - points[j]))
        derivative[i, i] = -np.sum(derivative[i])
    return (derivative, weights)


DERIV, WEIGHTS = gll_tables()
FACE_W = np.outer(WEIGHTS, WEIGHTS).reshape(16)


def split3(array):
    high = np.asarray(array, np.float32).astype(jnp.bfloat16)
    rest = np.asarray(array, np.float32) - high.astype(np.float32)
    middle = rest.astype(jnp.bfloat16)
    low = (rest - middle.astype(np.float32)).astype(jnp.bfloat16)
    return high, middle, low


def node_matrices():
    identity = np.eye(4)
    return np.concatenate(
        [
            np.kron(DERIV, np.kron(identity, identity)),
            np.kron(identity, np.kron(DERIV, identity)),
            np.kron(identity, np.kron(identity, DERIV)),
        ]
    )


def face_node(face, m):
    axis, layer = face // 2, 3 * (face % 2)
    a, b = m // 4, m % 4
    digits = [a, b]
    digits.insert(axis, layer)
    return 16 * digits[0] + 4 * digits[1] + digits[2]


def flow_matrix():
    table = np.zeros((3, 16, NODES), np.float32)
    for face in range(6):
        row = np.zeros(NODES)
        for m in range(16):
            row[face_node(face, m)] = FACE_W[m] * (2 * (face % 2) - 1)
        for part, values in enumerate(split3(row)):
            table[face // 2, 8 * (face % 2) + part] = values.astype(np.float32)
    return table.reshape(48, NODES)


def lane_slice(half):
    return slice(half * LANES, (half + 1) * LANES)


def slot_columns(link_ref, outlet_ref, square):
    square[...] = jnp.full((LANES, LANES), -1.0, F32)
    for level in range(LEVELS):
        square[level : level + 1, 0:CAP] = link_ref[level].astype(F32)
    square[LEVELS : LEVELS + 1, 0:CAP] = outlet_ref[...].astype(F32)
    turned = jnp.transpose(square[...])
    return jnp.concatenate(
        [
            jnp.broadcast_to(turned[0:CAP, b : b + 1], (CAP, LANES))
            for b in range(LEVELS + 1)
        ],
        axis=0,
    )


def one_hot(columns, face):
    lane = lax.broadcasted_iota(jnp.int32, columns.shape, 1).astype(F32)
    parts = [
        jnp.where(columns == lane + float(face * ELEMS + half * LANES), 1.0, 0.0)
        for half in range(2)
    ]
    return jnp.concatenate(parts, axis=1).astype(BF16)


def split2(value):
    high = value.astype(BF16)
    return high, (value - high.astype(F32)).astype(BF16)


def node_major(x_ref, work_ref, comp):
    for high in range(8):
        for half in range(2):
            block = jnp.stack(
                [
                    x_ref[pl.ds(((comp * OBJ + o) * 8 + high) * 16 + half * 8, 8), :]
                    for o in range(OBJ)
                ]
            )
            start = acc_rows(comp, high * 8, half).start
            work_ref[pl.ds(start, 64), :] = jnp.swapaxes(block, 0, 1).reshape(64, LANES)


def comp_traces(work_ref, comp):
    for face in range(6):
        for m in range(0, 16, 2):
            row = (comp * 16 + m) * OBJ
            for half in range(2):
                pair = jnp.concatenate(
                    [work_ref[acc_rows(comp, face_node(face, m + i), half), :] for i in range(2)],
                    axis=0,
                )
                yield face, row, half, split2(pair)


def fill_traces(work_ref, traces, comp):
    for face, row, half, (high, low) in comp_traces(work_ref, comp):
        cols = slice(face * ELEMS + half * LANES, face * ELEMS + (half + 1) * LANES)
        traces[row : row + 16, cols] = high
        traces[512 + row : 528 + row, cols] = low


def fill_pick(pick, row):
    sub = lax.broadcasted_iota(jnp.int32, (ELEMS, row.shape[1]), 0).astype(F32)
    for face in range(6):
        pick[face * ELEMS : (face + 1) * ELEMS, :] = jnp.where(
            sub == row - float(face * ELEMS), 1.0, 0.0
        ).astype(BF16)


def parts3(value):
    high = value.astype(BF16).astype(F32)
    rest = value - high
    middle = rest.astype(BF16).astype(F32)
    return high, middle, rest - middle


def gather_kernel(
    x_any, vel_any, scale_any, link_any, outlet_any, ids_any, res_any, flow_any, count_any,
    message_ref, live_ref,
    s0_ref, s1_ref, s2_ref, s3_ref, s4_ref, s5_ref, s6_ref,
    x_ref, vel_ref, scale_ref, link_ref, outlet_ref, ids_ref, res_ref, flow_ref, count_ref,
    work_ref, traces, pick, square, total, sems,
):
    small = (
        (link_any, link_ref), (outlet_any, outlet_ref), (vel_any, vel_ref),
        (scale_any, scale_ref), (flow_any, flow_ref), (ids_any, ids_ref), (res_any, res_ref),
        (count_any, count_ref),
    )
    copies = [
        pltpu.make_async_copy(src, dst, sems.at[4 + i]) for i, (src, dst) in enumerate(small)
    ]
    blocks = [
        pltpu.make_async_copy(
            x_any.at[pl.ds(c * 1024, 1024), :], x_ref.at[pl.ds(c * 1024, 1024), :], sems.at[c]
        )
        for c in range(COMPS)
    ]
    for copy in blocks + copies:
        copy.start()
    for copy in copies:
        copy.wait()
    element = lax.broadcasted_iota(jnp.int32, (8, ELEMS), 1)
    live_ref[...] = jnp.where(element < count_ref[...], 1.0, 0.0)
    square[0:8, :] = jnp.zeros((8, LANES), F32)
    for level in range(LEVELS):
        square[level : level + 1, 0:CAP] = link_ref[level].astype(F32)
    square[LEVELS : LEVELS + 1, 0:CAP] = outlet_ref[...].astype(F32)
    head = square[0:8, :]
    pieces = [
        (pltpu.roll(head, CAP * (b % 4), 1) if b % 4 else head)[b : b + 1] for b in range(8)
    ]
    row = jnp.concatenate([sum(pieces[1:4], pieces[0]), sum(pieces[5:], pieces[4])], axis=1)
    fill_pick(pick, row)
    kind = lax.broadcasted_iota(jnp.int32, (16, ELEMS), 0)
    for face in range(6):
        axis, sign = face // 2, 2.0 * (face % 2) - 1.0
        if face % 2 == 0:
            flows = jnp.dot(
                flow_ref[16 * axis : 16 * axis + 16, :], vel_ref[axis],
                preferred_element_type=F32,
            )
        scale = scale_ref[face : face + 1, :]
        first = 8 * (face % 2)
        flow = (flows[first : first + 1] + flows[first + 1 : first + 2]) + flows[
            first + 2 : first + 3
        ]
        table = jnp.where(kind == 6, float(axis), 0.0)
        for i, part in enumerate(parts3(scale * sign) + parts3(flow * scale)):
            table = jnp.where(kind == i, part, table)
        traces[1024:1040, face * ELEMS : (face + 1) * ELEMS] = table.astype(BF16)
    for comp in range(COMPS):
        blocks[comp].wait()
        node_major(x_ref, work_ref, comp)
        fill_traces(work_ref, traces, comp)
    both = jnp.dot(traces[...], pick[...], preferred_element_type=F32)
    chosen = both[:512] + both[512:1024]
    for comp in range(COMPS):
        for half in range(2):
            total[lane_slice(half), lane_slice(comp)] = jnp.transpose(
                chosen[lane_slice(comp), lane_slice(half)]
            )
    stats = both[1024:1040, LANES:]
    square[...] = jnp.zeros((LANES, LANES), F32)
    square[0:1, :] = (stats[0:1] + stats[1:2]) + stats[2:3]
    square[1:2, :] = (stats[3:4] + stats[4:5]) + stats[5:6]
    square[2:3, :] = stats[6:7]
    stats = jnp.transpose(square[...])[LANES - CAP :]
    homes = (s0_ref, s1_ref, s2_ref, s3_ref, s4_ref, s5_ref, s6_ref)
    for level, ref in enumerate(homes):
        for comp in range(COMPS):
            ref[comp * CAP : (comp + 1) * CAP, :] = total[
                level * CAP : (level + 1) * CAP, comp * LANES : (comp + 1) * LANES
            ]
    lane = lax.broadcasted_iota(jnp.int32, (CAP, LANES), 1)
    axis = jnp.broadcast_to(stats[:, 2:3], (CAP, LANES))
    moment = jnp.zeros((CAP, LANES), F32)
    for comp in range(3):
        moment += jnp.where(
            axis == float(comp), total[LEVELS * CAP :, comp * LANES : (comp + 1) * LANES], 0.0
        )
    node = lane[0:1] // OBJ
    weight = jnp.zeros((1, LANES), F32)
    for m in range(16):
        weight = jnp.where(node == m, float(FACE_W[m]), weight)
    moment = moment * weight
    for shift in (8, 16, 32, 64):
        moment = moment + pltpu.roll(moment, shift, 1)
    moment = moment * jnp.broadcast_to(stats[:, 0:1], (CAP, LANES))
    moment = jnp.where(
        lane < OBJ, moment,
        jnp.where(lane == OBJ, jnp.broadcast_to(stats[:, 1:2], (CAP, LANES)), 0.0),
    )
    spread = lax.broadcasted_iota(jnp.int32, (LANES, 4 * LANES), 0)
    group = lax.broadcasted_iota(jnp.int32, (LANES, 4 * LANES), 1) // CAP
    wide = jnp.dot(
        moment, jnp.where(spread == group, 1.0, 0.0), precision=HIGHEST,
        preferred_element_type=F32,
    )
    slot = lax.broadcasted_iota(jnp.int32, (CAP, 4 * LANES), 0)
    within = lax.broadcasted_iota(jnp.int32, (CAP, 4 * LANES), 1) % CAP
    flat = jnp.sum(jnp.where(slot == within, wide, 0.0), axis=0, keepdims=True)
    square[0:8, :] = jnp.zeros((8, LANES), F32)
    square[0:1, 0:CAP] = ids_ref[...].astype(F32)
    square[1:3, 0:OBJ] = res_ref[...]
    head = square[0:8, :]
    extra = (
        pltpu.roll(head, 32, 1)[0:1] + pltpu.roll(head, 64, 1)[1:2] + pltpu.roll(head, 72, 1)[2:3]
    )
    message = jnp.concatenate(
        [
            flat[:, 0:LANES],
            flat[:, LANES : 2 * LANES],
            flat[:, 2 * LANES : 3 * LANES] + extra,
            jnp.zeros((1, LANES), F32),
        ],
        axis=0,
    )
    double = jnp.concatenate([message, message], axis=0)
    for peer in range(32):
        message_ref[peer * 8 : (peer + 1) * 8, :] = double


def line_nodes(direction, line):
    p, q = line // 4, line % 4
    if direction == 0:
        return [16 * i + 4 * p + q for i in range(4)]
    if direction == 1:
        return [16 * p + 4 * i + q for i in range(4)]
    return [16 * p + 4 * q + i for i in range(4)]


def even_odd(v):
    return v[0] + v[3], v[1] + v[2], v[0] - v[3], v[1] - v[2]


STIFF = DERIV.T @ DERIV
EP, EQ = [0.5 * (DERIV[r, 0] - DERIV[3 - r, 0]) for r in range(2)]
OS = [0.5 * (DERIV[0, i] + DERIV[3, i]) for i in range(2)]
OT = [0.5 * (DERIV[1, i] + DERIV[2, i]) for i in range(2)]
KE = 0.5 * (STIFF[0, 0] + STIFF[0, 3])
KP = [0.5 * (STIFF[i, 0] - STIFF[i, 3]) for i in range(2)]
KQ = [0.5 * (STIFF[i, 1] - STIFF[i, 2]) for i in range(2)]


def transposed_parts(y):
    s, t, p, q = even_odd(y)
    even = float(EP) * p + float(EQ) * q
    odd = [float(OS[i]) * s + float(OT[i]) * t for i in range(2)]
    return even, odd


def combine(even, odd):
    return [odd[0] + even, odd[1] - even, -even - odd[1], even - odd[0]]


def acc_rows(comp, node, half):
    return pl.ds(((half * COMPS + comp) * NODES + node) * 8, 8)


def spread_row(ref, row):
    return ref[pl.ds(row, 8, stride=0), :]


def resolve_outlets(ids_ref, near_ref, far_ref, square, gathered, mult_ref, outlet_ref):
    rank = lax.axis_index("dom").astype(jnp.int32)
    for q in range(3):
        rows = jnp.concatenate(
            [ref[pl.ds(q, LANES // 2, stride=MSG), :] for ref in (near_ref, far_ref)], axis=0
        )
        gathered[q * LANES : (q + 1) * LANES, :] = jnp.transpose(rows)
    square[...] = jnp.zeros((LANES, LANES), F32)
    square[0:1, 0:CAP] = ids_ref[...].astype(F32)
    own_ids = jnp.transpose(square[...])[0:CAP, 0:1]
    sub = lax.broadcasted_iota(jnp.int32, (8, LANES), 0)
    wanted = jnp.concatenate(
        [(rank * 8 + sub).astype(F32), jnp.broadcast_to(own_ids, (CAP, LANES))], axis=0
    )

    def step(t, sums):
        hit = [
            wanted[g * 8 : g * 8 + 8] == spread_row(gathered, 2 * LANES + CAP + t)
            for g in range(5)
        ]
        new = []
        for r in range(9):
            row = spread_row(gathered, r * CAP + t)
            for g in range(5):
                new.append(sums[r * 5 + g] + jnp.where(hit[g], row, 0.0))
        return tuple(new)

    sums = lax.fori_loop(
        0, CAP, step, tuple(jnp.zeros((8, LANES), F32) for _ in range(45))
    )
    chip = lax.broadcasted_iota(jnp.int32, (8, LANES), 1)
    core = rank % 2
    device = jnp.where(
        chip < LANES // 2, 2 * chip + core, 2 * chip - LANES + 1 - core
    ).astype(F32)
    for g in range(5):
        linear = jnp.zeros((8, LANES), F32)
        quadratic = jnp.zeros((8, LANES), F32)
        for q in range(8):
            hit = wanted[g * 8 : g * 8 + 8] == device * 8.0 + float(q)
            linear += jnp.where(hit, spread_row(gathered, 2 * LANES + 64 + q), 0.0)
            quadratic += jnp.where(hit, spread_row(gathered, 2 * LANES + 72 + q), 0.0)
        flow = jnp.sum(sums[8 * 5 + g], axis=1, keepdims=True)
        factor = jnp.sum(linear, axis=1, keepdims=True) + 2.0 * jnp.sum(
            quadratic, axis=1, keepdims=True
        ) * jnp.abs(flow)
        lane = lax.broadcasted_iota(jnp.int32, (8, LANES), 1)
        table = jnp.zeros((8, LANES), F32)
        for o in range(OBJ):
            adj = jnp.sum(sums[o * 5 + g], axis=1, keepdims=True)
            table = jnp.where(lane == o, factor * adj, table)
        if g == 0:
            square[...] = jnp.zeros((LANES, LANES), F32)
            square[0:8, :] = table
            mult_ref[...] = jnp.transpose(square[...])[0:8, 0:8]
        else:
            outlet_ref[(g - 1) * 8 : g * 8, :] = table


def gather_pairs(work, partner_ref, pairs_ref, targets_ref, traces, pick):
    partner = partner_ref[...].astype(F32)
    ids = (
        lax.broadcasted_iota(jnp.int32, (6, ELEMS), 1)
        + lax.broadcasted_iota(jnp.int32, (6, ELEMS), 0) * ELEMS
    ).astype(F32)
    first = partner > ids
    flags = jnp.where(first, 1.0, 0.0)
    before = jnp.where(
        lax.broadcasted_iota(jnp.int32, (ELEMS, ELEMS), 0)
        < lax.broadcasted_iota(jnp.int32, (ELEMS, ELEMS), 1),
        1.0, 0.0,
    ).astype(BF16)
    padded = jnp.concatenate([flags, jnp.zeros((10, ELEMS), F32)], axis=0).astype(BF16)
    inside = jnp.dot(padded, before, preferred_element_type=F32)
    number = lax.broadcasted_iota(jnp.int32, (256, LANES), 0).astype(F32)
    offset = jnp.zeros((1, 1), F32)
    ranks = []
    for face in range(6):
        ranks.append(
            jnp.where(first[face : face + 1], inside[face : face + 1] + offset, -1.0)
        )
        offset = offset + jnp.sum(flags[face : face + 1], axis=1, keepdims=True)
    for which, table in enumerate((ids, partner)):
        found = jnp.zeros((256, LANES), F32)
        for face in range(6):
            for half in range(2):
                cut = lane_slice(half)
                found += jnp.where(
                    number == ranks[face][:, cut], table[face : face + 1, cut], 0.0
                )
        column = jnp.sum(found, axis=1, keepdims=True)
        targets_ref[256 * (1 - which) : 256 * (2 - which), :] = jnp.broadcast_to(
            column, (256, LANES)
        )
    row = jnp.concatenate(
        [
            jnp.transpose(targets_ref[start : start + LANES, :])[0:1]
            for start in (256, 384, 0, 128)
        ],
        axis=1,
    )
    fill_pick(pick, row)
    for comp in range(COMPS):
        fill_traces(work, traces, comp)
    pairs_ref[...] = jnp.dot(
        traces[...], pick[...], preferred_element_type=F32
    ).astype(BF16)


def volume_kernel(
    x_ref, vel_ref, metric_ref, scale_ref, deriv_ref, partner_ref,
    acc_ref, pairs_ref, targets_ref,
    work, flux, plain, grads, traces, pick,
):
    for comp in range(COMPS):
        node_major(x_ref, work, comp)
    gather_pairs(work, partner_ref, pairs_ref, targets_ref, traces, pick)
    for j in range(3):
        product = jnp.dot(deriv_ref[...], vel_ref[j], preferred_element_type=F32)
        product = (product[0:192] + product[192:384]) + product[384:576]
        velocity = vel_ref[j].astype(F32)
        for half in range(2):
            cut = lane_slice(half)
            row = (j * 2 + half) * NODES
            plain[row : row + NODES, :] = velocity[:, cut]
            flux[row : row + NODES, :] = velocity[:, cut] * metric_ref[j : j + 1, cut]
            for c in range(3):
                row = ((c * 3 + j) * 2 + half) * NODES
                grads[row : row + NODES, :] = (
                    product[c * NODES : (c + 1) * NODES, cut] * metric_ref[c : c + 1, cut]
                )
    for half in range(2):
        cut = lane_slice(half)
        for direction in range(3):
            gain = jnp.broadcast_to(metric_ref[direction : direction + 1, cut], (8, LANES))
            visc = float(VISCOUS) * gain * gain
            v_even = visc * float(KE)
            v_p = [visc * float(KP[i]) for i in range(2)]
            v_q = [visc * float(KQ[i]) for i in range(2)]
            for line in range(16):
                nodes = line_nodes(direction, line)
                values = []
                for comp in range(COMPS):
                    values.append([work[acc_rows(comp, n, half), :] for n in nodes])
                inner = [None] * 4
                if direction == 2:
                    inner = [inner_gain(plain, scale_ref, n, half) for n in nodes]
                base = (direction * 2 + half) * NODES
                speed = [spread_row(flux, base + n) for n in nodes]
                for comp in range(COMPS):
                    if comp < 3:
                        y = [speed[i] * values[comp][i] for i in range(4)]
                        if comp == direction:
                            y = [y[i] + gain * values[3][i] for i in range(4)]
                        even, odd = transposed_parts(y)
                        s, t, p, q = even_odd(values[comp])
                        even = even + v_even * (s - t)
                        odd = [odd[i] + (v_p[i] * p + v_q[i] * q) for i in range(2)]
                    else:
                        even, odd = transposed_parts(values[direction])
                        even = gain * even
                        odd = [gain * odd[i] for i in range(2)]
                    out = combine(even, odd)
                    for i, n in enumerate(nodes):
                        result = out[i]
                        if direction > 0:
                            result = result + acc_ref[acc_rows(comp, n, half), :]
                        if direction == 2 and comp < 3:
                            for j in range(3):
                                row = ((comp * 3 + j) * 2 + half) * NODES + n
                                result = result + spread_row(grads, row) * values[j][i]
                        if inner[i] is not None:
                            result = result + inner[i] * values[comp][i]
                        acc_ref[acc_rows(comp, n, half), :] = result


def inner_gain(plain, scale_ref, node, half):
    total = None
    for face, _ in touching(node):
        speed = spread_row(plain, ((face // 2) * 2 + half) * NODES + node)
        part = jnp.maximum(-speed if face % 2 else speed, 0.0) + float(PENALTY)
        part = part * jnp.broadcast_to(scale_ref[face : face + 1, lane_slice(half)], (8, LANES))
        total = part if total is None else total + part
    return total


def outer_gain(vel_row, scale_row, face):
    signed = vel_row if face % 2 else -vel_row
    return scale_row * (jnp.maximum(signed, 0.0) + float(PENALTY))


def fill_plain(vel_ref, plain):
    for d in range(3):
        velocity = vel_ref[d].astype(F32)
        for half in range(2):
            row = (d * 2 + half) * NODES
            plain[row : row + NODES, :] = velocity[:, lane_slice(half)]


def touching(node):
    digits = [node // 16, (node // 4) % 4, node % 4]
    found = []
    for d in range(3):
        if digits[d] in (0, 3):
            rest = digits[:d] + digits[d + 1 :]
            found.append((2 * d + digits[d] // 3, 4 * rest[0] + rest[1]))
    return found


def node_gain(plain, scale_ref, face, node, half):
    scale = jnp.broadcast_to(scale_ref[face : face + 1, lane_slice(half)], (8, LANES))
    return outer_gain(spread_row(plain, ((face // 2) * 2 + half) * NODES + node), scale, face)


def final_kernel(
    live_ref, pairs_ref, targets_ref, acc_ref, vel_ref, scale_ref, link_ref, outlet_ref,
    ids_ref, near_ref, far_ref, s0_ref, s1_ref, s2_ref, s3_ref, s4_ref, s5_ref, s6_ref,
    out_any, mult_ref,
    out_ref, traces, chosen, square, slots, outer, outlet, plain, gathered, terms, sem_out,
):
    resolve_outlets(ids_ref, near_ref, far_ref, square, gathered, mult_ref, terms)
    columns = slot_columns(link_ref, outlet_ref, square)
    fill_plain(vel_ref, plain)
    slots[0 : LEVELS * CAP, 4 * LANES :] = jnp.zeros((LEVELS * CAP, LANES), F32)
    slots[LEVELS * CAP :, 4 * LANES :] = terms[...]
    slots[LEVELS * CAP :, 0 : 4 * LANES] = jnp.zeros((CAP, 4 * LANES), F32)
    for level, ref in enumerate((s0_ref, s1_ref, s2_ref, s3_ref, s4_ref, s5_ref, s6_ref)):
        for comp in range(COMPS):
            row = comp * CAP
            slots[level * CAP : (level + 1) * CAP, comp * LANES : (comp + 1) * LANES] = ref[
                row : row + CAP, :
            ]
    traces[0:1024, 0:512] = pairs_ref[...]
    traces[1024:1056, 0:512] = jnp.zeros((32, 512), BF16)
    for comp in range(COMPS):
        high, low = split2(jnp.transpose(slots[:, comp * LANES : (comp + 1) * LANES]))
        traces[comp * LANES : (comp + 1) * LANES, 512:] = high
        traces[512 + comp * LANES : 512 + (comp + 1) * LANES, 512:] = low
    high, low = split2(jnp.transpose(slots[:, 4 * LANES :])[0:16])
    traces[1024:1040, 512:] = high
    traces[1040:1056, 512:] = low
    for face in range(6):
        chosen[0:512, :] = one_hot(targets_ref[...], face)
        chosen[512:, :] = one_hot(columns, face)
        both = jnp.dot(traces[...], chosen[...], preferred_element_type=F32)
        outer[face * 512 : (face + 1) * 512, :] = both[:512] + both[512:1024]
        scale = scale_ref[face : face + 1, :] * (2.0 * (face % 2) - 1.0)
        outlet[face * 8 : (face + 1) * 8, :] = (both[1024:1032] + both[1040:1048]) * scale
    live = [live_ref[:, lane_slice(half)] > 0.5 for half in range(2)]
    stores = []
    for high in range(8):
        for half in range(2):
            cut = lane_slice(half)
            block = [[] for _ in range(COMPS)]
            for n in range(high * 8, high * 8 + 8):
                results = [acc_ref[acc_rows(comp, n, half), :] for comp in range(COMPS)]
                for face, m in touching(n):
                    gain = node_gain(plain, scale_ref, face, n, half)
                    for comp in range(COMPS):
                        row = face * 512 + (comp * 16 + m) * OBJ
                        results[comp] = results[comp] - gain * outer[row : row + 8, cut]
                    axis = face // 2
                    results[axis] = (
                        results[axis] + float(FACE_W[m]) * outlet[face * 8 : face * 8 + 8, cut]
                    )
                for comp in range(COMPS):
                    block[comp].append(jnp.where(live[half], results[comp], 0.0))
            for comp in range(COMPS):
                turned_block = jnp.swapaxes(jnp.stack(block[comp]), 0, 1)
                out_ref[comp * OBJ : (comp + 1) * OBJ, high, half * 8 : half * 8 + 8, :] = (
                    turned_block
                )
        store = pltpu.make_async_copy(
            out_ref.at[:, high], out_any.at[:, high], sem_out.at[high]
        )
        store.start()
        stores.append(store)
    for store in stores:
        store.wait()


VMEM = pl.BlockSpec(memory_space=pltpu.VMEM)
ANY = pl.BlockSpec(memory_space=pltpu.MemorySpace.HBM)


def params(mebibytes):
    return pltpu.CompilerParams(vmem_limit_bytes=mebibytes * 2**20)


def cost(microseconds):
    return pl.CostEstimate(
        flops=int(microseconds * 1e3), bytes_accessed=int(microseconds * 3.0e6), transcendentals=0
    )


def f32(*shape):
    return jax.ShapeDtypeStruct(shape, F32)


def local(
    adjoint, velocity, metric, face_scale, resistance, elem_count, face_partner, link_face,
    outlet_face, outlet_id,
):
    x_view = (
        adjoint.reshape(COMPS, OBJ, 8, 8, 2, LANES).transpose(0, 1, 2, 4, 3, 5).reshape(4096, LANES)
    )
    link = link_face.transpose(1, 0, 2)
    deriv = jnp.asarray(np.concatenate(split3(node_matrices())), BF16)
    flow = jnp.asarray(flow_matrix(), BF16)
    devices = lax.axis_size("dom")
    chips = devices // 2

    message, live, *sent = pl.pallas_call(
        gather_kernel,
        out_shape=(f32(chips * MSG, LANES), f32(8, ELEMS))
        + (f32(FACE_ROWS, LANES),) * LEVELS,
        in_specs=[ANY] * 9,
        out_specs=(VMEM,) * (2 + LEVELS),
        scratch_shapes=[
            pltpu.VMEM((4096, LANES), F32), pltpu.VMEM((3, NODES, ELEMS), BF16),
            pltpu.VMEM((6, ELEMS), F32), pltpu.VMEM((LEVELS, 1, CAP), jnp.int32),
            pltpu.VMEM((1, CAP), jnp.int32), pltpu.VMEM((1, CAP), jnp.int32),
            pltpu.VMEM((2, OBJ), F32), pltpu.VMEM((48, NODES), BF16),
            pltpu.VMEM((1, 1), jnp.int32), pltpu.VMEM((4096, LANES), F32),
            pltpu.VMEM((1040, 6 * ELEMS), BF16), pltpu.VMEM((6 * ELEMS, 256), BF16),
            pltpu.VMEM((LANES, LANES), F32), pltpu.VMEM((256, 512), F32),
            pltpu.SemaphoreType.DMA((12,)),
        ],
        compiler_params=params(60),
        cost_estimate=cost(5),
        name="gather",
    )(x_view, velocity, face_scale, link, outlet_face, outlet_id, resistance, flow,
      elem_count.reshape(1, 1))

    same_core = [[2 * chip + core for chip in range(chips)] for core in range(2)]
    near = lax.all_to_all(
        message.reshape(chips, MSG, LANES), "dom", split_axis=0, concat_axis=0,
        axis_index_groups=same_core, tiled=True,
    ).reshape(chips * MSG, LANES)

    def swap(block, mask):
        return lax.ppermute(block, "dom", [(i, i ^ mask) for i in range(devices)])

    received = []
    for level, block in enumerate(sent):
        received.append(swap(block, 1 << level))
    vel_late, near = lax.optimization_barrier((velocity, near))
    far = swap(near, 1)

    acc, pairs, targets = pl.pallas_call(
        volume_kernel,
        out_shape=(
            f32(4096, LANES), jax.ShapeDtypeStruct((1024, 512), BF16), f32(512, LANES),
        ),
        in_specs=[VMEM] * 6,
        out_specs=(VMEM,) * 3,
        scratch_shapes=[
            pltpu.VMEM((4096, LANES), F32), pltpu.VMEM((384, LANES), F32),
            pltpu.VMEM((384, LANES), F32), pltpu.VMEM((1152, LANES), F32),
            pltpu.VMEM((1024, 6 * ELEMS), BF16), pltpu.VMEM((6 * ELEMS, 512), BF16),
        ],
        compiler_params=params(20),
        cost_estimate=cost(5),
        name="volume",
    )(x_view, vel_late, metric, face_scale, deriv, face_partner)

    out, multiplier = pl.pallas_call(
        final_kernel,
        out_shape=(f32(32, 8, 16, LANES), f32(OBJ, 8)),
        in_specs=[VMEM] * 18,
        out_specs=(ANY, VMEM),
        scratch_shapes=[
            pltpu.VMEM((32, 8, 16, LANES), F32),
            pltpu.VMEM((1056, 768), BF16), pltpu.VMEM((768, ELEMS), BF16),
            pltpu.VMEM((LANES, LANES), F32), pltpu.VMEM((256, 640), F32),
            pltpu.VMEM((6 * 512, ELEMS), F32),
            pltpu.VMEM((48, ELEMS), F32), pltpu.VMEM((384, LANES), F32),
            pltpu.VMEM((384, LANES), F32), pltpu.VMEM((CAP, LANES), F32),
            pltpu.SemaphoreType.DMA((8,)),
        ],
        compiler_params=params(20),
        cost_estimate=cost(9),
        name="finish",
    )(
        live, pairs, targets, acc, velocity, face_scale, link, outlet_face,
        outlet_id, near, far, *received,
    )
    out = (
        out.reshape(COMPS, OBJ, 8, 2, 8, LANES).transpose(0, 1, 2, 4, 3, 5)
        .reshape(COMPS, OBJ, NODES, ELEMS)
    )
    return out, multiplier


def solution(mesh):
    placed = (
        P(None, None, None, "dom"), P(None, None, "dom"), P(None, "dom"), P(None, "dom"),
        P(None, "dom"), P("dom"), P(None, "dom"), P("dom", None, None), P("dom", None),
        P("dom", None),
    )
    return jax.shard_map(
        local, mesh=mesh, in_specs=placed,
        out_specs=(P(None, None, None, "dom"), P(None, "dom")), check_vma=False,
    )
```

```python
import math

import jax
import jax.numpy as jnp
import numpy as np
from jax import lax
from jax.experimental import pallas as pl
from jax.experimental.pallas import tpu as pltpu
from jax.sharding import PartitionSpec as P


F32 = jnp.float32
BF16 = jnp.bfloat16
VISCOUS = 0.05
PENALTY = 1.0
COMPS, OBJ, NODES, ELEMS = 4, 8, 64, 256
LANES = 128
CAP, LEVELS = 32, 7
FACE_ROWS = COMPS * CAP
MSG = 4
HIGHEST = lax.Precision.HIGHEST


def gll_tables():
    root_five = math.sqrt(5.0)
    points = np.array([-1.0, -1.0 / root_five, 1.0 / root_five, 1.0])
    weights = np.array([1.0, 5.0, 5.0, 1.0]) / 6.0
    products = np.array(
        [np.prod([points[i] - points[k] for k in range(4) if k != i]) for i in range(4)]
    )
    derivative = np.zeros((4, 4))
    for i in range(4):
        for j in range(4):
            if i != j:
                derivative[i, j] = products[i] / (products[j] * (points[i] - points[j]))
        derivative[i, i] = -np.sum(derivative[i])
    return (derivative, weights)


DERIV, WEIGHTS = gll_tables()
FACE_W = np.outer(WEIGHTS, WEIGHTS).reshape(16)


def split3(array):
    high = np.asarray(array, np.float32).astype(jnp.bfloat16)
    rest = np.asarray(array, np.float32) - high.astype(np.float32)
    middle = rest.astype(jnp.bfloat16)
    low = (rest - middle.astype(np.float32)).astype(jnp.bfloat16)
    return high, middle, low


def node_matrices():
    identity = np.eye(4)
    return np.concatenate(
        [
            np.kron(DERIV, np.kron(identity, identity)),
            np.kron(identity, np.kron(DERIV, identity)),
            np.kron(identity, np.kron(identity, DERIV)),
        ]
    )


def face_node(face, m):
    axis, layer = face // 2, 3 * (face % 2)
    a, b = m // 4, m % 4
    digits = [a, b]
    digits.insert(axis, layer)
    return 16 * digits[0] + 4 * digits[1] + digits[2]


def flow_matrix():
    table = np.zeros((3, 16, NODES), np.float32)
    for face in range(6):
        row = np.zeros(NODES)
        for m in range(16):
            row[face_node(face, m)] = FACE_W[m] * (2 * (face % 2) - 1)
        for part, values in enumerate(split3(row)):
            table[face // 2, 8 * (face % 2) + part] = values.astype(np.float32)
    return table.reshape(48, NODES)


def lane_slice(half):
    return slice(half * LANES, (half + 1) * LANES)


def slot_columns(link_ref, outlet_ref, square):
    square[...] = jnp.full((LANES, LANES), -1.0, F32)
    for level in range(LEVELS):
        square[level : level + 1, 0:CAP] = link_ref[level].astype(F32)
    square[LEVELS : LEVELS + 1, 0:CAP] = outlet_ref[...].astype(F32)
    turned = jnp.transpose(square[...])
    return jnp.concatenate(
        [
            jnp.broadcast_to(turned[0:CAP, b : b + 1], (CAP, LANES))
            for b in range(LEVELS + 1)
        ],
        axis=0,
    )


def one_hot(columns, face):
    lane = lax.broadcasted_iota(jnp.int32, columns.shape, 1).astype(F32)
    parts = [
        jnp.where(columns == lane + float(face * ELEMS + half * LANES), 1.0, 0.0)
        for half in range(2)
    ]
    return jnp.concatenate(parts, axis=1).astype(BF16)


def split2(value):
    high = value.astype(BF16)
    return high, (value - high.astype(F32)).astype(BF16)


def node_major(x_ref, work_ref, comp):
    for high in range(8):
        for half in range(2):
            block = jnp.stack(
                [
                    x_ref[pl.ds(((comp * OBJ + o) * 8 + high) * 16 + half * 8, 8), :]
                    for o in range(OBJ)
                ]
            )
            start = acc_rows(comp, high * 8, half).start
            work_ref[pl.ds(start, 64), :] = jnp.swapaxes(block, 0, 1).reshape(64, LANES)


def comp_traces(work_ref, comp):
    for face in range(6):
        for m in range(0, 16, 2):
            row = (comp * 16 + m) * OBJ
            for half in range(2):
                pair = jnp.concatenate(
                    [work_ref[acc_rows(comp, face_node(face, m + i), half), :] for i in range(2)],
                    axis=0,
                )
                yield face, row, half, split2(pair)


def fill_traces(work_ref, traces, comp):
    for face, row, half, (high, low) in comp_traces(work_ref, comp):
        cols = slice(face * ELEMS + half * LANES, face * ELEMS + (half + 1) * LANES)
        traces[row : row + 16, cols] = high
        traces[512 + row : 528 + row, cols] = low


def fill_pick(pick, row):
    sub = lax.broadcasted_iota(jnp.int32, (ELEMS, row.shape[1]), 0).astype(F32)
    for face in range(6):
        pick[face * ELEMS : (face + 1) * ELEMS, :] = jnp.where(
            sub == row - float(face * ELEMS), 1.0, 0.0
        ).astype(BF16)


def parts3(value):
    high = value.astype(BF16).astype(F32)
    rest = value - high
    middle = rest.astype(BF16).astype(F32)
    return high, middle, rest - middle


def gather_kernel(
    x_any, vel_any, scale_any, link_any, outlet_any, ids_any, res_any, flow_any, count_any,
    message_ref, live_ref,
    s0_ref, s1_ref, s2_ref, s3_ref, s4_ref, s5_ref, s6_ref,
    x_ref, vel_ref, scale_ref, link_ref, outlet_ref, ids_ref, res_ref, flow_ref, count_ref,
    work_ref, traces, pick, square, total, sems,
):
    small = (
        (link_any, link_ref), (outlet_any, outlet_ref), (vel_any, vel_ref),
        (scale_any, scale_ref), (flow_any, flow_ref), (ids_any, ids_ref), (res_any, res_ref),
        (count_any, count_ref),
    )
    copies = [
        pltpu.make_async_copy(src, dst, sems.at[4 + i]) for i, (src, dst) in enumerate(small)
    ]
    blocks = [
        pltpu.make_async_copy(
            x_any.at[pl.ds(c * 1024, 1024), :], x_ref.at[pl.ds(c * 1024, 1024), :], sems.at[c]
        )
        for c in range(COMPS)
    ]
    for copy in blocks + copies:
        copy.start()
    for copy in copies:
        copy.wait()
    element = lax.broadcasted_iota(jnp.int32, (8, ELEMS), 1)
    live_ref[...] = jnp.where(element < count_ref[...], 1.0, 0.0)
    square[0:8, :] = jnp.zeros((8, LANES), F32)
    for level in range(LEVELS):
        square[level : level + 1, 0:CAP] = link_ref[level].astype(F32)
    square[LEVELS : LEVELS + 1, 0:CAP] = outlet_ref[...].astype(F32)
    head = square[0:8, :]
    pieces = [
        (pltpu.roll(head, CAP * (b % 4), 1) if b % 4 else head)[b : b + 1] for b in range(8)
    ]
    row = jnp.concatenate([sum(pieces[1:4], pieces[0]), sum(pieces[5:], pieces[4])], axis=1)
    fill_pick(pick, row)
    kind = lax.broadcasted_iota(jnp.int32, (16, ELEMS), 0)
    for face in range(6):
        axis, sign = face // 2, 2.0 * (face % 2) - 1.0
        if face % 2 == 0:
            flows = jnp.dot(
                flow_ref[16 * axis : 16 * axis + 16, :], vel_ref[axis],
                preferred_element_type=F32,
            )
        scale = scale_ref[face : face + 1, :]
        first = 8 * (face % 2)
        flow = (flows[first : first + 1] + flows[first + 1 : first + 2]) + flows[
            first + 2 : first + 3
        ]
        table = jnp.where(kind == 6, float(axis), 0.0)
        for i, part in enumerate(parts3(scale * sign) + parts3(flow * scale)):
            table = jnp.where(kind == i, part, table)
        traces[1024:1040, face * ELEMS : (face + 1) * ELEMS] = table.astype(BF16)
    for comp in range(COMPS):
        blocks[comp].wait()
        node_major(x_ref, work_ref, comp)
        fill_traces(work_ref, traces, comp)
    both = jnp.dot(traces[...], pick[...], preferred_element_type=F32)
    chosen = both[:512] + both[512:1024]
    for comp in range(COMPS):
        for half in range(2):
            total[lane_slice(half), lane_slice(comp)] = jnp.transpose(
                chosen[lane_slice(comp), lane_slice(half)]
            )
    stats = both[1024:1040, LANES:]
    square[...] = jnp.zeros((LANES, LANES), F32)
    square[0:1, :] = (stats[0:1] + stats[1:2]) + stats[2:3]
    square[1:2, :] = (stats[3:4] + stats[4:5]) + stats[5:6]
    square[2:3, :] = stats[6:7]
    stats = jnp.transpose(square[...])[LANES - CAP :]
    homes = (s0_ref, s1_ref, s2_ref, s3_ref, s4_ref, s5_ref, s6_ref)
    for level, ref in enumerate(homes):
        for comp in range(COMPS):
            ref[comp * CAP : (comp + 1) * CAP, :] = total[
                level * CAP : (level + 1) * CAP, comp * LANES : (comp + 1) * LANES
            ]
    lane = lax.broadcasted_iota(jnp.int32, (CAP, LANES), 1)
    axis = jnp.broadcast_to(stats[:, 2:3], (CAP, LANES))
    moment = jnp.zeros((CAP, LANES), F32)
    for comp in range(3):
        moment += jnp.where(
            axis == float(comp), total[LEVELS * CAP :, comp * LANES : (comp + 1) * LANES], 0.0
        )
    node = lane[0:1] // OBJ
    weight = jnp.zeros((1, LANES), F32)
    for m in range(16):
        weight = jnp.where(node == m, float(FACE_W[m]), weight)
    moment = moment * weight
    for shift in (8, 16, 32, 64):
        moment = moment + pltpu.roll(moment, shift, 1)
    moment = moment * jnp.broadcast_to(stats[:, 0:1], (CAP, LANES))
    moment = jnp.where(
        lane < OBJ, moment,
        jnp.where(lane == OBJ, jnp.broadcast_to(stats[:, 1:2], (CAP, LANES)), 0.0),
    )
    spread = lax.broadcasted_iota(jnp.int32, (LANES, 4 * LANES), 0)
    group = lax.broadcasted_iota(jnp.int32, (LANES, 4 * LANES), 1) // CAP
    wide = jnp.dot(
        moment, jnp.where(spread == group, 1.0, 0.0), precision=HIGHEST,
        preferred_element_type=F32,
    )
    slot = lax.broadcasted_iota(jnp.int32, (CAP, 4 * LANES), 0)
    within = lax.broadcasted_iota(jnp.int32, (CAP, 4 * LANES), 1) % CAP
    flat = jnp.sum(jnp.where(slot == within, wide, 0.0), axis=0, keepdims=True)
    square[0:8, :] = jnp.zeros((8, LANES), F32)
    square[0:1, 0:CAP] = ids_ref[...].astype(F32)
    square[1:3, 0:OBJ] = res_ref[...]
    head = square[0:8, :]
    extra = (
        pltpu.roll(head, 32, 1)[0:1] + pltpu.roll(head, 64, 1)[1:2] + pltpu.roll(head, 72, 1)[2:3]
    )
    message = jnp.concatenate(
        [
            flat[:, 0:LANES],
            flat[:, LANES : 2 * LANES],
            flat[:, 2 * LANES : 3 * LANES] + extra,
            jnp.zeros((1, LANES), F32),
        ],
        axis=0,
    )
    double = jnp.concatenate([message, message], axis=0)
    for peer in range(64):
        message_ref[peer * 8 : (peer + 1) * 8, :] = double


def line_nodes(direction, line):
    p, q = line // 4, line % 4
    if direction == 0:
        return [16 * i + 4 * p + q for i in range(4)]
    if direction == 1:
        return [16 * p + 4 * i + q for i in range(4)]
    return [16 * p + 4 * q + i for i in range(4)]


def even_odd(v):
    return v[0] + v[3], v[1] + v[2], v[0] - v[3], v[1] - v[2]


STIFF = DERIV.T @ DERIV
EP, EQ = [0.5 * (DERIV[r, 0] - DERIV[3 - r, 0]) for r in range(2)]
OS = [0.5 * (DERIV[0, i] + DERIV[3, i]) for i in range(2)]
OT = [0.5 * (DERIV[1, i] + DERIV[2, i]) for i in range(2)]
KE = 0.5 * (STIFF[0, 0] + STIFF[0, 3])
KP = [0.5 * (STIFF[i, 0] - STIFF[i, 3]) for i in range(2)]
KQ = [0.5 * (STIFF[i, 1] - STIFF[i, 2]) for i in range(2)]


def transposed_parts(y):
    s, t, p, q = even_odd(y)
    even = float(EP) * p + float(EQ) * q
    odd = [float(OS[i]) * s + float(OT[i]) * t for i in range(2)]
    return even, odd


def combine(even, odd):
    return [odd[0] + even, odd[1] - even, -even - odd[1], even - odd[0]]


def acc_rows(comp, node, half):
    return pl.ds(((half * COMPS + comp) * NODES + node) * 8, 8)


def spread_row(ref, row):
    return ref[pl.ds(row, 8, stride=0), :]


def resolve_outlets(ids_ref, messages_ref, square, gathered, mult_ref, outlet_ref):
    rank = lax.axis_index("dom").astype(jnp.int32)
    for q in range(3):
        rows = messages_ref[pl.ds(q, LANES, stride=MSG), :]
        gathered[q * LANES : (q + 1) * LANES, :] = jnp.transpose(rows)
    square[...] = jnp.zeros((LANES, LANES), F32)
    square[0:1, 0:CAP] = ids_ref[...].astype(F32)
    own_ids = jnp.transpose(square[...])[0:CAP, 0:1]
    sub = lax.broadcasted_iota(jnp.int32, (8, LANES), 0)
    wanted = jnp.concatenate(
        [(rank * 8 + sub).astype(F32), jnp.broadcast_to(own_ids, (CAP, LANES))], axis=0
    )

    def step(t, sums):
        hit = [
            wanted[g * 8 : g * 8 + 8] == spread_row(gathered, 2 * LANES + CAP + t)
            for g in range(5)
        ]
        new = []
        for r in range(9):
            row = spread_row(gathered, r * CAP + t)
            for g in range(5):
                new.append(sums[r * 5 + g] + jnp.where(hit[g], row, 0.0))
        return tuple(new)

    sums = lax.fori_loop(
        0, CAP, step, tuple(jnp.zeros((8, LANES), F32) for _ in range(45))
    )
    device = lax.broadcasted_iota(jnp.int32, (8, LANES), 1).astype(F32)
    for g in range(5):
        linear = jnp.zeros((8, LANES), F32)
        quadratic = jnp.zeros((8, LANES), F32)
        for q in range(8):
            hit = wanted[g * 8 : g * 8 + 8] == device * 8.0 + float(q)
            linear += jnp.where(hit, spread_row(gathered, 2 * LANES + 64 + q), 0.0)
            quadratic += jnp.where(hit, spread_row(gathered, 2 * LANES + 72 + q), 0.0)
        flow = jnp.sum(sums[8 * 5 + g], axis=1, keepdims=True)
        factor = jnp.sum(linear, axis=1, keepdims=True) + 2.0 * jnp.sum(
            quadratic, axis=1, keepdims=True
        ) * jnp.abs(flow)
        lane = lax.broadcasted_iota(jnp.int32, (8, LANES), 1)
        table = jnp.zeros((8, LANES), F32)
        for o in range(OBJ):
            adj = jnp.sum(sums[o * 5 + g], axis=1, keepdims=True)
            table = jnp.where(lane == o, factor * adj, table)
        if g == 0:
            square[...] = jnp.zeros((LANES, LANES), F32)
            square[0:8, :] = table
            mult_ref[...] = jnp.transpose(square[...])[0:8, 0:8]
        else:
            outlet_ref[(g - 1) * 8 : g * 8, :] = table


def gather_pairs(work, partner_ref, pairs_ref, targets_ref, traces, pick):
    partner = partner_ref[...].astype(F32)
    ids = (
        lax.broadcasted_iota(jnp.int32, (6, ELEMS), 1)
        + lax.broadcasted_iota(jnp.int32, (6, ELEMS), 0) * ELEMS
    ).astype(F32)
    first = partner > ids
    flags = jnp.where(first, 1.0, 0.0)
    before = jnp.where(
        lax.broadcasted_iota(jnp.int32, (ELEMS, ELEMS), 0)
        < lax.broadcasted_iota(jnp.int32, (ELEMS, ELEMS), 1),
        1.0, 0.0,
    ).astype(BF16)
    padded = jnp.concatenate([flags, jnp.zeros((10, ELEMS), F32)], axis=0).astype(BF16)
    inside = jnp.dot(padded, before, preferred_element_type=F32)
    number = lax.broadcasted_iota(jnp.int32, (256, LANES), 0).astype(F32)
    offset = jnp.zeros((1, 1), F32)
    ranks = []
    for face in range(6):
        ranks.append(
            jnp.where(first[face : face + 1], inside[face : face + 1] + offset, -1.0)
        )
        offset = offset + jnp.sum(flags[face : face + 1], axis=1, keepdims=True)
    for which, table in enumerate((ids, partner)):
        found = jnp.zeros((256, LANES), F32)
        for face in range(6):
            for half in range(2):
                cut = lane_slice(half)
                found += jnp.where(
                    number == ranks[face][:, cut], table[face : face + 1, cut], 0.0
                )
        column = jnp.sum(found, axis=1, keepdims=True)
        targets_ref[256 * (1 - which) : 256 * (2 - which), :] = jnp.broadcast_to(
            column, (256, LANES)
        )
    row = jnp.concatenate(
        [
            jnp.transpose(targets_ref[start : start + LANES, :])[0:1]
            for start in (256, 384, 0, 128)
        ],
        axis=1,
    )
    fill_pick(pick, row)
    for comp in range(COMPS):
        fill_traces(work, traces, comp)
    pairs_ref[...] = jnp.dot(
        traces[...], pick[...], preferred_element_type=F32
    ).astype(BF16)


def start_copies(pairs, sems):
    copies = [
        pltpu.make_async_copy(src, dst, sems.at[i]) for i, (src, dst) in enumerate(pairs)
    ]
    for copy in copies:
        copy.start()
    return copies


def place_outer(pairs_ref, targets_ref, link_ref, outlet_ref, shared, slots, square, lhs, chosen, outer):
    columns = slot_columns(link_ref, outlet_ref, square)
    slots[LEVELS * CAP :, :] = jnp.zeros((CAP, 4 * LANES), F32)
    for level in range(LEVELS):
        for comp in range(COMPS):
            slots[level * CAP : (level + 1) * CAP, lane_slice(comp)] = shared[level][
                comp * CAP : (comp + 1) * CAP, :
            ]
    lhs[:, 0:512] = pairs_ref[...]
    for comp in range(COMPS):
        high, low = split2(jnp.transpose(slots[:, lane_slice(comp)]))
        lhs[lane_slice(comp), 512:] = high
        lhs[512 + comp * LANES : 512 + (comp + 1) * LANES, 512:] = low
    for face in range(6):
        chosen[0:512, :] = one_hot(targets_ref[...], face)
        chosen[512:, :] = one_hot(columns, face)
        both = jnp.dot(lhs[...], chosen[...], preferred_element_type=F32)
        outer[face * 512 : (face + 1) * 512, :] = both[:512] + both[512:]


def main_kernel(
    x_any, vel_any, metric_any, scale_any, deriv_any, partner_any, link_any, outlet_any,
    s0_ref, s1_ref, s2_ref, s3_ref, s4_ref, s5_ref, s6_ref,
    acc_any,
    x_ref, vel_ref, metric_ref, scale_ref, deriv_ref, partner_ref, link_ref, outlet_ref,
    acc_ref, pairs_ref, targets_ref, work, flux, plain, grads, traces, pick,
    slots, square, lhs, chosen, outer, sems, sem_out,
):
    blocks = [
        (x_any.at[pl.ds(c * 1024, 1024), :], x_ref.at[pl.ds(c * 1024, 1024), :])
        for c in range(COMPS)
    ]
    small = [
        (vel_any, vel_ref), (metric_any, metric_ref), (scale_any, scale_ref),
        (deriv_any, deriv_ref), (partner_any, partner_ref), (link_any, link_ref),
        (outlet_any, outlet_ref),
    ]
    shared = (s0_ref, s1_ref, s2_ref, s3_ref, s4_ref, s5_ref, s6_ref)
    copies = start_copies(small + blocks, sems)
    for copy in copies[:7]:
        copy.wait()
    for comp in range(COMPS):
        copies[7 + comp].wait()
        node_major(x_ref, work, comp)
    gather_pairs(work, partner_ref, pairs_ref, targets_ref, traces, pick)
    place_outer(
        pairs_ref, targets_ref, link_ref, outlet_ref, shared, slots, square, lhs, chosen, outer
    )
    for j in range(3):
        product = jnp.dot(deriv_ref[...], vel_ref[j], preferred_element_type=F32)
        product = (product[0:192] + product[192:384]) + product[384:576]
        velocity = vel_ref[j].astype(F32)
        for half in range(2):
            cut = lane_slice(half)
            row = (j * 2 + half) * NODES
            plain[row : row + NODES, :] = velocity[:, cut]
            flux[row : row + NODES, :] = velocity[:, cut] * metric_ref[j : j + 1, cut]
            for c in range(3):
                row = ((c * 3 + j) * 2 + half) * NODES
                grads[row : row + NODES, :] = (
                    product[c * NODES : (c + 1) * NODES, cut] * metric_ref[c : c + 1, cut]
                )
    stores = []
    for half in range(2):
        cut = lane_slice(half)
        for direction in range(3):
            gain = jnp.broadcast_to(metric_ref[direction : direction + 1, cut], (8, LANES))
            visc = float(VISCOUS) * gain * gain
            v_even = visc * float(KE)
            v_p = [visc * float(KP[i]) for i in range(2)]
            v_q = [visc * float(KQ[i]) for i in range(2)]
            for line in range(16):
                nodes = line_nodes(direction, line)
                values = []
                for comp in range(COMPS):
                    values.append([work[acc_rows(comp, n, half), :] for n in nodes])
                inner = [None] * 4
                gains = [[]] * 4
                if direction == 2:
                    inner = [inner_gain(plain, scale_ref, n, half) for n in nodes]
                    gains = [
                        [
                            (face, m, node_gain(plain, scale_ref, face, n, half))
                            for face, m in touching(n)
                        ]
                        for n in nodes
                    ]
                base = (direction * 2 + half) * NODES
                speed = [spread_row(flux, base + n) for n in nodes]
                for comp in range(COMPS):
                    if comp < 3:
                        y = [speed[i] * values[comp][i] for i in range(4)]
                        if comp == direction:
                            y = [y[i] + gain * values[3][i] for i in range(4)]
                        even, odd = transposed_parts(y)
                        s, t, p, q = even_odd(values[comp])
                        even = even + v_even * (s - t)
                        odd = [odd[i] + (v_p[i] * p + v_q[i] * q) for i in range(2)]
                    else:
                        even, odd = transposed_parts(values[direction])
                        even = gain * even
                        odd = [gain * odd[i] for i in range(2)]
                    out = combine(even, odd)
                    for i, n in enumerate(nodes):
                        result = out[i]
                        if direction > 0:
                            result = result + acc_ref[acc_rows(comp, n, half), :]
                        if direction == 2 and comp < 3:
                            for j in range(3):
                                row = ((comp * 3 + j) * 2 + half) * NODES + n
                                result = result + spread_row(grads, row) * values[j][i]
                        if inner[i] is not None:
                            result = result + inner[i] * values[comp][i]
                        for face, m, face_gain in gains[i]:
                            row = face * 512 + (comp * 16 + m) * OBJ
                            result = result - face_gain * outer[row : row + 8, cut]
                        acc_ref[acc_rows(comp, n, half), :] = result
        part = pl.ds(half * 2048, 2048)
        store = pltpu.make_async_copy(acc_ref.at[part, :], acc_any.at[part, :], sem_out.at[half])
        store.start()
        stores.append(store)
    for store in stores:
        store.wait()


def inner_gain(plain, scale_ref, node, half):
    total = None
    for face, _ in touching(node):
        speed = spread_row(plain, ((face // 2) * 2 + half) * NODES + node)
        part = jnp.maximum(-speed if face % 2 else speed, 0.0) + float(PENALTY)
        part = part * jnp.broadcast_to(scale_ref[face : face + 1, lane_slice(half)], (8, LANES))
        total = part if total is None else total + part
    return total


def outer_gain(vel_row, scale_row, face):
    signed = vel_row if face % 2 else -vel_row
    return scale_row * (jnp.maximum(signed, 0.0) + float(PENALTY))


def touching(node):
    digits = [node // 16, (node // 4) % 4, node % 4]
    found = []
    for d in range(3):
        if digits[d] in (0, 3):
            rest = digits[:d] + digits[d + 1 :]
            found.append((2 * d + digits[d] // 3, 4 * rest[0] + rest[1]))
    return found


def node_gain(plain, scale_ref, face, node, half):
    scale = jnp.broadcast_to(scale_ref[face : face + 1, lane_slice(half)], (8, LANES))
    return outer_gain(spread_row(plain, ((face // 2) * 2 + half) * NODES + node), scale, face)


def final_kernel(
    live_any, acc_any, scale_any, link_any, outlet_any, ids_any, messages_ref,
    out_any, mult_ref,
    live_ref, acc_ref, scale_ref, link_ref, outlet_ref, ids_ref,
    out_ref, square, outlet, gathered, terms, sems, sem_out,
):
    copies = start_copies(
        [
            (ids_any, ids_ref), (link_any, link_ref),
            (outlet_any, outlet_ref), (scale_any, scale_ref), (live_any, live_ref),
            (acc_any, acc_ref),
        ],
        sems,
    )
    for copy in copies[:5]:
        copy.wait()
    resolve_outlets(ids_ref, messages_ref, square, gathered, mult_ref, terms)
    columns = slot_columns(link_ref, outlet_ref, square)[LEVELS * CAP :]
    square[...] = jnp.zeros((LANES, LANES), F32)
    square[0:CAP, :] = terms[...]
    high, low = split2(jnp.transpose(square[...])[0:16, 0:CAP])
    both = jnp.concatenate([high, low], axis=0)
    for face in range(6):
        term = jnp.dot(both, one_hot(columns, face), preferred_element_type=F32)
        scale = scale_ref[face : face + 1, :] * (2.0 * (face % 2) - 1.0)
        outlet[face * 8 : (face + 1) * 8, :] = (term[0:8] + term[16:24]) * scale
    copies[5].wait()
    live = [live_ref[:, lane_slice(half)] > 0.5 for half in range(2)]
    stores = []
    for high in range(8):
        for half in range(2):
            cut = lane_slice(half)
            block = [[] for _ in range(COMPS)]
            for n in range(high * 8, high * 8 + 8):
                results = [acc_ref[acc_rows(comp, n, half), :] for comp in range(COMPS)]
                for face, m in touching(n):
                    axis = face // 2
                    results[axis] = (
                        results[axis] + float(FACE_W[m]) * outlet[face * 8 : face * 8 + 8, cut]
                    )
                for comp in range(COMPS):
                    block[comp].append(jnp.where(live[half], results[comp], 0.0))
            for comp in range(COMPS):
                turned_block = jnp.swapaxes(jnp.stack(block[comp]), 0, 1)
                out_ref[comp * OBJ : (comp + 1) * OBJ, high, half * 8 : half * 8 + 8, :] = (
                    turned_block
                )
        store = pltpu.make_async_copy(
            out_ref.at[:, high], out_any.at[:, high], sem_out.at[high]
        )
        store.start()
        stores.append(store)
    for store in stores:
        store.wait()


VMEM = pl.BlockSpec(memory_space=pltpu.VMEM)
ANY = pl.BlockSpec(memory_space=pltpu.MemorySpace.HBM)


def params(mebibytes):
    return pltpu.CompilerParams(vmem_limit_bytes=mebibytes * 2**20)


def cost(microseconds):
    return pl.CostEstimate(
        flops=int(microseconds * 1e3), bytes_accessed=int(microseconds * 3.0e6), transcendentals=0
    )


def f32(*shape):
    return jax.ShapeDtypeStruct(shape, F32)


def local(
    adjoint, velocity, metric, face_scale, resistance, elem_count, face_partner, link_face,
    outlet_face, outlet_id,
):
    x_view = (
        adjoint.reshape(COMPS, OBJ, 8, 8, 2, LANES).transpose(0, 1, 2, 4, 3, 5).reshape(4096, LANES)
    )
    link = link_face.transpose(1, 0, 2)
    deriv = jnp.asarray(np.concatenate(split3(node_matrices())), BF16)
    flow = jnp.asarray(flow_matrix(), BF16)
    devices = lax.axis_size("dom")

    message, live, *sent = pl.pallas_call(
        gather_kernel,
        out_shape=(f32(devices * MSG, LANES), f32(8, ELEMS))
        + (f32(FACE_ROWS, LANES),) * LEVELS,
        in_specs=[ANY] * 9,
        out_specs=(VMEM,) * (2 + LEVELS),
        scratch_shapes=[
            pltpu.VMEM((4096, LANES), F32), pltpu.VMEM((3, NODES, ELEMS), BF16),
            pltpu.VMEM((6, ELEMS), F32), pltpu.VMEM((LEVELS, 1, CAP), jnp.int32),
            pltpu.VMEM((1, CAP), jnp.int32), pltpu.VMEM((1, CAP), jnp.int32),
            pltpu.VMEM((2, OBJ), F32), pltpu.VMEM((48, NODES), BF16),
            pltpu.VMEM((1, 1), jnp.int32), pltpu.VMEM((4096, LANES), F32),
            pltpu.VMEM((1040, 6 * ELEMS), BF16), pltpu.VMEM((6 * ELEMS, 256), BF16),
            pltpu.VMEM((LANES, LANES), F32), pltpu.VMEM((256, 512), F32),
            pltpu.SemaphoreType.DMA((12,)),
        ],
        compiler_params=params(60),
        cost_estimate=cost(5),
        name="gather",
    )(x_view, velocity, face_scale, link, outlet_face, outlet_id, resistance, flow,
      elem_count.reshape(1, 1))

    messages = lax.all_to_all(
        message.reshape(devices, MSG, LANES), "dom", split_axis=0, concat_axis=0, tiled=True
    ).reshape(devices * MSG, LANES)

    def swap(block, mask):
        return lax.ppermute(block, "dom", [(i, i ^ mask) for i in range(devices)])

    received = []
    for level, block in enumerate(sent):
        received.append(swap(block, 1 << level))
    acc = pl.pallas_call(
        main_kernel,
        out_shape=f32(4096, LANES),
        in_specs=[ANY] * 8 + [VMEM] * LEVELS,
        out_specs=ANY,
        scratch_shapes=[
            pltpu.VMEM((4096, LANES), F32), pltpu.VMEM((3, NODES, ELEMS), BF16),
            pltpu.VMEM((3, ELEMS), F32), pltpu.VMEM((6, ELEMS), F32),
            pltpu.VMEM((576, NODES), BF16), pltpu.VMEM((6, ELEMS), jnp.int32),
            pltpu.VMEM((LEVELS, 1, CAP), jnp.int32), pltpu.VMEM((1, CAP), jnp.int32),
            pltpu.VMEM((4096, LANES), F32), pltpu.VMEM((1024, 512), BF16),
            pltpu.VMEM((512, LANES), F32), pltpu.VMEM((4096, LANES), F32),
            pltpu.VMEM((384, LANES), F32), pltpu.VMEM((384, LANES), F32),
            pltpu.VMEM((1152, LANES), F32), pltpu.VMEM((1024, 6 * ELEMS), BF16),
            pltpu.VMEM((6 * ELEMS, 512), BF16), pltpu.VMEM((256, 512), F32),
            pltpu.VMEM((LANES, LANES), F32), pltpu.VMEM((1024, 768), BF16),
            pltpu.VMEM((768, ELEMS), BF16), pltpu.VMEM((6 * 512, ELEMS), F32),
            pltpu.SemaphoreType.DMA((11,)), pltpu.SemaphoreType.DMA((2,)),
        ],
        compiler_params=params(30),
        cost_estimate=cost(10),
        name="volume",
    )(
        x_view, velocity, metric, face_scale, deriv, face_partner, link, outlet_face, *received
    )

    out, multiplier = pl.pallas_call(
        final_kernel,
        out_shape=(f32(32, 8, 16, LANES), f32(OBJ, 8)),
        in_specs=[ANY] * 6 + [VMEM],
        out_specs=(ANY, VMEM),
        scratch_shapes=[
            pltpu.VMEM((8, ELEMS), F32), pltpu.VMEM((4096, LANES), F32),
            pltpu.VMEM((6, ELEMS), F32), pltpu.VMEM((LEVELS, 1, CAP), jnp.int32),
            pltpu.VMEM((1, CAP), jnp.int32), pltpu.VMEM((1, CAP), jnp.int32),
            pltpu.VMEM((32, 8, 16, LANES), F32),
            pltpu.VMEM((LANES, LANES), F32), pltpu.VMEM((48, ELEMS), F32),
            pltpu.VMEM((384, LANES), F32), pltpu.VMEM((CAP, LANES), F32),
            pltpu.SemaphoreType.DMA((6,)), pltpu.SemaphoreType.DMA((8,)),
        ],
        compiler_params=params(30),
        cost_estimate=cost(3),
        name="finish",
    )(live, acc, face_scale, link, outlet_face, outlet_id, messages)
    out = (
        out.reshape(COMPS, OBJ, 8, 2, 8, LANES).transpose(0, 1, 2, 4, 3, 5)
        .reshape(COMPS, OBJ, NODES, ELEMS)
    )
    return out, multiplier


def solution(mesh):
    placed = (
        P(None, None, None, "dom"), P(None, None, "dom"), P(None, "dom"), P(None, "dom"),
        P(None, "dom"), P("dom"), P(None, "dom"), P("dom", None, None), P("dom", None),
        P("dom", None),
    )
    return jax.shard_map(
        local, mesh=mesh, in_specs=placed,
        out_specs=(P(None, None, None, "dom"), P(None, "dom")), check_vma=False,
    )
```

```python
import math

import jax
import jax.numpy as jnp
import numpy as np
from jax import lax
from jax.experimental import pallas as pl
from jax.experimental.pallas import tpu as pltpu
from jax.sharding import PartitionSpec as P


F32 = jnp.float32
BF16 = jnp.bfloat16
VISCOUS = 0.05
PENALTY = 1.0
COMPS, OBJ, NODES, ELEMS = 4, 8, 64, 256
LANES = 128
CAP, LEVELS = 32, 7
FACE_ROWS = COMPS * CAP
MSG = 4
HIGHEST = lax.Precision.HIGHEST


def gll_tables():
    root_five = math.sqrt(5.0)
    points = np.array([-1.0, -1.0 / root_five, 1.0 / root_five, 1.0])
    weights = np.array([1.0, 5.0, 5.0, 1.0]) / 6.0
    products = np.array(
        [np.prod([points[i] - points[k] for k in range(4) if k != i]) for i in range(4)]
    )
    derivative = np.zeros((4, 4))
    for i in range(4):
        for j in range(4):
            if i != j:
                derivative[i, j] = products[i] / (products[j] * (points[i] - points[j]))
        derivative[i, i] = -np.sum(derivative[i])
    return (derivative, weights)


DERIV, WEIGHTS = gll_tables()
FACE_W = np.outer(WEIGHTS, WEIGHTS).reshape(16)


def split3(array):
    high = np.asarray(array, np.float32).astype(jnp.bfloat16)
    rest = np.asarray(array, np.float32) - high.astype(np.float32)
    middle = rest.astype(jnp.bfloat16)
    low = (rest - middle.astype(np.float32)).astype(jnp.bfloat16)
    return high, middle, low


def node_matrices():
    identity = np.eye(4)
    return np.concatenate(
        [
            np.kron(DERIV, np.kron(identity, identity)),
            np.kron(identity, np.kron(DERIV, identity)),
            np.kron(identity, np.kron(identity, DERIV)),
        ]
    )


def face_node(face, m):
    axis, layer = face // 2, 3 * (face % 2)
    a, b = m // 4, m % 4
    digits = [a, b]
    digits.insert(axis, layer)
    return 16 * digits[0] + 4 * digits[1] + digits[2]


def flow_matrix():
    table = np.zeros((3, 16, NODES), np.float32)
    for face in range(6):
        row = np.zeros(NODES)
        for m in range(16):
            row[face_node(face, m)] = FACE_W[m] * (2 * (face % 2) - 1)
        for part, values in enumerate(split3(row)):
            table[face // 2, 8 * (face % 2) + part] = values.astype(np.float32)
    return table.reshape(48, NODES)


def lane_slice(half):
    return slice(half * LANES, (half + 1) * LANES)


def slot_columns(link_ref, outlet_ref, square):
    square[...] = jnp.full((LANES, LANES), -1.0, F32)
    for level in range(LEVELS):
        square[level : level + 1, 0:CAP] = link_ref[level].astype(F32)
    square[LEVELS : LEVELS + 1, 0:CAP] = outlet_ref[...].astype(F32)
    turned = jnp.transpose(square[...])
    return jnp.concatenate(
        [
            jnp.broadcast_to(turned[0:CAP, b : b + 1], (CAP, LANES))
            for b in range(LEVELS + 1)
        ],
        axis=0,
    )


def one_hot(columns, face):
    lane = lax.broadcasted_iota(jnp.int32, columns.shape, 1).astype(F32)
    parts = [
        jnp.where(columns == lane + float(face * ELEMS + half * LANES), 1.0, 0.0)
        for half in range(2)
    ]
    return jnp.concatenate(parts, axis=1).astype(BF16)


def split2(value):
    high = value.astype(BF16)
    return high, (value - high.astype(F32)).astype(BF16)


def node_major(x_ref, work_ref, comp):
    for high in range(8):
        for half in range(2):
            block = jnp.stack(
                [
                    x_ref[pl.ds(((comp * OBJ + o) * 8 + high) * 16 + half * 8, 8), :]
                    for o in range(OBJ)
                ]
            )
            start = acc_rows(comp, high * 8, half).start
            work_ref[pl.ds(start, 64), :] = jnp.swapaxes(block, 0, 1).reshape(64, LANES)


def comp_traces(work_ref, comp):
    for face in range(6):
        for m in range(0, 16, 2):
            row = (comp * 16 + m) * OBJ
            for half in range(2):
                pair = jnp.concatenate(
                    [work_ref[acc_rows(comp, face_node(face, m + i), half), :] for i in range(2)],
                    axis=0,
                )
                yield face, row, half, split2(pair)


def fill_traces(work_ref, traces, comp):
    for face, row, half, (high, low) in comp_traces(work_ref, comp):
        cols = slice(face * ELEMS + half * LANES, face * ELEMS + (half + 1) * LANES)
        traces[row : row + 16, cols] = high
        traces[512 + row : 528 + row, cols] = low


def fill_pick(pick, row):
    sub = lax.broadcasted_iota(jnp.int32, (ELEMS, row.shape[1]), 0).astype(F32)
    for face in range(6):
        pick[face * ELEMS : (face + 1) * ELEMS, :] = jnp.where(
            sub == row - float(face * ELEMS), 1.0, 0.0
        ).astype(BF16)


def parts3(value):
    high = value.astype(BF16).astype(F32)
    rest = value - high
    middle = rest.astype(BF16).astype(F32)
    return high, middle, rest - middle


def gather_kernel(
    x_any, vel_any, scale_any, link_any, outlet_any, ids_any, res_any, flow_any,
    message_ref,
    s0_ref, s1_ref, s2_ref, s3_ref, s4_ref, s5_ref, s6_ref,
    x_ref, vel_ref, scale_ref, link_ref, outlet_ref, ids_ref, res_ref, flow_ref,
    work_ref, traces, pick, square, total, sems,
):
    small = (
        (link_any, link_ref), (outlet_any, outlet_ref), (vel_any, vel_ref),
        (scale_any, scale_ref), (flow_any, flow_ref), (ids_any, ids_ref), (res_any, res_ref),
    )
    copies = [
        pltpu.make_async_copy(src, dst, sems.at[4 + i]) for i, (src, dst) in enumerate(small)
    ]
    blocks = [
        pltpu.make_async_copy(
            x_any.at[pl.ds(c * 1024, 1024), :], x_ref.at[pl.ds(c * 1024, 1024), :], sems.at[c]
        )
        for c in range(COMPS)
    ]
    for copy in blocks + copies:
        copy.start()
    for copy in copies:
        copy.wait()
    square[0:8, :] = jnp.zeros((8, LANES), F32)
    for level in range(LEVELS):
        square[level : level + 1, 0:CAP] = link_ref[level].astype(F32)
    square[LEVELS : LEVELS + 1, 0:CAP] = outlet_ref[...].astype(F32)
    head = square[0:8, :]
    pieces = [
        (pltpu.roll(head, CAP * (b % 4), 1) if b % 4 else head)[b : b + 1] for b in range(8)
    ]
    row = jnp.concatenate([sum(pieces[1:4], pieces[0]), sum(pieces[5:], pieces[4])], axis=1)
    fill_pick(pick, row)
    kind = lax.broadcasted_iota(jnp.int32, (16, ELEMS), 0)
    for face in range(6):
        axis, sign = face // 2, 2.0 * (face % 2) - 1.0
        if face % 2 == 0:
            flows = jnp.dot(
                flow_ref[16 * axis : 16 * axis + 16, :], vel_ref[axis],
                preferred_element_type=F32,
            )
        scale = scale_ref[face : face + 1, :]
        first = 8 * (face % 2)
        flow = (flows[first : first + 1] + flows[first + 1 : first + 2]) + flows[
            first + 2 : first + 3
        ]
        table = jnp.where(kind == 6, float(axis), 0.0)
        for i, part in enumerate(parts3(scale * sign) + parts3(flow * scale)):
            table = jnp.where(kind == i, part, table)
        traces[1024:1040, face * ELEMS : (face + 1) * ELEMS] = table.astype(BF16)
    for comp in range(COMPS):
        blocks[comp].wait()
        node_major(x_ref, work_ref, comp)
        fill_traces(work_ref, traces, comp)
    both = jnp.dot(traces[...], pick[...], preferred_element_type=F32)
    chosen = both[:512] + both[512:1024]
    for comp in range(COMPS):
        for half in range(2):
            total[lane_slice(half), lane_slice(comp)] = jnp.transpose(
                chosen[lane_slice(comp), lane_slice(half)]
            )
    stats = both[1024:1040, LANES:]
    square[...] = jnp.zeros((LANES, LANES), F32)
    square[0:1, :] = (stats[0:1] + stats[1:2]) + stats[2:3]
    square[1:2, :] = (stats[3:4] + stats[4:5]) + stats[5:6]
    square[2:3, :] = stats[6:7]
    stats = jnp.transpose(square[...])[LANES - CAP :]
    homes = (s0_ref, s1_ref, s2_ref, s3_ref, s4_ref, s5_ref, s6_ref)
    for level, ref in enumerate(homes):
        for comp in range(COMPS):
            ref[comp * CAP : (comp + 1) * CAP, :] = total[
                level * CAP : (level + 1) * CAP, comp * LANES : (comp + 1) * LANES
            ]
    lane = lax.broadcasted_iota(jnp.int32, (CAP, LANES), 1)
    axis = jnp.broadcast_to(stats[:, 2:3], (CAP, LANES))
    moment = jnp.zeros((CAP, LANES), F32)
    for comp in range(3):
        moment += jnp.where(
            axis == float(comp), total[LEVELS * CAP :, comp * LANES : (comp + 1) * LANES], 0.0
        )
    node = lane[0:1] // OBJ
    weight = jnp.zeros((1, LANES), F32)
    for m in range(16):
        weight = jnp.where(node == m, float(FACE_W[m]), weight)
    moment = moment * weight
    for shift in (8, 16, 32, 64):
        moment = moment + pltpu.roll(moment, shift, 1)
    moment = moment * jnp.broadcast_to(stats[:, 0:1], (CAP, LANES))
    moment = jnp.where(
        lane < OBJ, moment,
        jnp.where(lane == OBJ, jnp.broadcast_to(stats[:, 1:2], (CAP, LANES)), 0.0),
    )
    spread = lax.broadcasted_iota(jnp.int32, (LANES, 4 * LANES), 0)
    group = lax.broadcasted_iota(jnp.int32, (LANES, 4 * LANES), 1) // CAP
    wide = jnp.dot(
        moment, jnp.where(spread == group, 1.0, 0.0), precision=HIGHEST,
        preferred_element_type=F32,
    )
    slot = lax.broadcasted_iota(jnp.int32, (CAP, 4 * LANES), 0)
    within = lax.broadcasted_iota(jnp.int32, (CAP, 4 * LANES), 1) % CAP
    flat = jnp.sum(jnp.where(slot == within, wide, 0.0), axis=0, keepdims=True)
    square[0:8, :] = jnp.zeros((8, LANES), F32)
    square[0:1, 0:CAP] = ids_ref[...].astype(F32)
    square[1:3, 0:OBJ] = res_ref[...]
    head = square[0:8, :]
    extra = (
        pltpu.roll(head, 32, 1)[0:1] + pltpu.roll(head, 64, 1)[1:2] + pltpu.roll(head, 72, 1)[2:3]
    )
    message = jnp.concatenate(
        [
            flat[:, 0:LANES],
            flat[:, LANES : 2 * LANES],
            flat[:, 2 * LANES : 3 * LANES] + extra,
            jnp.zeros((1, LANES), F32),
        ],
        axis=0,
    )
    double = jnp.concatenate([message, message], axis=0)
    for peer in range(64):
        message_ref[peer * 8 : (peer + 1) * 8, :] = double


def line_nodes(direction, line):
    p, q = line // 4, line % 4
    if direction == 0:
        return [16 * i + 4 * p + q for i in range(4)]
    if direction == 1:
        return [16 * p + 4 * i + q for i in range(4)]
    return [16 * p + 4 * q + i for i in range(4)]


def even_odd(v):
    return v[0] + v[3], v[1] + v[2], v[0] - v[3], v[1] - v[2]


STIFF = DERIV.T @ DERIV
EP, EQ = [0.5 * (DERIV[r, 0] - DERIV[3 - r, 0]) for r in range(2)]
OS = [0.5 * (DERIV[0, i] + DERIV[3, i]) for i in range(2)]
OT = [0.5 * (DERIV[1, i] + DERIV[2, i]) for i in range(2)]
KE = 0.5 * (STIFF[0, 0] + STIFF[0, 3])
KP = [0.5 * (STIFF[i, 0] - STIFF[i, 3]) for i in range(2)]
KQ = [0.5 * (STIFF[i, 1] - STIFF[i, 2]) for i in range(2)]


def transposed_parts(y):
    s, t, p, q = even_odd(y)
    even = float(EP) * p + float(EQ) * q
    odd = [float(OS[i]) * s + float(OT[i]) * t for i in range(2)]
    return even, odd


def combine(even, odd):
    return [odd[0] + even, odd[1] - even, -even - odd[1], even - odd[0]]


def acc_rows(comp, node, half):
    return pl.ds(((half * COMPS + comp) * NODES + node) * 8, 8)


def spread_row(ref, row):
    return ref[pl.ds(row, 8, stride=0), :]


def resolve_outlets(ids_ref, messages_ref, square, gathered, mult_ref, outlet_ref):
    rank = lax.axis_index("dom").astype(jnp.int32)
    for q in range(3):
        rows = messages_ref[pl.ds(q, LANES, stride=MSG), :]
        gathered[q * LANES : (q + 1) * LANES, :] = jnp.transpose(rows)
    square[...] = jnp.zeros((LANES, LANES), F32)
    square[0:1, 0:CAP] = ids_ref[...].astype(F32)
    own_ids = jnp.transpose(square[...])[0:CAP, 0:1]
    sub = lax.broadcasted_iota(jnp.int32, (8, LANES), 0)
    wanted = jnp.concatenate(
        [(rank * 8 + sub).astype(F32), jnp.broadcast_to(own_ids, (CAP, LANES))], axis=0
    )

    def step(t, sums):
        hit = [
            wanted[g * 8 : g * 8 + 8] == spread_row(gathered, 2 * LANES + CAP + t)
            for g in range(5)
        ]
        new = []
        for r in range(9):
            row = spread_row(gathered, r * CAP + t)
            for g in range(5):
                new.append(sums[r * 5 + g] + jnp.where(hit[g], row, 0.0))
        return tuple(new)

    sums = lax.fori_loop(
        0, CAP, step, tuple(jnp.zeros((8, LANES), F32) for _ in range(45))
    )
    device = lax.broadcasted_iota(jnp.int32, (8, LANES), 1).astype(F32)
    for g in range(5):
        linear = jnp.zeros((8, LANES), F32)
        quadratic = jnp.zeros((8, LANES), F32)
        for q in range(8):
            hit = wanted[g * 8 : g * 8 + 8] == device * 8.0 + float(q)
            linear += jnp.where(hit, spread_row(gathered, 2 * LANES + 64 + q), 0.0)
            quadratic += jnp.where(hit, spread_row(gathered, 2 * LANES + 72 + q), 0.0)
        flow = jnp.sum(sums[8 * 5 + g], axis=1, keepdims=True)
        factor = jnp.sum(linear, axis=1, keepdims=True) + 2.0 * jnp.sum(
            quadratic, axis=1, keepdims=True
        ) * jnp.abs(flow)
        lane = lax.broadcasted_iota(jnp.int32, (8, LANES), 1)
        table = jnp.zeros((8, LANES), F32)
        for o in range(OBJ):
            adj = jnp.sum(sums[o * 5 + g], axis=1, keepdims=True)
            table = jnp.where(lane == o, factor * adj, table)
        if g == 0:
            square[...] = jnp.zeros((LANES, LANES), F32)
            square[0:8, :] = table
            mult_ref[...] = jnp.transpose(square[...])[0:8, 0:8]
        else:
            outlet_ref[(g - 1) * 8 : g * 8, :] = table


def gather_pairs(work, partner_ref, pairs_ref, targets_ref, traces, pick):
    partner = partner_ref[...].astype(F32)
    ids = (
        lax.broadcasted_iota(jnp.int32, (6, ELEMS), 1)
        + lax.broadcasted_iota(jnp.int32, (6, ELEMS), 0) * ELEMS
    ).astype(F32)
    first = partner > ids
    flags = jnp.where(first, 1.0, 0.0)
    before = jnp.where(
        lax.broadcasted_iota(jnp.int32, (ELEMS, ELEMS), 0)
        < lax.broadcasted_iota(jnp.int32, (ELEMS, ELEMS), 1),
        1.0, 0.0,
    ).astype(BF16)
    padded = jnp.concatenate([flags, jnp.zeros((10, ELEMS), F32)], axis=0).astype(BF16)
    inside = jnp.dot(padded, before, preferred_element_type=F32)
    number = lax.broadcasted_iota(jnp.int32, (256, LANES), 0).astype(F32)
    offset = jnp.zeros((1, 1), F32)
    ranks = []
    for face in range(6):
        ranks.append(
            jnp.where(first[face : face + 1], inside[face : face + 1] + offset, -1.0)
        )
        offset = offset + jnp.sum(flags[face : face + 1], axis=1, keepdims=True)
    for which, table in enumerate((ids, partner)):
        found = jnp.zeros((256, LANES), F32)
        for face in range(6):
            for half in range(2):
                cut = lane_slice(half)
                found += jnp.where(
                    number == ranks[face][:, cut], table[face : face + 1, cut], 0.0
                )
        column = jnp.sum(found, axis=1, keepdims=True)
        targets_ref[256 * (1 - which) : 256 * (2 - which), :] = jnp.broadcast_to(
            column, (256, LANES)
        )
    row = jnp.concatenate(
        [
            jnp.transpose(targets_ref[start : start + LANES, :])[0:1]
            for start in (256, 384, 0, 128)
        ],
        axis=1,
    )
    fill_pick(pick, row)
    for comp in range(COMPS):
        fill_traces(work, traces, comp)
    pairs_ref[...] = jnp.dot(
        traces[...], pick[...], preferred_element_type=F32
    ).astype(BF16)


def start_copies(pairs, sems):
    copies = [
        pltpu.make_async_copy(src, dst, sems.at[i]) for i, (src, dst) in enumerate(pairs)
    ]
    for copy in copies:
        copy.start()
    return copies


def place_outer(pairs_ref, targets_ref, link_ref, outlet_ref, shared, slots, square, lhs, chosen, outer):
    columns = slot_columns(link_ref, outlet_ref, square)
    slots[LEVELS * CAP :, :] = jnp.zeros((CAP, 4 * LANES), F32)
    for level in range(LEVELS):
        for comp in range(COMPS):
            slots[level * CAP : (level + 1) * CAP, lane_slice(comp)] = shared[level][
                comp * CAP : (comp + 1) * CAP, :
            ]
    lhs[:, 0:512] = pairs_ref[...]
    for comp in range(COMPS):
        high, low = split2(jnp.transpose(slots[:, lane_slice(comp)]))
        lhs[lane_slice(comp), 512:] = high
        lhs[512 + comp * LANES : 512 + (comp + 1) * LANES, 512:] = low
    for face in range(6):
        chosen[0:512, :] = one_hot(targets_ref[...], face)
        chosen[512:, :] = one_hot(columns, face)
        both = jnp.dot(lhs[...], chosen[...], preferred_element_type=F32)
        outer[face * 512 : (face + 1) * 512, :] = both[:512] + both[512:]


def main_kernel(
    x_any, vel_any, metric_any, scale_any, deriv_any, partner_any, link_any, outlet_any, count_any,
    s0_ref, s1_ref, s2_ref, s3_ref, s4_ref, s5_ref, s6_ref,
    acc_any,
    x_ref, vel_ref, metric_ref, scale_ref, deriv_ref, partner_ref, link_ref, outlet_ref, count_ref,
    acc_ref, pairs_ref, targets_ref, work, flux, plain, grads, traces, pick,
    slots, square, lhs, chosen, outer, sems, sem_out,
):
    blocks = [
        (x_any.at[pl.ds(c * 1024, 1024), :], x_ref.at[pl.ds(c * 1024, 1024), :])
        for c in range(COMPS)
    ]
    small = [
        (vel_any, vel_ref), (metric_any, metric_ref), (scale_any, scale_ref),
        (deriv_any, deriv_ref), (partner_any, partner_ref), (link_any, link_ref),
        (outlet_any, outlet_ref), (count_any, count_ref),
    ]
    shared = (s0_ref, s1_ref, s2_ref, s3_ref, s4_ref, s5_ref, s6_ref)
    copies = start_copies(small + blocks, sems)
    for copy in copies[:8]:
        copy.wait()
    for comp in range(COMPS):
        copies[8 + comp].wait()
        node_major(x_ref, work, comp)
    gather_pairs(work, partner_ref, pairs_ref, targets_ref, traces, pick)
    place_outer(
        pairs_ref, targets_ref, link_ref, outlet_ref, shared, slots, square, lhs, chosen, outer
    )
    for j in range(3):
        product = jnp.dot(deriv_ref[...], vel_ref[j], preferred_element_type=F32)
        product = (product[0:192] + product[192:384]) + product[384:576]
        velocity = vel_ref[j].astype(F32)
        for half in range(2):
            cut = lane_slice(half)
            row = (j * 2 + half) * NODES
            plain[row : row + NODES, :] = velocity[:, cut]
            flux[row : row + NODES, :] = velocity[:, cut] * metric_ref[j : j + 1, cut]
            for c in range(3):
                row = ((c * 3 + j) * 2 + half) * NODES
                grads[row : row + NODES, :] = (
                    product[c * NODES : (c + 1) * NODES, cut] * metric_ref[c : c + 1, cut]
                )
    stores = []
    for half in range(2):
        cut = lane_slice(half)
        lane = lax.broadcasted_iota(jnp.int32, (8, LANES), 1) + half * LANES
        live = lane < count_ref[...]
        for direction in range(3):
            gain = jnp.broadcast_to(metric_ref[direction : direction + 1, cut], (8, LANES))
            visc = float(VISCOUS) * gain * gain
            v_even = visc * float(KE)
            v_p = [visc * float(KP[i]) for i in range(2)]
            v_q = [visc * float(KQ[i]) for i in range(2)]
            for line in range(16):
                nodes = line_nodes(direction, line)
                values = []
                for comp in range(COMPS):
                    values.append([work[acc_rows(comp, n, half), :] for n in nodes])
                inner = [None] * 4
                gains = [[]] * 4
                if direction == 2:
                    inner = [inner_gain(plain, scale_ref, n, half) for n in nodes]
                    gains = [
                        [
                            (face, m, node_gain(plain, scale_ref, face, n, half))
                            for face, m in touching(n)
                        ]
                        for n in nodes
                    ]
                base = (direction * 2 + half) * NODES
                speed = [spread_row(flux, base + n) for n in nodes]
                for comp in range(COMPS):
                    if comp < 3:
                        y = [speed[i] * values[comp][i] for i in range(4)]
                        if comp == direction:
                            y = [y[i] + gain * values[3][i] for i in range(4)]
                        even, odd = transposed_parts(y)
                        s, t, p, q = even_odd(values[comp])
                        even = even + v_even * (s - t)
                        odd = [odd[i] + (v_p[i] * p + v_q[i] * q) for i in range(2)]
                    else:
                        even, odd = transposed_parts(values[direction])
                        even = gain * even
                        odd = [gain * odd[i] for i in range(2)]
                    out = combine(even, odd)
                    for i, n in enumerate(nodes):
                        result = out[i]
                        if direction > 0:
                            result = result + acc_ref[acc_rows(comp, n, half), :]
                        if direction == 2 and comp < 3:
                            for j in range(3):
                                row = ((comp * 3 + j) * 2 + half) * NODES + n
                                result = result + spread_row(grads, row) * values[j][i]
                        if inner[i] is not None:
                            result = result + inner[i] * values[comp][i]
                        for face, m, face_gain in gains[i]:
                            row = face * 512 + (comp * 16 + m) * OBJ
                            result = result - face_gain * outer[row : row + 8, cut]
                        if direction == 2:
                            result = jnp.where(live, result, 0.0)
                        acc_ref[acc_rows(comp, n, half), :] = result
        part = pl.ds(half * 2048, 2048)
        store = pltpu.make_async_copy(acc_ref.at[part, :], acc_any.at[part, :], sem_out.at[half])
        store.start()
        stores.append(store)
    for store in stores:
        store.wait()


def inner_gain(plain, scale_ref, node, half):
    total = None
    for face, _ in touching(node):
        speed = spread_row(plain, ((face // 2) * 2 + half) * NODES + node)
        part = jnp.maximum(-speed if face % 2 else speed, 0.0) + float(PENALTY)
        part = part * jnp.broadcast_to(scale_ref[face : face + 1, lane_slice(half)], (8, LANES))
        total = part if total is None else total + part
    return total


def outer_gain(vel_row, scale_row, face):
    signed = vel_row if face % 2 else -vel_row
    return scale_row * (jnp.maximum(signed, 0.0) + float(PENALTY))


def touching(node):
    digits = [node // 16, (node // 4) % 4, node % 4]
    found = []
    for d in range(3):
        if digits[d] in (0, 3):
            rest = digits[:d] + digits[d + 1 :]
            found.append((2 * d + digits[d] // 3, 4 * rest[0] + rest[1]))
    return found


def node_gain(plain, scale_ref, face, node, half):
    scale = jnp.broadcast_to(scale_ref[face : face + 1, lane_slice(half)], (8, LANES))
    return outer_gain(spread_row(plain, ((face // 2) * 2 + half) * NODES + node), scale, face)


def final_kernel(
    acc_any, scale_any, link_any, outlet_any, ids_any, messages_ref,
    out_any, mult_ref,
    acc_ref, scale_ref, link_ref, outlet_ref, ids_ref,
    out_ref, square, outlet, gathered, terms, sems, sem_out,
):
    copies = start_copies(
        [
            (ids_any, ids_ref), (link_any, link_ref),
            (outlet_any, outlet_ref), (scale_any, scale_ref),
            (acc_any, acc_ref),
        ],
        sems,
    )
    for copy in copies[:4]:
        copy.wait()
    resolve_outlets(ids_ref, messages_ref, square, gathered, mult_ref, terms)
    columns = slot_columns(link_ref, outlet_ref, square)[LEVELS * CAP :]
    square[...] = jnp.zeros((LANES, LANES), F32)
    square[0:CAP, :] = terms[...]
    high, low = split2(jnp.transpose(square[...])[0:16, 0:CAP])
    both = jnp.concatenate([high, low], axis=0)
    for face in range(6):
        term = jnp.dot(both, one_hot(columns, face), preferred_element_type=F32)
        scale = scale_ref[face : face + 1, :] * (2.0 * (face % 2) - 1.0)
        outlet[face * 8 : (face + 1) * 8, :] = (term[0:8] + term[16:24]) * scale
    copies[4].wait()
    stores = []
    for high in range(8):
        for half in range(2):
            cut = lane_slice(half)
            block = [[] for _ in range(COMPS)]
            for n in range(high * 8, high * 8 + 8):
                results = [acc_ref[acc_rows(comp, n, half), :] for comp in range(COMPS)]
                for face, m in touching(n):
                    axis = face // 2
                    results[axis] = (
                        results[axis] + float(FACE_W[m]) * outlet[face * 8 : face * 8 + 8, cut]
                    )
                for comp in range(COMPS):
                    block[comp].append(results[comp])
            for comp in range(COMPS):
                turned_block = jnp.swapaxes(jnp.stack(block[comp]), 0, 1)
                out_ref[comp * OBJ : (comp + 1) * OBJ, high, half * 8 : half * 8 + 8, :] = (
                    turned_block
                )
        store = pltpu.make_async_copy(
            out_ref.at[:, high], out_any.at[:, high], sem_out.at[high]
        )
        store.start()
        stores.append(store)
    for store in stores:
        store.wait()


VMEM = pl.BlockSpec(memory_space=pltpu.VMEM)
ANY = pl.BlockSpec(memory_space=pltpu.MemorySpace.HBM)


def params(mebibytes):
    return pltpu.CompilerParams(vmem_limit_bytes=mebibytes * 2**20)


def cost(microseconds):
    return pl.CostEstimate(
        flops=int(microseconds * 1e3), bytes_accessed=int(microseconds * 3.0e6), transcendentals=0
    )


def f32(*shape):
    return jax.ShapeDtypeStruct(shape, F32)


def local(
    adjoint, velocity, metric, face_scale, resistance, elem_count, face_partner, link_face,
    outlet_face, outlet_id,
):
    x_view = (
        adjoint.reshape(COMPS, OBJ, 8, 8, 2, LANES).transpose(0, 1, 2, 4, 3, 5).reshape(4096, LANES)
    )
    link = link_face.transpose(1, 0, 2)
    deriv = jnp.asarray(np.concatenate(split3(node_matrices())), BF16)
    flow = jnp.asarray(flow_matrix(), BF16)
    devices = lax.axis_size("dom")

    message, *sent = pl.pallas_call(
        gather_kernel,
        out_shape=(f32(devices * MSG, LANES),)
        + (f32(FACE_ROWS, LANES),) * LEVELS,
        in_specs=[ANY] * 8,
        out_specs=(VMEM,) * (1 + LEVELS),
        scratch_shapes=[
            pltpu.VMEM((4096, LANES), F32), pltpu.VMEM((3, NODES, ELEMS), BF16),
            pltpu.VMEM((6, ELEMS), F32), pltpu.VMEM((LEVELS, 1, CAP), jnp.int32),
            pltpu.VMEM((1, CAP), jnp.int32), pltpu.VMEM((1, CAP), jnp.int32),
            pltpu.VMEM((2, OBJ), F32), pltpu.VMEM((48, NODES), BF16),
            pltpu.VMEM((4096, LANES), F32),
            pltpu.VMEM((1040, 6 * ELEMS), BF16), pltpu.VMEM((6 * ELEMS, 256), BF16),
            pltpu.VMEM((LANES, LANES), F32), pltpu.VMEM((256, 512), F32),
            pltpu.SemaphoreType.DMA((12,)),
        ],
        compiler_params=params(60),
        cost_estimate=cost(5),
        name="gather",
    )(x_view, velocity, face_scale, link, outlet_face, outlet_id, resistance, flow)

    messages = lax.all_to_all(
        message.reshape(devices, MSG, LANES), "dom", split_axis=0, concat_axis=0, tiled=True
    ).reshape(devices * MSG, LANES)

    def swap(block, mask):
        return lax.ppermute(block, "dom", [(i, i ^ mask) for i in range(devices)])

    received = []
    for level, block in enumerate(sent):
        received.append(swap(block, 1 << level))
    acc = pl.pallas_call(
        main_kernel,
        out_shape=f32(4096, LANES),
        in_specs=[ANY] * 9 + [VMEM] * LEVELS,
        out_specs=ANY,
        scratch_shapes=[
            pltpu.VMEM((4096, LANES), F32), pltpu.VMEM((3, NODES, ELEMS), BF16),
            pltpu.VMEM((3, ELEMS), F32), pltpu.VMEM((6, ELEMS), F32),
            pltpu.VMEM((576, NODES), BF16), pltpu.VMEM((6, ELEMS), jnp.int32),
            pltpu.VMEM((LEVELS, 1, CAP), jnp.int32), pltpu.VMEM((1, CAP), jnp.int32),
            pltpu.VMEM((1, 1), jnp.int32),
            pltpu.VMEM((4096, LANES), F32), pltpu.VMEM((1024, 512), BF16),
            pltpu.VMEM((512, LANES), F32), pltpu.VMEM((4096, LANES), F32),
            pltpu.VMEM((384, LANES), F32), pltpu.VMEM((384, LANES), F32),
            pltpu.VMEM((1152, LANES), F32), pltpu.VMEM((1024, 6 * ELEMS), BF16),
            pltpu.VMEM((6 * ELEMS, 512), BF16), pltpu.VMEM((256, 512), F32),
            pltpu.VMEM((LANES, LANES), F32), pltpu.VMEM((1024, 768), BF16),
            pltpu.VMEM((768, ELEMS), BF16), pltpu.VMEM((6 * 512, ELEMS), F32),
            pltpu.SemaphoreType.DMA((12,)), pltpu.SemaphoreType.DMA((2,)),
        ],
        compiler_params=params(30),
        cost_estimate=cost(10),
        name="volume",
    )(
        x_view, velocity, metric, face_scale, deriv, face_partner, link, outlet_face,
        elem_count.reshape(1, 1), *received
    )

    out, multiplier = pl.pallas_call(
        final_kernel,
        out_shape=(f32(32, 8, 16, LANES), f32(OBJ, 8)),
        in_specs=[ANY] * 5 + [VMEM],
        out_specs=(ANY, VMEM),
        scratch_shapes=[
            pltpu.VMEM((4096, LANES), F32),
            pltpu.VMEM((6, ELEMS), F32), pltpu.VMEM((LEVELS, 1, CAP), jnp.int32),
            pltpu.VMEM((1, CAP), jnp.int32), pltpu.VMEM((1, CAP), jnp.int32),
            pltpu.VMEM((32, 8, 16, LANES), F32),
            pltpu.VMEM((LANES, LANES), F32), pltpu.VMEM((48, ELEMS), F32),
            pltpu.VMEM((384, LANES), F32), pltpu.VMEM((CAP, LANES), F32),
            pltpu.SemaphoreType.DMA((5,)), pltpu.SemaphoreType.DMA((8,)),
        ],
        compiler_params=params(30),
        cost_estimate=cost(3),
        name="finish",
    )(acc, face_scale, link, outlet_face, outlet_id, messages)
    out = (
        out.reshape(COMPS, OBJ, 8, 2, 8, LANES).transpose(0, 1, 2, 4, 3, 5)
        .reshape(COMPS, OBJ, NODES, ELEMS)
    )
    return out, multiplier


def solution(mesh):
    placed = (
        P(None, None, None, "dom"), P(None, None, "dom"), P(None, "dom"), P(None, "dom"),
        P(None, "dom"), P("dom"), P(None, "dom"), P("dom", None, None), P("dom", None),
        P("dom", None),
    )
    return jax.shard_map(
        local, mesh=mesh, in_specs=placed,
        out_specs=(P(None, None, None, "dom"), P(None, "dom")), check_vma=False,
    )
```
